32 devices in a mesh: dp: 8 (over z, core), own: 4 (over y, x).
Axes of the slice: x: 2, y: 2, z: 4, core: 2. Of those that a mesh axis runs over, the one named last changes fastest.
Arguments:
- tokens_in: bfloat16 [64, 256, 768], P(('dp', 'own')), may hold values from -6 to 6
- condition: float32 [64, 768], P(('dp', 'own')), may hold values from -6 to 6
- cotangent: bfloat16 [64, 256, 768], P(('dp', 'own')), may hold values from -6 to 6
- w_qkv: float32 [768, 2304], P('own', 'dp'), may hold values from -0.21875 to 0.21875
- w_proj: float32 [768, 768], P('own', 'dp'), may hold values from -0.625 to 0.625
- w_fc1: float32 [768, 3072], P('own', 'dp'), may hold values from -0.21875 to 0.21875
- w_fc2: float32 [3072, 768], P('dp', 'own'), may hold values from -0.109375 to 0.109375
- w_ada: float32 [768, 4608], P('own', 'dp'), may hold values from -0.21875 to 0.21875
- mom_qkv: float32 [768, 2304], P('own', 'dp'), may hold values from -384 to 384
- mom_proj: float32 [768, 768], P('own', 'dp'), may hold values from -384 to 384
- mom_fc1: float32 [768, 3072], P('own', 'dp'), may hold values from -384 to 384
- mom_fc2: float32 [3072, 768], P('dp', 'own'), may hold values from -384 to 384
- mom_ada: float32 [768, 4608], P('own', 'dp'), may hold values from -384 to 384
- biases: float32 [10752], P(('dp', 'own')), may hold values from -4 to 4
- bias_mom: float32 [10752], P(('dp', 'own')), may hold values from -224 to 224
Outputs:
- block_out: float32 [64, 256, 768], P(('dp', 'own'))
- grad_in: float32 [64, 256, 768], P(('dp', 'own'))
- grad_cond: float32 [64, 768], P(('dp', 'own'))
- grad_qkv: float32 [768, 2304], P('own', 'dp')
- grad_proj: float32 [768, 768], P('own', 'dp')
- grad_fc1: float32 [768, 3072], P('own', 'dp')
- grad_fc2: float32 [3072, 768], P('dp', 'own')
- grad_ada: float32 [768, 4608], P('own', 'dp')
- grad_bias: float32 [10752], P(('dp', 'own'))
- new_qkv: float32 [768, 2304], P('own', 'dp')
- new_proj: float32 [768, 768], P('own', 'dp')
- new_fc1: float32 [768, 3072], P('own', 'dp')
- new_fc2: float32 [3072, 768], P('dp', 'own')
- new_ada: float32 [768, 4608], P('own', 'dp')
- moment_qkv: float32 [768, 2304], P('own', 'dp')
- moment_proj: float32 [768, 768], P('own', 'dp')
- moment_fc1: float32 [768, 3072], P('own', 'dp')
- moment_fc2: float32 [3072, 768], P('dp', 'own')
- moment_ada: float32 [768, 4608], P('own', 'dp')
- new_bias: float32 [10752], P(('dp', 'own'))
- moment_bias: float32 [10752], P(('dp', 'own'))
- moment_norms: float32 [5], replicated
The draws below stay inside these ranges and needn't reach their ends.
All inputs are finite; a program needn't handle non-finite values.
Results may differ from the reference program's by a relative error of at most 0.028.
Values may be sent and summed in bfloat16 or wider, within the bound.
No kernel may reach another device: no remote copies, remote signals or barrier semaphores. Data moves between devices by JAX's collectives and lax.ppermute only.
A program may use at most 192 MiB of HBM per device.

```python
import math
import jax
import jax.numpy as jnp
from jax import lax

D = 768
FF = 3072
HEADS = 12
SEQ = 256
LAT_DEV = 2
NS_ITERS = 5
LATENTS = 64
NBIAS = 10752
N_DP = 8
N_OWN = 4


def moment_draw(key, rows, cols):
    base = jnp.clip(jax.random.normal(key, (rows, cols), jnp.float32), -6.0, 6.0)
    base = base * (0.2 * (LATENTS * SEQ) ** 0.5)
    ramp = jnp.arange(rows, dtype=jnp.float32) / (rows - 1)
    row_scale = 0.6 * jnp.exp(jnp.log(3.0) * ramp)
    return base * row_scale[:, None]


def draw_mom_qkv(key, part):
    return moment_draw(jax.random.fold_in(key, 11), D, 3 * D)


def draw_mom_proj(key, part):
    return moment_draw(jax.random.fold_in(key, 12), D, D)


def draw_mom_fc1(key, part):
    return moment_draw(jax.random.fold_in(key, 13), D, FF)


def draw_mom_fc2(key, part):
    return moment_draw(jax.random.fold_in(key, 14), FF, D)


def draw_mom_ada(key, part):
    return moment_draw(jax.random.fold_in(key, 15), D, 6 * D)


def steps_of(stream_key, dims, cuts, smallest, largest):
    loudness = 1.0
    for axis_at, shards_of in cuts:
        steps = jax.random.uniform(jax.random.fold_in(jax.random.fold_in(stream_key, 6), axis_at), (shards_of,), jnp.float32, smallest / len(cuts), largest / len(cuts))
        loudness = loudness * jnp.repeat(jnp.exp(steps), dims[axis_at] // shards_of).reshape((-1,) + (1,) * (len(dims) - 1 - axis_at))
    return loudness


def bell_draw(own_key, extent, deviation, most, shards=(), kind=jnp.bfloat16):
    factor_of = steps_of(own_key, extent, shards, -0.22, 0.18) if shards else 1.0
    drawn = jax.random.normal(own_key, extent, jnp.float32) * deviation * factor_of
    return jnp.minimum(jnp.maximum(drawn, -most), most).astype(kind)


def setup_inputs(seed: int = 0) -> dict:
    key_of = jax.random.split(jax.random.key(seed), 16)
    return {
        "tokens_in": bell_draw(key_of[0], (LATENTS, SEQ, D), 1.0, 6.0, ((0, 32),)),
        "condition": bell_draw(key_of[1], (LATENTS, D), 1.0, 6.0, ((0, 32),), jnp.float32),
        "cotangent": bell_draw(key_of[2], (LATENTS, SEQ, D), 1.0, 6.0, ((0, 32),)),
        "w_qkv": bell_draw(key_of[3], (D, 3 * D), D ** -0.5, 0.21875, ((0, 4), (1, 8)), jnp.float32),
        "w_proj": bell_draw(key_of[4], (D, D), (D // 8) ** -0.5, 0.625, ((0, 4), (1, 8)), jnp.float32),
        "w_fc1": bell_draw(key_of[5], (D, FF), D ** -0.5, 0.21875, ((0, 4), (1, 8)), jnp.float32),
        "w_fc2": bell_draw(key_of[6], (FF, D), FF ** -0.5, 0.109375, ((0, 8), (1, 4)), jnp.float32),
        "w_ada": bell_draw(key_of[7], (D, 6 * D), D ** -0.5, 0.21875, ((0, 4), (1, 8)), jnp.float32),
        "mom_qkv": draw_mom_qkv(jax.random.fold_in(key_of[15], 71), 0),
        "mom_proj": draw_mom_proj(jax.random.fold_in(key_of[15], 71), 0),
        "mom_fc1": draw_mom_fc1(jax.random.fold_in(key_of[15], 71), 0),
        "mom_fc2": draw_mom_fc2(jax.random.fold_in(key_of[15], 71), 0),
        "mom_ada": draw_mom_ada(jax.random.fold_in(key_of[15], 71), 0),
        "biases": bell_draw(key_of[13], (NBIAS,), 0.5, 4.0, ((0, 32),), jnp.float32),
        "bias_mom": bell_draw(key_of[14], (NBIAS,), (0.3 * (LAT_DEV * N_DP * N_OWN * SEQ) ** 0.5), 224.0, ((0, 32),), jnp.float32),
    }


momentum_rate = 0.9
learn_rate = 0.15
bias_rate = 0.002
coef_first = 3.4445
coef_second = -4.775
coef_third = 2.0315
gelu_scale = math.sqrt(2.0 / math.pi)
norm_epsilon = 1e-06

def batched(form, left, right):
    return jnp.einsum(form, left.astype(jnp.float32), right.astype(jnp.float32))

def layer_stats(values):
    mean_value = lax.optimization_barrier(jnp.mean(values, axis=-1, keepdims=True))
    centered = values - mean_value
    inv_std = lax.rsqrt(lax.optimization_barrier(jnp.mean(centered * centered, axis=-1, keepdims=True)) + norm_epsilon)
    return (centered * inv_std, inv_std)

def norm_back(grad_normed, normed, inv_std):
    first = lax.optimization_barrier(jnp.mean(grad_normed, axis=-1, keepdims=True))
    second = lax.optimization_barrier(jnp.mean(grad_normed * normed, axis=-1, keepdims=True))
    return inv_std * (grad_normed - first - normed * second)

def gelu_value(inner):
    return 0.5 * inner * (1.0 + jnp.tanh(gelu_scale * (inner + 0.044715 * inner * inner * inner)))

def gelu_slope(inner):
    tangent = jnp.tanh(gelu_scale * (inner + 0.044715 * inner * inner * inner))
    return 0.5 * (1.0 + tangent) + 0.5 * inner * (1.0 - tangent * tangent) * gelu_scale * (1.0 + 3.0 * 0.044715 * inner * inner)

def block_pass(tokens_in, condition, cotangent, w_qkv, w_proj, w_fc1, w_fc2, w_ada, bias_low):
    latents, length, features = tokens_in.shape
    hidden_units = w_fc1.shape[1]
    head_count = HEADS
    head_size = features // head_count
    score_scale = 1.0 / math.sqrt(head_size)
    row_count = latents * length
    bias_full = bias_low.astype(jnp.float32)
    b_query = bias_full[:features]
    b_value = bias_full[features:2 * features]
    b_proj = bias_full[2 * features:3 * features]
    b_fc1 = bias_full[3 * features:3 * features + hidden_units]
    b_fc2 = bias_full[3 * features + hidden_units:4 * features + hidden_units]
    b_ada = bias_full[4 * features + hidden_units:]
    cond_act = jax.nn.silu(condition).astype(jnp.bfloat16)
    modulation = jnp.dot(cond_act, w_ada, preferred_element_type=jnp.float32) + b_ada
    pieces = [modulation[:, index * features:(index + 1) * features][:, None, :] for index in range(6)]
    shift_one, scale_one, gate_one, shift_two, scale_two, gate_two = pieces
    residual = tokens_in.astype(jnp.float32)
    normed_one, inv_one = layer_stats(residual)
    modulated_one = (normed_one * (1.0 + scale_one) + shift_one).astype(jnp.bfloat16)
    qkv_proj = jnp.dot(modulated_one.reshape(row_count, features), w_qkv, preferred_element_type=jnp.float32)
    qkv_proj = qkv_proj.reshape(latents, length, 3 * features)
    head_shape = (latents, length, head_count, head_size)
    query_heads = (qkv_proj[..., :features] + b_query).astype(jnp.bfloat16).reshape(head_shape)
    key_heads = qkv_proj[..., features:2 * features].astype(jnp.bfloat16).reshape(head_shape)
    value_heads = (qkv_proj[..., 2 * features:] + b_value).astype(jnp.bfloat16).reshape(head_shape)
    scores = batched('bqhd,bkhd->bhqk', query_heads, key_heads) * score_scale
    row_max = lax.optimization_barrier(jnp.max(scores, axis=-1, keepdims=True))
    log_total = row_max + jnp.log(lax.optimization_barrier(jnp.sum(jnp.exp(scores - row_max), axis=-1, keepdims=True)))
    attn_probs = jnp.exp(scores - log_total).astype(jnp.bfloat16)
    attn_out = batched('bhqk,bkhd->bqhd', attn_probs, value_heads).astype(jnp.bfloat16).reshape(row_count, features)
    branch_one = (jnp.dot(attn_out, w_proj, preferred_element_type=jnp.float32) + b_proj).reshape(latents, length, features)
    middle = residual + gate_one * branch_one
    normed_two, inv_two = layer_stats(middle)
    modulated_two = (normed_two * (1.0 + scale_two) + shift_two).astype(jnp.bfloat16).reshape(row_count, features)
    fc1_pre = jnp.dot(modulated_two, w_fc1, preferred_element_type=jnp.float32) + b_fc1
    fc1_act = gelu_value(fc1_pre).astype(jnp.bfloat16)
    branch_two = (jnp.dot(fc1_act, w_fc2, preferred_element_type=jnp.float32) + b_fc2).reshape(latents, length, features)
    block_out = middle + gate_two * branch_two
    cot_float = cotangent.astype(jnp.float32)
    d_gate_two = lax.optimization_barrier(jnp.sum(cot_float * branch_two, axis=1))
    d_branch_two = cot_float * gate_two
    dbranch_low = d_branch_two.astype(jnp.bfloat16).reshape(row_count, features)
    g_fc2 = jnp.dot(fc1_act.T, dbranch_low, preferred_element_type=jnp.float32)
    gb_fc2 = lax.optimization_barrier(jnp.sum(d_branch_two, axis=(0, 1)))
    d_pre = jnp.dot(dbranch_low, w_fc2.T, preferred_element_type=jnp.float32) * gelu_slope(fc1_pre)
    dpre_low = d_pre.astype(jnp.bfloat16)
    g_fc1 = jnp.dot(modulated_two.T, dpre_low, preferred_element_type=jnp.float32)
    gb_fc1 = lax.optimization_barrier(jnp.sum(d_pre, axis=0))
    d_mod_two = jnp.dot(dpre_low, w_fc1.T, preferred_element_type=jnp.float32).reshape(latents, length, features)
    d_shift_two = lax.optimization_barrier(jnp.sum(d_mod_two, axis=1))
    d_scale_two = lax.optimization_barrier(jnp.sum(d_mod_two * normed_two, axis=1))
    d_middle = cot_float + norm_back(d_mod_two * (1.0 + scale_two), normed_two, inv_two)
    d_gate_one = lax.optimization_barrier(jnp.sum(d_middle * branch_one, axis=1))
    d_branch_one = d_middle * gate_one
    dbranch_one_low = d_branch_one.astype(jnp.bfloat16).reshape(row_count, features)
    g_proj = jnp.dot(attn_out.T, dbranch_one_low, preferred_element_type=jnp.float32)
    gb_proj = lax.optimization_barrier(jnp.sum(d_branch_one, axis=(0, 1)))
    d_attn = jnp.dot(dbranch_one_low, w_proj.T, preferred_element_type=jnp.float32).astype(jnp.bfloat16).reshape(head_shape)
    scores_again = batched('bqhd,bkhd->bhqk', query_heads, key_heads) * score_scale
    probs_again = jnp.exp(scores_again - log_total)
    d_probs = batched('bqhd,bkhd->bhqk', d_attn, value_heads)
    delta = lax.optimization_barrier(jnp.sum(probs_again * d_probs, axis=-1, keepdims=True))
    d_scores = (probs_again * (d_probs - delta) * score_scale).astype(jnp.bfloat16)
    d_query = batched('bhqk,bkhd->bqhd', d_scores, key_heads)
    d_key = batched('bhqk,bqhd->bkhd', d_scores, query_heads)
    d_value = batched('bhqk,bqhd->bkhd', probs_again.astype(jnp.bfloat16), d_attn)
    flat_shape = (latents, length, features)
    d_qkv = jnp.concatenate([d_query.reshape(flat_shape), d_key.reshape(flat_shape), d_value.reshape(flat_shape)], axis=-1)
    dqkv_low = d_qkv.astype(jnp.bfloat16).reshape(row_count, 3 * features)
    g_qkv = jnp.dot(modulated_one.reshape(row_count, features).T, dqkv_low, preferred_element_type=jnp.float32)
    gb_query = lax.optimization_barrier(jnp.sum(d_query, axis=(0, 1))).reshape(features)
    gb_value = lax.optimization_barrier(jnp.sum(d_value, axis=(0, 1))).reshape(features)
    d_mod_one = jnp.dot(dqkv_low, w_qkv.T, preferred_element_type=jnp.float32).reshape(flat_shape)
    d_shift_one = lax.optimization_barrier(jnp.sum(d_mod_one, axis=1))
    d_scale_one = lax.optimization_barrier(jnp.sum(d_mod_one * normed_one, axis=1))
    grad_in = d_middle + norm_back(d_mod_one * (1.0 + scale_one), normed_one, inv_one)
    d_modulation = jnp.concatenate([d_shift_one, d_scale_one, d_gate_one, d_shift_two, d_scale_two, d_gate_two], axis=-1)
    dmod_low = d_modulation.astype(jnp.bfloat16)
    g_ada = jnp.dot(cond_act.T, dmod_low, preferred_element_type=jnp.float32)
    gb_ada = lax.optimization_barrier(jnp.sum(d_modulation, axis=0))
    sigmoid_c = jax.nn.sigmoid(condition)
    grad_cond = jnp.dot(dmod_low, w_ada.T, preferred_element_type=jnp.float32) * (sigmoid_c * (1.0 + condition * (1.0 - sigmoid_c)))
    grad_bias = jnp.concatenate([gb_query, gb_value, gb_proj, gb_fc1, gb_fc2, gb_ada])
    return (block_out, grad_in, grad_cond, (g_qkv, g_proj, g_fc1, g_fc2, g_ada), grad_bias, cond_act, dmod_low)

def orthogonalize(oriented):
    iterate = oriented / (jnp.sqrt(jnp.sum(oriented * oriented)) + 1e-07)
    for ns_step in range(NS_ITERS):
        gram = jnp.dot(iterate, iterate.T, precision=lax.Precision.HIGHEST)
        square = jnp.dot(gram, gram, precision=lax.Precision.HIGHEST)
        mixer = coef_second * gram + coef_third * square
        iterate = coef_first * iterate + jnp.dot(mixer, iterate, precision=lax.Precision.HIGHEST)
    return iterate

def muon_step(weight, moment, gradient, flipped):
    fresh = momentum_rate * moment + gradient
    oriented = fresh.T if flipped else fresh
    magnitude = jnp.sqrt(jnp.sum(oriented * oriented))
    ortho = orthogonalize(oriented)
    if flipped:
        ortho = ortho.T
    factor = 0.2 * math.sqrt(max(weight.shape[0], weight.shape[1]))
    return (weight - learn_rate * factor * ortho, fresh, magnitude)

def reference(tokens_in, condition, cotangent, w_qkv, w_proj, w_fc1, w_fc2, w_ada, mom_qkv, mom_proj, mom_fc1, mom_fc2, mom_ada, biases, bias_mom):
    low_qkv = w_qkv.astype(jnp.bfloat16)
    low_proj = w_proj.astype(jnp.bfloat16)
    low_fc1 = w_fc1.astype(jnp.bfloat16)
    low_fc2 = w_fc2.astype(jnp.bfloat16)
    low_ada = w_ada.astype(jnp.bfloat16)
    low_bias = biases.astype(jnp.bfloat16)
    group = math.gcd(LATENTS, max(1, 4096 // SEQ))
    blocks = LATENTS // group

    def one_block(carry, pieces):
        part_in, part_cond, part_cot = pieces
        block_out, grad_in, grad_cond, partials, grad_b, cond_act, dmod_low = block_pass(part_in, part_cond, part_cot, low_qkv, low_proj, low_fc1, low_fc2, low_ada, low_bias)
        new_carry = (carry[0] + partials[0], carry[1] + partials[1], carry[2] + partials[2], carry[3] + partials[3], carry[4] + partials[4], carry[5] + grad_b)
        return (new_carry, (block_out, grad_in, grad_cond))
    start = (jnp.zeros((D, 3 * D), jnp.float32), jnp.zeros((D, D), jnp.float32), jnp.zeros((D, FF), jnp.float32), jnp.zeros((FF, D), jnp.float32), jnp.zeros((D, 6 * D), jnp.float32), jnp.zeros((NBIAS,), jnp.float32))
    inputs_blocked = (tokens_in.reshape(blocks, group, SEQ, D), condition.reshape(blocks, group, D), cotangent.reshape(blocks, group, SEQ, D))
    totals, outputs = lax.scan(one_block, start, inputs_blocked)
    block_out = outputs[0].reshape(LATENTS, SEQ, D)
    grad_in = outputs[1].reshape(LATENTS, SEQ, D)
    grad_cond = outputs[2].reshape(LATENTS, D)
    grad_qkv, grad_proj, grad_fc1, grad_fc2, grad_ada, grad_bias = totals
    new_qkv, moment_qkv, norm_qkv = muon_step(w_qkv, mom_qkv, grad_qkv, False)
    new_proj, moment_proj, norm_proj = muon_step(w_proj, mom_proj, grad_proj, False)
    new_fc1, moment_fc1, norm_fc1 = muon_step(w_fc1, mom_fc1, grad_fc1, False)
    new_fc2, moment_fc2, norm_fc2 = muon_step(w_fc2, mom_fc2, grad_fc2, True)
    new_ada, moment_ada, norm_ada = muon_step(w_ada, mom_ada, grad_ada, False)
    moment_norms = jnp.stack([norm_qkv, norm_proj, norm_fc1, norm_fc2, norm_ada])
    moment_bias = momentum_rate * bias_mom + grad_bias
    new_bias = biases - bias_rate * moment_bias
    return (block_out, grad_in, grad_cond, grad_qkv, grad_proj, grad_fc1, grad_fc2, grad_ada, grad_bias, new_qkv, new_proj, new_fc1, new_fc2, new_ada, moment_qkv, moment_proj, moment_fc1, moment_fc2, moment_ada, new_bias, moment_bias, moment_norms)
```

```python
import math

import jax
import jax.numpy as jnp
from jax import lax
from jax.sharding import PartitionSpec as P

HEADS = 12
NS_ITERS = 5


momentum_rate = 0.9
learn_rate = 0.15
bias_rate = 0.002
coef_first = 3.4445
coef_second = -4.775
coef_third = 2.0315
gelu_scale = math.sqrt(2.0 / math.pi)
norm_epsilon = 1e-06


def gather_own(piece, count):
    place = lax.axis_index("own")
    whole = jnp.zeros((count,) + piece.shape, piece.dtype)
    whole = lax.dynamic_update_index_in_dim(whole, piece, place, 0)
    for step in range(1, count):
        pairs = [(index, index ^ step) for index in range(count)]
        other = lax.ppermute(piece, "own", pairs)
        whole = lax.dynamic_update_index_in_dim(whole, other, place ^ step, 0)
    return whole


def gather_dp(piece, count):
    place = lax.axis_index("dp")
    whole = jnp.zeros((count,) + piece.shape, piece.dtype)
    whole = lax.dynamic_update_index_in_dim(whole, piece, place, 0)
    for step in range(1, count):
        pairs = [(index, index ^ step) for index in range(count)]
        other = lax.ppermute(piece, "dp", pairs)
        whole = lax.dynamic_update_index_in_dim(whole, other, place ^ step, 0)
    return whole


def swap_dp(blocks):
    return lax.all_to_all(blocks, "dp", split_axis=0, concat_axis=0, tiled=True)


def fine_dot(left, right):
    return jnp.dot(left, right, precision=lax.Precision.HIGH)


def columns_of(blocks, start, width):
    count, rows, _ = blocks.shape
    part = blocks[:, :, start : start + width]
    return part.transpose(1, 0, 2).reshape(rows, count * width)


def tiles_of(matrix, n_dp, n_own):
    rows, cols = matrix.shape
    split = matrix.reshape(n_own, rows // n_own, n_dp, cols // n_dp).transpose(2, 0, 1, 3)
    return split.reshape(n_dp * n_own, rows // n_own, cols // n_dp)

def batched(form, left, right):
    return jnp.einsum(form, left, right, preferred_element_type=jnp.float32)


def layer_stats(values):
    mean_value = jnp.mean(values, axis=-1, keepdims=True)
    centered = values - mean_value
    inv_std = lax.rsqrt(jnp.mean(centered * centered, axis=-1, keepdims=True) + norm_epsilon)
    return (centered * inv_std, inv_std)


def norm_back(grad_normed, normed, inv_std):
    first = jnp.mean(grad_normed, axis=-1, keepdims=True)
    second = jnp.mean(grad_normed * normed, axis=-1, keepdims=True)
    return inv_std * (grad_normed - first - normed * second)


def gelu_value(inner):
    return 0.5 * inner * (1.0 + jnp.tanh(gelu_scale * (inner + 0.044715 * inner * inner * inner)))


def gelu_slope(inner):
    tangent = jnp.tanh(gelu_scale * (inner + 0.044715 * inner * inner * inner))
    return 0.5 * (1.0 + tangent) + 0.5 * inner * (1.0 - tangent * tangent) * gelu_scale * (
        1.0 + 3.0 * 0.044715 * inner * inner
    )


def block_pass(tokens_in, modulation, cotangent, w_qkv, w_proj, w_fc1, w_fc2_t, bias_full):
    latents, length, features = tokens_in.shape
    hidden_units = w_fc1.shape[1]
    head_count = HEADS
    head_size = features // head_count
    score_scale = 1.0 / math.sqrt(head_size)
    row_count = latents * length
    b_query = bias_full[:features]
    b_value = bias_full[features : 2 * features]
    b_proj = bias_full[2 * features : 3 * features]
    b_fc1 = bias_full[3 * features : 3 * features + hidden_units]
    b_fc2 = bias_full[3 * features + hidden_units : 4 * features + hidden_units]
    pieces = [
        modulation[:, index * features : (index + 1) * features][:, None, :] for index in range(6)
    ]
    shift_one, scale_one, gate_one, shift_two, scale_two, gate_two = pieces
    residual = tokens_in.astype(jnp.float32)
    normed_one, inv_one = layer_stats(residual)
    modulated_one = (normed_one * (1.0 + scale_one) + shift_one).astype(jnp.bfloat16)
    qkv_proj = jnp.dot(
        modulated_one.reshape(row_count, features), w_qkv, preferred_element_type=jnp.float32
    )
    qkv_proj = qkv_proj.reshape(latents, length, 3 * features)
    head_shape = (latents, length, head_count, head_size)
    query_heads = (qkv_proj[..., :features] + b_query).astype(jnp.bfloat16).reshape(head_shape)
    key_heads = qkv_proj[..., features : 2 * features].astype(jnp.bfloat16).reshape(head_shape)
    value_heads = (qkv_proj[..., 2 * features :] + b_value).astype(jnp.bfloat16).reshape(head_shape)
    scores = batched("bqhd,bkhd->bhqk", query_heads, key_heads) * score_scale
    row_max = jnp.max(scores, axis=-1, keepdims=True)
    log_total = row_max + jnp.log(jnp.sum(jnp.exp(scores - row_max), axis=-1, keepdims=True))
    attn_probs = jnp.exp(scores - log_total).astype(jnp.bfloat16)
    attn_out = (
        batched("bhqk,bkhd->bqhd", attn_probs, value_heads)
        .astype(jnp.bfloat16)
        .reshape(row_count, features)
    )
    branch_one = (jnp.dot(attn_out, w_proj, preferred_element_type=jnp.float32) + b_proj).reshape(
        latents, length, features
    )
    middle = residual + gate_one * branch_one
    normed_two, inv_two = layer_stats(middle)
    modulated_two = (
        (normed_two * (1.0 + scale_two) + shift_two)
        .astype(jnp.bfloat16)
        .reshape(row_count, features)
    )
    fc1_pre = jnp.dot(modulated_two, w_fc1, preferred_element_type=jnp.float32) + b_fc1
    fc1_act = gelu_value(fc1_pre).astype(jnp.bfloat16)
    branch_two = (jnp.dot(fc1_act, w_fc2_t.T, preferred_element_type=jnp.float32) + b_fc2).reshape(
        latents, length, features
    )
    block_out = middle + gate_two * branch_two
    cot_float = cotangent.astype(jnp.float32)
    d_gate_two = jnp.sum(cot_float * branch_two, axis=1)
    d_branch_two = cot_float * gate_two
    dbranch_low = d_branch_two.astype(jnp.bfloat16).reshape(row_count, features)
    g_fc2_t = jnp.dot(dbranch_low.T, fc1_act, preferred_element_type=jnp.float32)
    gb_fc2 = jnp.sum(d_branch_two, axis=(0, 1))
    d_pre = jnp.dot(dbranch_low, w_fc2_t, preferred_element_type=jnp.float32) * gelu_slope(fc1_pre)
    dpre_low = d_pre.astype(jnp.bfloat16)
    g_fc1 = jnp.dot(modulated_two.T, dpre_low, preferred_element_type=jnp.float32)
    gb_fc1 = jnp.sum(d_pre, axis=0)
    d_mod_two = jnp.dot(dpre_low, w_fc1.T, preferred_element_type=jnp.float32).reshape(
        latents, length, features
    )
    d_shift_two = jnp.sum(d_mod_two, axis=1)
    d_scale_two = jnp.sum(d_mod_two * normed_two, axis=1)
    d_middle = cot_float + norm_back(d_mod_two * (1.0 + scale_two), normed_two, inv_two)
    d_gate_one = jnp.sum(d_middle * branch_one, axis=1)
    d_branch_one = d_middle * gate_one
    dbranch_one_low = d_branch_one.astype(jnp.bfloat16).reshape(row_count, features)
    g_proj = jnp.dot(attn_out.T, dbranch_one_low, preferred_element_type=jnp.float32)
    gb_proj = jnp.sum(d_branch_one, axis=(0, 1))
    d_attn = (
        jnp.dot(dbranch_one_low, w_proj.T, preferred_element_type=jnp.float32)
        .astype(jnp.bfloat16)
        .reshape(head_shape)
    )
    scores_again = batched("bqhd,bkhd->bhqk", query_heads, key_heads) * score_scale
    probs_again = jnp.exp(scores_again - log_total)
    d_probs = batched("bqhd,bkhd->bhqk", d_attn, value_heads)
    delta = jnp.sum(probs_again * d_probs, axis=-1, keepdims=True)
    d_scores = (probs_again * (d_probs - delta) * score_scale).astype(jnp.bfloat16)
    d_query = batched("bhqk,bkhd->bqhd", d_scores, key_heads)
    d_key = batched("bhqk,bqhd->bkhd", d_scores, query_heads)
    d_value = batched("bhqk,bqhd->bkhd", probs_again.astype(jnp.bfloat16), d_attn)
    flat_shape = (latents, length, features)
    d_qkv = jnp.concatenate(
        [d_query.reshape(flat_shape), d_key.reshape(flat_shape), d_value.reshape(flat_shape)],
        axis=-1,
    )
    dqkv_low = d_qkv.astype(jnp.bfloat16).reshape(row_count, 3 * features)
    g_qkv = jnp.dot(
        modulated_one.reshape(row_count, features).T, dqkv_low, preferred_element_type=jnp.float32
    )
    gb_query = jnp.sum(d_query, axis=(0, 1)).reshape(features)
    gb_value = jnp.sum(d_value, axis=(0, 1)).reshape(features)
    d_mod_one = jnp.dot(dqkv_low, w_qkv.T, preferred_element_type=jnp.float32).reshape(flat_shape)
    d_shift_one = jnp.sum(d_mod_one, axis=1)
    d_scale_one = jnp.sum(d_mod_one * normed_one, axis=1)
    grad_in = d_middle + norm_back(d_mod_one * (1.0 + scale_one), normed_one, inv_one)
    d_modulation = jnp.concatenate(
        [d_shift_one, d_scale_one, d_gate_one, d_shift_two, d_scale_two, d_gate_two], axis=-1
    )
    gb_ada = jnp.sum(d_modulation, axis=0)
    grad_bias = jnp.concatenate([gb_query, gb_value, gb_proj, gb_fc1, gb_fc2, gb_ada])
    return block_out, grad_in, d_modulation, (g_qkv, g_proj, g_fc1, g_fc2_t), grad_bias


def per_device(
    tokens_in,
    condition,
    cotangent,
    w_qkv,
    w_proj,
    w_fc1,
    w_fc2,
    w_ada,
    mom_qkv,
    mom_proj,
    mom_fc1,
    mom_fc2,
    mom_ada,
    biases,
    bias_mom,
):
    low = jnp.bfloat16
    n_dp, n_own = lax.axis_size("dp"), lax.axis_size("own")
    dp_place, own_place = lax.axis_index("dp"), lax.axis_index("own")
    both = ("dp", "own")
    latents, features = condition.shape
    rows = w_qkv.shape[0]
    n_qkv, n_proj, n_fc1, n_fc2, n_ada = (
        w_qkv.shape[1],
        w_proj.shape[1],
        w_fc1.shape[1],
        w_fc2.shape[0],
        w_ada.shape[1],
    )
    cond_act = jax.nn.silu(condition).astype(low)
    small = jnp.concatenate([cond_act.reshape(-1), biases.astype(low)])
    small_own = gather_dp(small, n_dp)
    cond_own = small_own[:, : latents * features].reshape(n_dp * latents, features)
    w_ada_rows = gather_own(w_ada.astype(low), n_own).reshape(features, n_ada)
    mod_mine = jnp.dot(cond_own, w_ada_rows, preferred_element_type=jnp.float32)
    mod_parts = swap_dp(mod_mine.reshape(n_dp, latents, n_ada))
    small_all = gather_own(small_own, n_own)
    bias_full = (
        small_all[:, :, latents * features :].transpose(1, 0, 2).reshape(-1).astype(jnp.float32)
    )
    modulation = mod_parts.transpose(1, 0, 2).reshape(latents, n_dp * n_ada)
    modulation = modulation + bias_full[bias_full.shape[0] - n_dp * n_ada :]
    first = jnp.concatenate([w_qkv, w_proj], axis=1).astype(low)
    second = jnp.concatenate([w_fc1, w_fc2.T], axis=1).astype(low)
    first_all = lax.all_gather(first, both).reshape(n_dp, features, n_qkv + n_proj)
    second_all = lax.all_gather(second, both).reshape(n_dp, features, n_fc1 + n_fc2)
    block_out, grad_in, d_modulation, partials, bias_terms = block_pass(
        tokens_in,
        modulation,
        cotangent,
        columns_of(first_all, 0, n_qkv),
        columns_of(first_all, n_qkv, n_proj),
        columns_of(second_all, 0, n_fc1),
        columns_of(second_all, n_fc1, n_fc2),
        bias_full,
    )
    fc_terms = jnp.concatenate(
        [
            tiles_of(partials[2].astype(low), n_dp, n_own),
            tiles_of(partials[3].astype(low), n_dp, n_own),
        ],
        axis=2,
    )
    fc_tile = lax.psum_scatter(fc_terms, both, scatter_dimension=0).astype(jnp.float32)
    attn_terms = jnp.concatenate(
        [
            tiles_of(partials[0].astype(low), n_dp, n_own),
            tiles_of(partials[1].astype(low), n_dp, n_own),
        ],
        axis=2,
    )
    bias_count = biases.shape[0]
    wide = n_qkv + n_proj
    bias_rows = -(-bias_count // wide)
    bias_rows = -(-bias_rows // 16) * 16
    bias_slots = bias_terms.reshape(n_dp * n_own, bias_count).astype(low)
    bias_slots = jnp.pad(bias_slots, ((0, 0), (0, bias_rows * wide - bias_count)))
    attn_terms = jnp.concatenate(
        [attn_terms, bias_slots.reshape(n_dp * n_own, bias_rows, wide)], axis=1
    )
    attn_tile = lax.psum_scatter(attn_terms, both, scatter_dimension=0).astype(jnp.float32)
    bias_tile = attn_tile[rows:].reshape(-1)[:bias_count]
    dmod_low = d_modulation.astype(low)
    dmod_own = swap_dp(dmod_low.reshape(latents, n_dp, n_ada).transpose(1, 0, 2))
    dmod_own = dmod_own.reshape(n_dp * latents, n_ada)
    cond_terms = jnp.dot(dmod_own, w_ada_rows.T, preferred_element_type=jnp.float32)
    cond_parts = swap_dp(cond_terms.reshape(n_dp, latents, features))
    sigmoid_c = jax.nn.sigmoid(condition)
    grad_cond = jnp.sum(cond_parts, axis=0) * (sigmoid_c * (1.0 + condition * (1.0 - sigmoid_c)))
    dmod_all = gather_own(dmod_own, n_own).reshape(n_own * n_dp * latents, n_ada)
    cond_all = small_all[:, :, : latents * features].reshape(n_own * n_dp * latents, features)
    cond_cols = lax.dynamic_slice_in_dim(cond_all, own_place * rows, rows, 1)
    g_ada = jnp.dot(cond_cols.T, dmod_all, preferred_element_type=jnp.float32)
    tiles = (
        attn_tile[:rows, :n_qkv],
        attn_tile[:rows, n_qkv:],
        fc_tile[:, :n_fc1],
        fc_tile[:, n_fc1:],
        g_ada,
    )
    weights = (w_qkv, w_proj, w_fc1, w_fc2.T, w_ada)
    moments = (mom_qkv, mom_proj, mom_fc1, mom_fc2.T, mom_ada)
    fresh = [momentum_rate * moments[index] + tiles[index] for index in range(5)]
    widths = [n_qkv, n_proj, n_fc1, n_fc2, n_ada]
    fc_rows = jnp.concatenate([fresh[2], fresh[3]], axis=1).astype(low)
    rest_rows = jnp.concatenate([fresh[0], fresh[1], fresh[4]], axis=1).astype(low)
    fc_all = gather_own(fc_rows, n_own).reshape(features, n_fc1 + n_fc2)
    rest_all = gather_own(rest_rows, n_own).reshape(features, n_qkv + n_proj + n_ada)
    low_rows = [
        rest_rows[:, :n_qkv],
        rest_rows[:, n_qkv : n_qkv + n_proj],
        fc_rows[:, :n_fc1],
        fc_rows[:, n_fc1:],
        rest_rows[:, n_qkv + n_proj :],
    ]
    low_all = [
        rest_all[:, :n_qkv],
        rest_all[:, n_qkv : n_qkv + n_proj],
        fc_all[:, :n_fc1],
        fc_all[:, n_fc1:],
        rest_all[:, n_qkv + n_proj :],
    ]
    gram_terms = [
        jnp.dot(low_rows[index], low_all[index].T, preferred_element_type=jnp.float32)
        for index in range(5)
    ]
    slots = jnp.concatenate(
        [jnp.stack(gram_terms), jnp.zeros((n_dp - 5, rows, features), jnp.float32)]
    )
    gram_rows = lax.psum_scatter(slots, "dp", scatter_dimension=0)
    gram = gather_own(gram_rows, n_own).reshape(features, features)
    unit = jnp.eye(features, dtype=jnp.float32)
    magnitude = jnp.sqrt(jnp.sum(gram * unit))
    divisor = magnitude + 1e-07
    gram = gram / (divisor * divisor)
    total = None
    for ns_step in range(NS_ITERS):
        square = fine_dot(gram, gram)
        mixer = coef_first * unit + coef_second * gram + coef_third * square
        if ns_step == NS_ITERS - 1:
            break
        gram = fine_dot(fine_dot(gram, mixer), mixer)
        gram = 0.5 * (gram + gram.T)
        total = mixer if total is None else fine_dot(total, mixer)
    middle = jnp.sum(total * mixer.T) / features
    my_rows = fine_dot(lax.dynamic_slice_in_dim(total, own_place * rows, rows, 0), mixer)
    my_unit = lax.dynamic_slice_in_dim(unit, own_place * rows, rows, 0)
    my_rows = ((my_rows - middle * my_unit) / divisor).astype(low)
    scalars = jnp.stack([middle / divisor, magnitude])
    high_part = scalars.astype(low)
    low_part = (scalars - high_part.astype(jnp.float32)).astype(low)
    extra = jnp.pad(jnp.stack([high_part, low_part]), ((0, 14), (0, features - 2)))
    factors = lax.all_gather(jnp.concatenate([my_rows, extra]), "dp")
    numbers = factors[:, rows].astype(jnp.float32) + factors[:, rows + 1].astype(jnp.float32)
    ortho = [
        numbers[index, 0] * fresh[index]
        + jnp.dot(factors[index, :rows], low_all[index], preferred_element_type=jnp.float32)
        for index in range(5)
    ]
    moment_norms = numbers[:5, 1]
    sides = (n_qkv * n_dp, n_proj * n_dp, n_fc1 * n_dp, n_fc2 * n_dp, n_ada * n_dp)
    updated = [
        weights[index]
        - learn_rate * 0.2 * math.sqrt(max(features, sides[index])) * ortho[index]
        for index in range(5)
    ]
    moment_bias = momentum_rate * bias_mom + bias_tile
    new_bias = biases - bias_rate * moment_bias
    return (
        block_out,
        grad_in,
        grad_cond,
        tiles[0],
        tiles[1],
        tiles[2],
        tiles[3].T,
        tiles[4],
        bias_tile,
        updated[0],
        updated[1],
        updated[2],
        updated[3].T,
        updated[4],
        fresh[0],
        fresh[1],
        fresh[2],
        fresh[3].T,
        fresh[4],
        new_bias,
        moment_bias,
        moment_norms,
    )


def solution(mesh):
    placed = (
        P(("dp", "own"), None, None),
        P(("dp", "own"), None),
        P(("dp", "own"), None, None),
        P("own", "dp"),
        P("own", "dp"),
        P("own", "dp"),
        P("dp", "own"),
        P("own", "dp"),
        P("own", "dp"),
        P("own", "dp"),
        P("own", "dp"),
        P("dp", "own"),
        P("own", "dp"),
        P(("dp", "own")),
        P(("dp", "own")),
    )
    return jax.shard_map(
        per_device,
        mesh=mesh,
        in_specs=placed,
        out_specs=(
            P(("dp", "own"), None, None),
            P(("dp", "own"), None, None),
            P(("dp", "own"), None),
            P("own", "dp"),
            P("own", "dp"),
            P("own", "dp"),
            P("dp", "own"),
            P("own", "dp"),
            P(("dp", "own")),
            P("own", "dp"),
            P("own", "dp"),
            P("own", "dp"),
            P("dp", "own"),
            P("own", "dp"),
            P("own", "dp"),
            P("own", "dp"),
            P("own", "dp"),
            P("dp", "own"),
            P("own", "dp"),
            P(("dp", "own")),
            P(("dp", "own")),
            P(),
        ),
        check_vma=False,
    )
```

```python
import math

import jax
import jax.numpy as jnp
from jax import lax
from jax.experimental import pallas as pl
from jax.experimental.pallas import tpu as pltpu
from jax.sharding import PartitionSpec as P

HEADS = 12
NS_ITERS = 5


momentum_rate = 0.9
learn_rate = 0.15
bias_rate = 0.002
coef_first = 3.4445
coef_second = -4.775
coef_third = 2.0315
gelu_scale = math.sqrt(2.0 / math.pi)
norm_epsilon = 1e-06


def gather_own(piece, count):
    place = lax.axis_index("own")
    whole = jnp.zeros((count,) + piece.shape, piece.dtype)
    whole = lax.dynamic_update_index_in_dim(whole, piece, place, 0)
    for step in range(1, count):
        pairs = [(index, index ^ step) for index in range(count)]
        other = lax.ppermute(piece, "own", pairs)
        whole = lax.dynamic_update_index_in_dim(whole, other, place ^ step, 0)
    return whole


def gather_dp(piece, count):
    return swap_dp(jnp.broadcast_to(piece, (count,) + piece.shape))


def after(value, other):
    return lax.optimization_barrier((value, other))


def own_bits(count):
    return [1 << index for index in range(count.bit_length() - 1)]


def share_z(tile, n_dp):
    n_z = n_dp // 2
    place = lax.axis_index("dp") // 2
    whole = jnp.zeros((n_z,) + tile.shape, tile.dtype)
    whole = lax.dynamic_update_index_in_dim(whole, tile, place, 0)
    for step in range(1, n_z):
        pairs = [(index, index ^ (2 * step)) for index in range(n_dp)]
        whole = lax.dynamic_update_index_in_dim(
            whole, lax.ppermute(tile, "dp", pairs), place ^ step, 0
        )
    return (whole[: n_z // 2], whole[n_z // 2 :])


def orders(n_own):
    bits = own_bits(n_own)
    return (bits, bits[::-1])


def share_own(parts, n_own, index):
    me = lax.axis_index("own")
    result = []
    for part, order in zip(parts, orders(n_own)):
        bit = order[index]
        axis = 1 + len([other for other in order[:index] if other > bit])
        pairs = [(place, place ^ bit) for place in range(n_own)]
        came = lax.ppermute(part, "own", pairs)
        upper = (me & bit) != 0
        result.append(
            jnp.where(upper, jnp.stack([came, part], axis), jnp.stack([part, came], axis))
        )
    return tuple(result)


def share_core(parts, n_dp, n_own, shape):
    mine = jnp.concatenate([part.reshape((part.shape[0], n_own) + shape) for part in parts])
    other = lax.ppermute(mine, "dp", [(index, index ^ 1) for index in range(n_dp)])
    return mine, other


def add_low(left, right):
    total = left.astype(jnp.float32) + right.astype(jnp.float32)
    return total.astype(jnp.bfloat16)


def reduce_core(mine, other, n_dp, n_own):
    came = lax.ppermute(other, "dp", [(index, index ^ 1) for index in range(n_dp)])
    return mine, came


def reduce_halves(mine, came, n_dp, n_own):
    n_z = n_dp // 2
    summed = add_low(mine, came)
    inner = (n_z // 2,) + (2,) * len(own_bits(n_own)) + mine.shape[2:]
    return (summed[: n_z // 2].reshape(inner), summed[n_z // 2 :].reshape(inner))


def reduce_own(parts, n_own, index):
    me = lax.axis_index("own")
    result = []
    for part, order in zip(parts, orders(n_own)):
        bit = order[index]
        left = sorted(order[index:], reverse=True)
        axis = 1 + left.index(bit)
        side = jnp.where((me & bit) != 0, 1, 0)
        keep = lax.dynamic_index_in_dim(part, side, axis, keepdims=False)
        send = lax.dynamic_index_in_dim(part, 1 - side, axis, keepdims=False)
        pairs = [(place, place ^ bit) for place in range(n_own)]
        result.append(add_low(keep, lax.ppermute(send, "own", pairs)))
    return tuple(result)


def reduce_z(parts, n_dp):
    n_z = n_dp // 2
    place = lax.axis_index("dp") // 2
    summed = jnp.concatenate(parts)
    total = lax.dynamic_index_in_dim(summed, place, 0, keepdims=False).astype(jnp.float32)
    for step in range(1, n_z):
        pairs = [(index, index ^ (2 * step)) for index in range(n_dp)]
        send = lax.dynamic_index_in_dim(summed, place ^ step, 0, keepdims=False)
        total = total + lax.ppermute(send, "dp", pairs).astype(jnp.float32)
    return total


GRAM_SLOTS = (2, 4, 3, 0, 5)


def gram_to_owner(terms, slots, n_dp):
    n_z = n_dp // 2
    core, place = lax.axis_index("dp") % 2, lax.axis_index("dp") // 2
    sides = []
    for side in range(2):
        mine = [term for term, slot in zip(terms, slots) if slot % 2 == side]
        if not mine:
            continue
        group = jnp.stack(mine)
        pairs = [(2 * z + 1 - side, 2 * z + side) for z in range(n_z)]
        sides.append((side, group + lax.ppermute(group, "dp", pairs)))

    def term_for(z_index):
        value = None
        for side, group in sides:
            inside = [slot // 2 for slot in slots if slot % 2 == side]
            for index, at in enumerate(inside):
                hit = jnp.logical_and(core == side, z_index == at)
                value = group[index] if value is None else jnp.where(hit, group[index], value)
        return value

    total = term_for(place)
    for step in range(1, n_z):
        pairs = [(slot ^ (2 * step), slot) for slot in slots]
        total = total + lax.ppermute(term_for(place ^ step), "dp", pairs)
    return total


def spread_from_owners(piece, n_dp):
    n_z = n_dp // 2
    core, place = lax.axis_index("dp") % 2, lax.axis_index("dp") // 2
    came = [piece]
    for step in range(1, n_z):
        pairs = [(slot, slot ^ (2 * step)) for slot in GRAM_SLOTS]
        came.append(lax.ppermute(piece, "dp", pairs))
    sides = [[slot for slot in GRAM_SLOTS if slot % 2 == side] for side in range(2)]
    have = []
    for index in range(max(len(side) for side in sides)):
        at = [side[min(index, len(side) - 1)] // 2 for side in sides]
        distance = place ^ jnp.where(core == 0, at[0], at[1])
        value = came[0]
        for step in range(1, n_z):
            value = jnp.where(distance == step, came[step], value)
        have.append(value)
    have = jnp.stack(have)
    other = lax.ppermute(have, "dp", [(index, index ^ 1) for index in range(n_dp)])
    result = []
    for slot in GRAM_SLOTS:
        index = sides[slot % 2].index(slot)
        result.append(jnp.where(core == slot % 2, have[index], other[index]))
    return result


def split_two(value):
    high = value.astype(jnp.bfloat16)
    return high, (value - high.astype(jnp.float32)).astype(jnp.bfloat16)


def chain_kernel(place_ref, gram_ref, rows_ref, middle_ref, a_hi, a_lo, p_hi, p_lo, t_hi, t_lo, r_hi, r_lo):
    side = gram_ref.shape[0]
    rows = rows_ref.shape[0]
    block = 256

    def product(left_hi, left_lo, right_hi, right_lo, start, count):
        here = pl.ds(start, count)
        high = left_hi[here, :]
        dot = lambda x, y: jnp.dot(x, y, preferred_element_type=jnp.float32)
        return (
            dot(high, right_hi[...]) + dot(high, right_lo[...]) + dot(left_lo[here, :], right_hi[...])
        )

    def put(high_ref, low_ref, start, value):
        high, low = split_two(value)
        high_ref[pl.ds(start, block), :] = high
        low_ref[pl.ds(start, block), :] = low

    def each(run):
        def body(index, carry):
            run(pl.multiple_of(index * block, block))
            return carry

        lax.fori_loop(0, side // block, body, 0)

    def polynomial(start):
        square = product(a_hi, a_lo, a_hi, a_lo, start, block)
        here = pl.ds(start, block)
        gram = a_hi[here, :].astype(jnp.float32) + a_lo[here, :].astype(jnp.float32)
        row = lax.broadcasted_iota(jnp.int32, (block, side), 0) + start
        column = lax.broadcasted_iota(jnp.int32, (block, side), 1)
        unit = jnp.where(row == column, coef_first, 0.0)
        put(p_hi, p_lo, start, unit + coef_second * gram + coef_third * square)

    def times(start):
        put(r_hi, r_lo, start, product(a_hi, a_lo, p_hi, p_lo, start, block))

    def again(start):
        put(a_hi, a_lo, start, product(r_hi, r_lo, p_hi, p_lo, start, block))

    def collect(start):
        put(r_hi, r_lo, start, product(t_hi, t_lo, p_hi, p_lo, start, block))

    def store(start):
        here = pl.ds(start, block)
        t_hi[here, :] = r_hi[here, :]
        t_lo[here, :] = r_lo[here, :]

    def store_first(start):
        here = pl.ds(start, block)
        t_hi[here, :] = p_hi[here, :]
        t_lo[here, :] = p_lo[here, :]

    each(lambda start: put(a_hi, a_lo, start, gram_ref[pl.ds(start, block), :]))
    each(polynomial)
    each(store_first)
    each(times)
    each(again)

    def step(index, carry):
        each(polynomial)
        each(collect)
        each(store)
        each(times)
        each(again)
        return carry

    lax.fori_loop(0, NS_ITERS - 2, step, 0)
    each(polynomial)
    middle_ref[...] = jnp.zeros_like(middle_ref)

    def trace(start):
        here = pl.ds(start, block)
        left = t_hi[here, :].astype(jnp.float32) + t_lo[here, :].astype(jnp.float32)
        right = p_hi[here, :].astype(jnp.float32) + p_lo[here, :].astype(jnp.float32)
        middle_ref[...] += jnp.sum(left * right, axis=0, keepdims=True)

    each(trace)
    first = pl.multiple_of(place_ref[0] * rows, rows)
    rows_ref[...] = product(t_hi, t_lo, p_hi, p_lo, first, rows)


def newton_schulz(gram, place, rows):
    side = gram.shape[0]
    return pl.pallas_call(
        chain_kernel,
        grid_spec=pltpu.PrefetchScalarGridSpec(
            num_scalar_prefetch=1,
            grid=(1,),
            in_specs=[pl.BlockSpec((side, side), lambda g, p: (0, 0))],
            out_specs=[
                pl.BlockSpec((rows, side), lambda g, p: (0, 0)),
                pl.BlockSpec((1, side), lambda g, p: (0, 0)),
            ],
            scratch_shapes=[pltpu.VMEM((side, side), jnp.bfloat16)] * 8,
        ),
        out_shape=[
            jax.ShapeDtypeStruct((rows, side), jnp.float32),
            jax.ShapeDtypeStruct((1, side), jnp.float32),
        ],
        compiler_params=pltpu.CompilerParams(vmem_limit_bytes=40 << 20),
    )(place.reshape(1), gram)


def two_cores(n_z):
    mine = lambda g, p: (jnp.minimum(g, n_z - 1), 0, 0, 0, 0)
    other = lambda g, p: (jnp.maximum(g - n_z, 0), 0, 0, 0, 0)
    column = lambda g, p: (0, 2 * (g % n_z) + (p[0] ^ (g // n_z)))
    return mine, other, column


def mlp_forward(core, modulated, mine, other, bias):
    n_z, n_own, _, rows, width = mine.shape
    tokens, features = modulated.shape
    at_mine, at_other, at_column = two_cores(n_z)

    def kernel(core_ref, mod_ref, mine_ref, other_ref, bias_ref, pre_ref, out_ref):
        g = pl.program_id(0)

        @pl.when(g == 0)
        def _():
            out_ref[...] = jnp.zeros_like(out_ref)

        def run(weights):
            first = weights[0, :, 0].reshape(features, width)
            second = weights[0, :, 1].reshape(features, width)
            pre = jnp.dot(mod_ref[...], first, preferred_element_type=jnp.float32) + bias_ref[...]
            pre_ref[...] = pre
            act = gelu_value(pre).astype(jnp.bfloat16)
            out_ref[...] += lax.dot_general(
                act, second, (((1,), (1,)), ((), ())), preferred_element_type=jnp.float32
            )

        @pl.when(g < n_z)
        def _():
            run(mine_ref)

        @pl.when(g >= n_z)
        def _():
            run(other_ref)

    block = (1, n_own, 2, rows, width)
    return pl.pallas_call(
        kernel,
        grid_spec=pltpu.PrefetchScalarGridSpec(
            num_scalar_prefetch=1,
            grid=(2 * n_z,),
            in_specs=[
                pl.BlockSpec((tokens, features), lambda g, p: (0, 0)),
                pl.BlockSpec(block, at_mine),
                pl.BlockSpec(block, at_other),
                pl.BlockSpec((None, 1, width), lambda g, p: (at_column(g, p)[1], 0, 0)),
            ],
            out_specs=[
                pl.BlockSpec((None, tokens, width), lambda g, p: (at_column(g, p)[1], 0, 0)),
                pl.BlockSpec((tokens, features), lambda g, p: (0, 0)),
            ],
        ),
        out_shape=[
            jax.ShapeDtypeStruct((2 * n_z, tokens, width), jnp.float32),
            jax.ShapeDtypeStruct((tokens, features), jnp.float32),
        ],
        compiler_params=pltpu.CompilerParams(vmem_limit_bytes=48 << 20),
    )(core.reshape(1), modulated, mine, other, bias.reshape(2 * n_z, 1, width))


def mlp_backward(core, modulated_t, branch_low, branch_t, pre, mine, other):
    n_z, n_own, _, rows, width = mine.shape
    features, tokens = modulated_t.shape
    at_mine, at_other, at_column = two_cores(n_z)

    def kernel(
        core_ref, mod_ref, low_ref, lowt_ref, pre_ref, mine_ref, other_ref,
        gmine_ref, gother_ref, dmod_ref, gb_ref,
    ):
        g = pl.program_id(0)

        @pl.when(g == 0)
        def _():
            dmod_ref[...] = jnp.zeros_like(dmod_ref)

        def run(weights, grads):
            first = weights[0, :, 0].reshape(features, width)
            second = weights[0, :, 1].reshape(features, width)
            inner = pre_ref[...]
            act = gelu_value(inner).astype(jnp.bfloat16)
            d_act = jnp.dot(low_ref[...], second, preferred_element_type=jnp.float32)
            d_pre = d_act * gelu_slope(inner)
            gb_ref[...] = jnp.sum(d_pre, axis=0, keepdims=True)
            dpre_low = d_pre.astype(jnp.bfloat16)
            g_first = jnp.dot(mod_ref[...], dpre_low, preferred_element_type=jnp.float32)
            g_second = jnp.dot(lowt_ref[...], act, preferred_element_type=jnp.float32)
            grads[0, :, 0] = g_first.astype(jnp.bfloat16).reshape(n_own, rows, width)
            grads[0, :, 1] = g_second.astype(jnp.bfloat16).reshape(n_own, rows, width)
            dmod_ref[...] += lax.dot_general(
                dpre_low, first, (((1,), (1,)), ((), ())), preferred_element_type=jnp.float32
            )

        @pl.when(g < n_z)
        def _():
            run(mine_ref, gmine_ref)

        @pl.when(g >= n_z)
        def _():
            run(other_ref, gother_ref)

    block = (1, n_own, 2, rows, width)
    whole = lambda g, p: (0, 0)
    low = jnp.bfloat16
    grads, others, d_mod, gb = pl.pallas_call(
        kernel,
        grid_spec=pltpu.PrefetchScalarGridSpec(
            num_scalar_prefetch=1,
            grid=(2 * n_z,),
            in_specs=[
                pl.BlockSpec((features, tokens), whole),
                pl.BlockSpec((tokens, features), whole),
                pl.BlockSpec((features, tokens), whole),
                pl.BlockSpec((None, tokens, width), lambda g, p: (at_column(g, p)[1], 0, 0)),
                pl.BlockSpec(block, at_mine),
                pl.BlockSpec(block, at_other),
            ],
            out_specs=[
                pl.BlockSpec(block, at_mine),
                pl.BlockSpec(block, at_other),
                pl.BlockSpec((tokens, features), whole),
                pl.BlockSpec((None, 1, width), lambda g, p: (at_column(g, p)[1], 0, 0)),
            ],
        ),
        out_shape=[
            jax.ShapeDtypeStruct(mine.shape, low),
            jax.ShapeDtypeStruct(mine.shape, low),
            jax.ShapeDtypeStruct((tokens, features), jnp.float32),
            jax.ShapeDtypeStruct((2 * n_z, 1, width), jnp.float32),
        ],
        compiler_params=pltpu.CompilerParams(vmem_limit_bytes=56 << 20),
    )(core.reshape(1), modulated_t, branch_low, branch_t, pre, mine, other)
    return grads, others, d_mod, gb.reshape(-1)


def swap_dp(blocks):
    return lax.all_to_all(blocks, "dp", split_axis=0, concat_axis=0, tiled=True)


def columns_of(blocks, start, width):
    count, rows, _ = blocks.shape
    part = blocks[:, :, start : start + width]
    return part.transpose(1, 0, 2).reshape(rows, count * width)


def batched(form, left, right):
    return jnp.einsum(form, left, right, preferred_element_type=jnp.float32)


def layer_stats(values):
    mean_value = jnp.mean(values, axis=-1, keepdims=True)
    centered = values - mean_value
    inv_std = lax.rsqrt(jnp.mean(centered * centered, axis=-1, keepdims=True) + norm_epsilon)
    return (centered * inv_std, inv_std)


def norm_back(grad_normed, normed, inv_std):
    first = jnp.mean(grad_normed, axis=-1, keepdims=True)
    second = jnp.mean(grad_normed * normed, axis=-1, keepdims=True)
    return inv_std * (grad_normed - first - normed * second)


def gelu_value(inner):
    return 0.5 * inner * (1.0 + jnp.tanh(gelu_scale * (inner + 0.044715 * inner * inner * inner)))


def gelu_slope(inner):
    tangent = jnp.tanh(gelu_scale * (inner + 0.044715 * inner * inner * inner))
    return 0.5 * (1.0 + tangent) + 0.5 * inner * (1.0 - tangent * tangent) * gelu_scale * (
        1.0 + 3.0 * 0.044715 * inner * inner
    )


def attn_gradients(core, modulated_t, attn_t, outer, bias_slots, n_qkv):
    n_dp, tokens, width = outer.shape
    _, n_own, bias_rows, _ = bias_slots.shape
    n_z = n_dp // 2
    features = modulated_t.shape[0]
    rows = features // n_own

    def column(g, p):
        return 2 * (g % n_z) + (p[0] ^ (g // n_z))

    def kernel(core_ref, mod_ref, attn_ref, outer_ref, bias_ref, mine_ref, other_ref):
        g = pl.program_id(0)

        def run(slots):
            left = jnp.dot(mod_ref[...], outer_ref[...], preferred_element_type=jnp.float32)
            right = jnp.dot(attn_ref[...], outer_ref[...], preferred_element_type=jnp.float32)
            lane = lax.broadcasted_iota(jnp.int32, left.shape, 1)
            both = jnp.where(lane < n_qkv, left, right).astype(jnp.bfloat16)
            slots[0, :, :rows] = both.reshape(n_own, rows, width)
            slots[0, :, rows:] = bias_ref[...]

        @pl.when(g < n_z)
        def _():
            run(mine_ref)

        @pl.when(g >= n_z)
        def _():
            run(other_ref)

    whole = lambda g, p: (0, 0)
    block = (1, n_own, rows + bias_rows, width)
    shape = jax.ShapeDtypeStruct((n_z,) + block[1:], jnp.bfloat16)
    return pl.pallas_call(
        kernel,
        grid_spec=pltpu.PrefetchScalarGridSpec(
            num_scalar_prefetch=1,
            grid=(n_dp,),
            in_specs=[
                pl.BlockSpec((features, tokens), whole),
                pl.BlockSpec((features, tokens), whole),
                pl.BlockSpec((None, tokens, width), lambda g, p: (column(g, p), 0, 0)),
                pl.BlockSpec((None, n_own, bias_rows, width), lambda g, p: (column(g, p), 0, 0, 0)),
            ],
            out_specs=[
                pl.BlockSpec(block, lambda g, p: (jnp.minimum(g, n_z - 1), 0, 0, 0)),
                pl.BlockSpec(block, lambda g, p: (jnp.maximum(g - n_z, 0), 0, 0, 0)),
            ],
        ),
        out_shape=[shape, shape],
        compiler_params=pltpu.CompilerParams(vmem_limit_bytes=40 << 20),
    )(core.reshape(1), modulated_t, attn_t, outer, bias_slots)


def block_pass(tokens_in, modulation, cotangent, w_qkv, w_proj, fc_parts, fc_shape, bias_full):
    latents, length, features = tokens_in.shape
    core = lax.axis_index("dp") % 2
    n_dp, n_own = lax.axis_size("dp"), lax.axis_size("own")
    steps = len(own_bits(n_own))
    hidden_units = n_dp * fc_shape[2]
    head_count = HEADS
    head_size = features // head_count
    score_scale = 1.0 / math.sqrt(head_size)
    row_count = latents * length
    b_query = bias_full[:features]
    b_value = bias_full[features : 2 * features]
    b_proj = bias_full[2 * features : 3 * features]
    b_fc1 = bias_full[3 * features : 3 * features + hidden_units]
    b_fc2 = bias_full[3 * features + hidden_units : 4 * features + hidden_units]
    pieces = [
        modulation[:, index * features : (index + 1) * features][:, None, :] for index in range(6)
    ]
    shift_one, scale_one, gate_one, shift_two, scale_two, gate_two = pieces
    residual = tokens_in.astype(jnp.float32)
    normed_one, inv_one = layer_stats(residual)
    modulated_one = (normed_one * (1.0 + scale_one) + shift_one).astype(jnp.bfloat16)
    qkv_proj = jnp.dot(
        modulated_one.reshape(row_count, features), w_qkv, preferred_element_type=jnp.float32
    )
    for index in range(steps - 1):
        fc_parts = share_own(fc_parts, n_own, index)
    qkv_proj, fc_parts = after(qkv_proj, fc_parts)
    qkv_proj = qkv_proj.reshape(latents, length, 3 * features)
    fc_parts = share_own(fc_parts, n_own, steps - 1)
    head_shape = (latents, length, head_count, head_size)
    query_heads = (qkv_proj[..., :features] + b_query).astype(jnp.bfloat16).reshape(head_shape)
    key_heads = qkv_proj[..., features : 2 * features].astype(jnp.bfloat16).reshape(head_shape)
    value_heads = (qkv_proj[..., 2 * features :] + b_value).astype(jnp.bfloat16).reshape(head_shape)
    scores = batched("bqhd,bkhd->bhqk", query_heads, key_heads) * score_scale
    row_max = jnp.max(scores, axis=-1, keepdims=True)
    log_total = row_max + jnp.log(jnp.sum(jnp.exp(scores - row_max), axis=-1, keepdims=True))
    attn_probs = jnp.exp(scores - log_total).astype(jnp.bfloat16)
    attn_out = (
        batched("bhqk,bkhd->bqhd", attn_probs, value_heads)
        .astype(jnp.bfloat16)
        .reshape(row_count, features)
    )
    attn_out, fc_parts = after(attn_out, fc_parts)
    fc_mine, fc_other = share_core(fc_parts, n_dp, n_own, fc_shape)
    branch_one = (jnp.dot(attn_out, w_proj, preferred_element_type=jnp.float32) + b_proj).reshape(
        latents, length, features
    )
    middle = residual + gate_one * branch_one
    normed_two, inv_two = layer_stats(middle)
    modulated_two = (
        (normed_two * (1.0 + scale_two) + shift_two)
        .astype(jnp.bfloat16)
        .reshape(row_count, features)
    )
    fc1_pre, branch_two = mlp_forward(core, modulated_two, fc_mine, fc_other, b_fc1)
    branch_two = (branch_two + b_fc2).reshape(latents, length, features)
    block_out = middle + gate_two * branch_two
    cot_float = cotangent.astype(jnp.float32)
    d_gate_two = jnp.sum(cot_float * branch_two, axis=1)
    d_branch_two = cot_float * gate_two
    dbranch_low = d_branch_two.astype(jnp.bfloat16).reshape(row_count, features)
    gb_fc2 = jnp.sum(d_branch_two, axis=(0, 1))
    fc_terms, fc_others, d_mod_two, gb_fc1 = mlp_backward(
        core, modulated_two.T, dbranch_low, dbranch_low.T, fc1_pre, fc_mine, fc_other
    )
    d_mod_two = d_mod_two.reshape(latents, length, features)
    fc_terms, fc_came = reduce_core(fc_terms, fc_others, n_dp, n_own)
    d_shift_two = jnp.sum(d_mod_two, axis=1)
    d_scale_two = jnp.sum(d_mod_two * normed_two, axis=1)
    d_middle = cot_float + norm_back(d_mod_two * (1.0 + scale_two), normed_two, inv_two)
    d_gate_one = jnp.sum(d_middle * branch_one, axis=1)
    d_branch_one = d_middle * gate_one
    dbranch_one_low = d_branch_one.astype(jnp.bfloat16).reshape(row_count, features)
    gb_proj = jnp.sum(d_branch_one, axis=(0, 1))
    d_attn = (
        jnp.dot(dbranch_one_low, w_proj.T, preferred_element_type=jnp.float32)
        .astype(jnp.bfloat16)
        .reshape(head_shape)
    )
    d_attn, fc_came = after(d_attn, fc_came)
    fc_parts = reduce_halves(fc_terms, fc_came, n_dp, n_own)
    for index in range(steps - 1):
        fc_parts = reduce_own(fc_parts, n_own, index)
    scores_again = batched("bqhd,bkhd->bhqk", query_heads, key_heads) * score_scale
    probs_again = jnp.exp(scores_again - log_total)
    d_probs = batched("bqhd,bkhd->bhqk", d_attn, value_heads)
    delta = jnp.sum(probs_again * d_probs, axis=-1, keepdims=True)
    d_scores = (probs_again * (d_probs - delta) * score_scale).astype(jnp.bfloat16)
    d_query = batched("bhqk,bkhd->bqhd", d_scores, key_heads)
    d_key = batched("bhqk,bqhd->bkhd", d_scores, query_heads)
    d_value = batched("bhqk,bqhd->bkhd", probs_again.astype(jnp.bfloat16), d_attn)
    flat_shape = (latents, length, features)
    d_qkv = jnp.concatenate(
        [d_query.reshape(flat_shape), d_key.reshape(flat_shape), d_value.reshape(flat_shape)],
        axis=-1,
    )
    dqkv_low = d_qkv.astype(jnp.bfloat16).reshape(row_count, 3 * features)
    dqkv_low, fc_parts = after(dqkv_low, fc_parts)
    fc_parts = reduce_own(fc_parts, n_own, steps - 1)
    outer = jnp.concatenate(
        [
            dqkv_low.reshape(row_count, n_dp, 3 * features // n_dp),
            dbranch_one_low.reshape(row_count, n_dp, features // n_dp),
        ],
        axis=2,
    ).transpose(1, 0, 2)
    gb_query = jnp.sum(d_query, axis=(0, 1)).reshape(features)
    gb_value = jnp.sum(d_value, axis=(0, 1)).reshape(features)
    d_mod_one = jnp.dot(dqkv_low, w_qkv.T, preferred_element_type=jnp.float32).reshape(flat_shape)
    d_mod_one, fc_parts = after(d_mod_one, fc_parts)
    fc_tile = reduce_z(fc_parts, n_dp)
    d_shift_one = jnp.sum(d_mod_one, axis=1)
    d_scale_one = jnp.sum(d_mod_one * normed_one, axis=1)
    grad_in = d_middle + norm_back(d_mod_one * (1.0 + scale_one), normed_one, inv_one)
    d_modulation = jnp.concatenate(
        [d_shift_one, d_scale_one, d_gate_one, d_shift_two, d_scale_two, d_gate_two], axis=-1
    )
    gb_ada = jnp.sum(d_modulation, axis=0)
    grad_bias = jnp.concatenate([gb_query, gb_value, gb_proj, gb_fc1, gb_fc2, gb_ada])
    width = outer.shape[2]
    bias_count = grad_bias.shape[0] // (n_dp * n_own)
    bias_rows = -(-bias_count // (16 * width)) * 16
    bias_slots = grad_bias.reshape(n_dp, n_own, bias_count).astype(jnp.bfloat16)
    bias_slots = jnp.pad(bias_slots, ((0, 0), (0, 0), (0, bias_rows * width - bias_count)))
    attn_terms, attn_others = attn_gradients(
        core,
        modulated_one.reshape(row_count, features).T,
        attn_out.T,
        outer,
        bias_slots.reshape(n_dp, n_own, bias_rows, width),
        3 * features // n_dp,
    )
    attn_came = reduce_core(attn_terms, attn_others, n_dp, n_own)[1]
    attn_parts = reduce_halves(attn_terms, attn_came, n_dp, n_own)
    return block_out, grad_in, d_modulation, attn_parts, fc_tile


def per_device(
    tokens_in,
    condition,
    cotangent,
    w_qkv,
    w_proj,
    w_fc1,
    w_fc2,
    w_ada,
    mom_qkv,
    mom_proj,
    mom_fc1,
    mom_fc2,
    mom_ada,
    biases,
    bias_mom,
):
    low = jnp.bfloat16
    n_dp, n_own = lax.axis_size("dp"), lax.axis_size("own")
    dp_place, own_place = lax.axis_index("dp"), lax.axis_index("own")
    latents, features = condition.shape
    rows = w_qkv.shape[0]
    n_qkv, n_proj, n_fc1, n_fc2, n_ada = (
        w_qkv.shape[1],
        w_proj.shape[1],
        w_fc1.shape[1],
        w_fc2.shape[0],
        w_ada.shape[1],
    )
    cond_act = jax.nn.silu(condition).astype(low)
    small = jnp.concatenate([cond_act.reshape(-1), biases.astype(low)])
    small_own = gather_dp(small, n_dp)
    cond_own = small_own[:, : latents * features].reshape(n_dp * latents, features)
    w_ada_rows = gather_own(w_ada.astype(low), n_own).reshape(features, n_ada)
    mod_mine = jnp.dot(cond_own, w_ada_rows, preferred_element_type=jnp.float32)
    mod_parts = swap_dp(mod_mine.reshape(n_dp, latents, n_ada))
    small_all = gather_own(small_own, n_own)
    bias_full = (
        small_all[:, :, latents * features :].transpose(1, 0, 2).reshape(-1).astype(jnp.float32)
    )
    modulation = mod_parts.transpose(1, 0, 2).reshape(latents, n_dp * n_ada)
    modulation = modulation + bias_full[bias_full.shape[0] - n_dp * n_ada :]
    core = dp_place % 2
    first = jnp.concatenate([w_qkv, w_proj], axis=1).astype(low)
    second = jnp.stack([w_fc1, w_fc2.T]).astype(low)
    steps = len(own_bits(n_own))
    first_parts = share_z(first, n_dp)
    second, first_parts = after(second, first_parts)
    fc_parts = share_z(second, n_dp)
    for index in range(steps):
        first_parts = share_own(first_parts, n_own, index)
    fc_parts, first_parts = after(fc_parts, first_parts)
    first_mine, first_other = share_core(first_parts, n_dp, n_own, first.shape)
    first_all = jnp.where(
        core == 0,
        jnp.stack([first_mine, first_other], axis=1),
        jnp.stack([first_other, first_mine], axis=1),
    ).reshape(n_dp, features, n_qkv + n_proj)
    block_out, grad_in, d_modulation, attn_parts, fc_tile = block_pass(
        tokens_in,
        modulation,
        cotangent,
        columns_of(first_all, 0, n_qkv),
        columns_of(first_all, n_qkv, n_proj),
        fc_parts,
        second.shape,
        bias_full,
    )
    for index in range(steps):
        attn_parts = reduce_own(attn_parts, n_own, index)
    attn_tile = reduce_z(attn_parts, n_dp)
    bias_count = biases.shape[0]
    bias_tile = attn_tile[rows:].reshape(-1)[:bias_count]
    dmod_low = d_modulation.astype(low)
    dmod_own = swap_dp(dmod_low.reshape(latents, n_dp, n_ada).transpose(1, 0, 2))
    dmod_own = dmod_own.reshape(n_dp * latents, n_ada)
    cond_terms = jnp.dot(dmod_own, w_ada_rows.T, preferred_element_type=jnp.float32)
    cond_parts = swap_dp(cond_terms.reshape(n_dp, latents, features))
    dmod_all = gather_own(dmod_own, n_own).reshape(n_own * n_dp * latents, n_ada)
    cond_all = small_all[:, :, : latents * features].reshape(n_own * n_dp * latents, features)
    cond_cols = lax.dynamic_slice_in_dim(cond_all, own_place * rows, rows, 1)
    g_ada = jnp.dot(cond_cols.T, dmod_all, preferred_element_type=jnp.float32)
    tiles = (
        attn_tile[:rows, :n_qkv],
        attn_tile[:rows, n_qkv:],
        fc_tile[0],
        fc_tile[1],
        g_ada,
    )
    weights = (w_qkv, w_proj, w_fc1, w_fc2.T, w_ada)
    moments = (mom_qkv, mom_proj, mom_fc1, mom_fc2.T, mom_ada)
    fresh = [momentum_rate * moments[index] + tiles[index] for index in range(5)]
    widths = [n_qkv, n_proj, n_fc1, n_fc2, n_ada]
    fc_rows = jnp.concatenate([fresh[2], fresh[3]], axis=1).astype(low)
    fc_rows, _ = after(fc_rows, attn_parts)
    rest_rows = jnp.concatenate([fresh[0], fresh[1], fresh[4]], axis=1).astype(low)
    fc_all = gather_own(fc_rows, n_own).reshape(features, n_fc1 + n_fc2)
    rest_all = gather_own(rest_rows, n_own).reshape(features, n_qkv + n_proj + n_ada)
    low_rows = [
        rest_rows[:, :n_qkv],
        rest_rows[:, n_qkv : n_qkv + n_proj],
        fc_rows[:, :n_fc1],
        fc_rows[:, n_fc1:],
        rest_rows[:, n_qkv + n_proj :],
    ]
    low_all = [
        rest_all[:, :n_qkv],
        rest_all[:, n_qkv : n_qkv + n_proj],
        fc_all[:, :n_fc1],
        fc_all[:, n_fc1:],
        rest_all[:, n_qkv + n_proj :],
    ]
    gram_terms = [
        jnp.dot(low_rows[index], low_all[index].T, preferred_element_type=jnp.float32)
        for index in range(5)
    ]
    fc_gram = gram_to_owner(gram_terms[2:4], GRAM_SLOTS[2:4], n_dp)
    rest_slots = GRAM_SLOTS[:2] + GRAM_SLOTS[4:]
    rest_gram = gram_to_owner(gram_terms[:2] + gram_terms[4:], rest_slots, n_dp)
    fc_owner = jnp.logical_or(dp_place == GRAM_SLOTS[2], dp_place == GRAM_SLOTS[3])
    gram_rows = jnp.where(fc_owner, fc_gram, rest_gram)
    gram_rows, cond_parts = after(gram_rows, cond_parts)
    gram = gather_own(gram_rows, n_own).reshape(features, features)
    sigmoid_c = jax.nn.sigmoid(condition)
    grad_cond = jnp.sum(cond_parts, axis=0) * (sigmoid_c * (1.0 + condition * (1.0 - sigmoid_c)))
    unit = jnp.eye(features, dtype=jnp.float32)
    magnitude = jnp.sqrt(jnp.sum(gram * unit))
    divisor = magnitude + 1e-07
    gram = gram / (divisor * divisor)
    my_rows, by_column = newton_schulz(gram, own_place, rows)
    middle = jnp.sum(by_column) / features
    my_unit = lax.dynamic_slice_in_dim(unit, own_place * rows, rows, 0)
    my_rows = ((my_rows - middle * my_unit) / divisor).astype(low)
    scalars = jnp.stack([middle / divisor, magnitude])
    high_part = scalars.astype(low)
    low_part = (scalars - high_part.astype(jnp.float32)).astype(low)
    extra = jnp.pad(jnp.stack([high_part, low_part]), ((0, 14), (0, features - 2)))
    factors = spread_from_owners(jnp.concatenate([my_rows, extra]), n_dp)
    numbers = [
        factor[rows, :2].astype(jnp.float32) + factor[rows + 1, :2].astype(jnp.float32)
        for factor in factors
    ]
    ortho = [
        numbers[index][0] * fresh[index]
        + jnp.dot(factors[index][:rows], low_all[index], preferred_element_type=jnp.float32)
        for index in range(5)
    ]
    moment_norms = jnp.stack([number[1] for number in numbers])
    sides = (n_qkv * n_dp, n_proj * n_dp, n_fc1 * n_dp, n_fc2 * n_dp, n_ada * n_dp)
    updated = [
        weights[index]
        - learn_rate * 0.2 * math.sqrt(max(features, sides[index])) * ortho[index]
        for index in range(5)
    ]
    moment_bias = momentum_rate * bias_mom + bias_tile
    new_bias = biases - bias_rate * moment_bias
    return (
        block_out,
        grad_in,
        grad_cond,
        tiles[0],
        tiles[1],
        tiles[2],
        tiles[3].T,
        tiles[4],
        bias_tile,
        updated[0],
        updated[1],
        updated[2],
        updated[3].T,
        updated[4],
        fresh[0],
        fresh[1],
        fresh[2],
        fresh[3].T,
        fresh[4],
        new_bias,
        moment_bias,
        moment_norms,
    )


def solution(mesh):
    placed = (
        P(("dp", "own"), None, None),
        P(("dp", "own"), None),
        P(("dp", "own"), None, None),
        P("own", "dp"),
        P("own", "dp"),
        P("own", "dp"),
        P("dp", "own"),
        P("own", "dp"),
        P("own", "dp"),
        P("own", "dp"),
        P("own", "dp"),
        P("dp", "own"),
        P("own", "dp"),
        P(("dp", "own")),
        P(("dp", "own")),
    )
    return jax.shard_map(
        per_device,
        mesh=mesh,
        in_specs=placed,
        out_specs=(
            P(("dp", "own"), None, None),
            P(("dp", "own"), None, None),
            P(("dp", "own"), None),
            P("own", "dp"),
            P("own", "dp"),
            P("own", "dp"),
            P("dp", "own"),
            P("own", "dp"),
            P(("dp", "own")),
            P("own", "dp"),
            P("own", "dp"),
            P("own", "dp"),
            P("dp", "own"),
            P("own", "dp"),
            P("own", "dp"),
            P("own", "dp"),
            P("own", "dp"),
            P("dp", "own"),
            P("own", "dp"),
            P(("dp", "own")),
            P(("dp", "own")),
            P(),
        ),
        check_vma=False,
    )
```

```python
import math

import jax
import jax.numpy as jnp
from jax import lax
from jax.experimental import pallas as pl
from jax.experimental.pallas import tpu as pltpu
from jax.sharding import PartitionSpec as P

HEADS = 12
NS_ITERS = 5


momentum_rate = 0.9
learn_rate = 0.15
bias_rate = 0.002
coef_first = 3.4445
coef_second = -4.775
coef_third = 2.0315
gelu_scale = math.sqrt(2.0 / math.pi)
norm_epsilon = 1e-06


def gather_own(piece, count):
    place = lax.axis_index("own")
    whole = jnp.zeros((count,) + piece.shape, piece.dtype)
    whole = lax.dynamic_update_index_in_dim(whole, piece, place, 0)
    for step in range(1, count):
        pairs = [(index, index ^ step) for index in range(count)]
        other = lax.ppermute(piece, "own", pairs)
        whole = lax.dynamic_update_index_in_dim(whole, other, place ^ step, 0)
    return whole


def gather_dp(piece, count):
    return swap_dp(jnp.broadcast_to(piece, (count,) + piece.shape))


def after(value, other):
    return lax.optimization_barrier((value, other))


def own_bits(count):
    return [1 << index for index in range(count.bit_length() - 1)]


def share_z(tile, n_dp):
    n_z = n_dp // 2
    place = lax.axis_index("dp") // 2
    whole = jnp.zeros((n_z,) + tile.shape, tile.dtype)
    whole = lax.dynamic_update_index_in_dim(whole, tile, place, 0)
    for step in range(1, n_z):
        pairs = [(index, index ^ (2 * step)) for index in range(n_dp)]
        whole = lax.dynamic_update_index_in_dim(
            whole, lax.ppermute(tile, "dp", pairs), place ^ step, 0
        )
    return (whole[: n_z // 2], whole[n_z // 2 :])


def orders(n_own):
    bits = own_bits(n_own)
    return (bits, bits[::-1])


def share_send(parts, n_own, index):
    result = []
    for part, order in zip(parts, orders(n_own)):
        pairs = [(place, place ^ order[index]) for place in range(n_own)]
        result.append(lax.ppermute(part, "own", pairs))
    return tuple(result)


def share_merge(parts, arrived, n_own, index):
    me = lax.axis_index("own")
    result = []
    for part, came, order in zip(parts, arrived, orders(n_own)):
        bit = order[index]
        axis = 1 + len([other for other in order[:index] if other > bit])
        upper = (me & bit) != 0
        result.append(
            jnp.where(upper, jnp.stack([came, part], axis), jnp.stack([part, came], axis))
        )
    return tuple(result)


def share_core(parts, n_dp, n_own, shape):
    mine = jnp.concatenate([part.reshape((part.shape[0], n_own) + shape) for part in parts])
    other = lax.ppermute(mine, "dp", [(index, index ^ 1) for index in range(n_dp)])
    return mine, other


def add_low(left, right):
    total = left.astype(jnp.float32) + right.astype(jnp.float32)
    return total.astype(jnp.bfloat16)


def reduce_core(mine, other, n_dp, n_own):
    came = lax.ppermute(other, "dp", [(index, index ^ 1) for index in range(n_dp)])
    return mine, came


def reduce_halves(mine, came, n_dp, n_own):
    n_z = n_dp // 2
    summed = add_low(mine, came)
    inner = (n_z // 2,) + (2,) * len(own_bits(n_own)) + mine.shape[2:]
    return (summed[: n_z // 2].reshape(inner), summed[n_z // 2 :].reshape(inner))


def reduce_own(parts, n_own, index):
    me = lax.axis_index("own")
    result = []
    for part, order in zip(parts, orders(n_own)):
        bit = order[index]
        left = sorted(order[index:], reverse=True)
        axis = 1 + left.index(bit)
        side = jnp.where((me & bit) != 0, 1, 0)
        keep = lax.dynamic_index_in_dim(part, side, axis, keepdims=False)
        send = lax.dynamic_index_in_dim(part, 1 - side, axis, keepdims=False)
        pairs = [(place, place ^ bit) for place in range(n_own)]
        result.append(add_low(keep, lax.ppermute(send, "own", pairs)))
    return tuple(result)


def reduce_z(parts, n_dp):
    n_z = n_dp // 2
    place = lax.axis_index("dp") // 2
    summed = jnp.concatenate(parts)
    total = lax.dynamic_index_in_dim(summed, place, 0, keepdims=False)
    arrived = []
    for step in range(1, n_z):
        pairs = [(index, index ^ (2 * step)) for index in range(n_dp)]
        send = lax.dynamic_index_in_dim(summed, place ^ step, 0, keepdims=False)
        arrived.append(lax.ppermute(send, "dp", pairs))
    return total, tuple(arrived)


def add_arrived(total, arrived):
    total = total.astype(jnp.float32)
    for came in arrived:
        total = total + came.astype(jnp.float32)
    return total


GRAM_SLOTS = (2, 4, 3, 0, 5)


def gram_to_owner(terms, slots, n_dp):
    n_z = n_dp // 2
    core, place = lax.axis_index("dp") % 2, lax.axis_index("dp") // 2
    sides = []
    for side in range(2):
        mine = [term for term, slot in zip(terms, slots) if slot % 2 == side]
        if not mine:
            continue
        group = jnp.stack(mine)
        pairs = [(2 * z + 1 - side, 2 * z + side) for z in range(n_z)]
        sides.append((side, group + lax.ppermute(group, "dp", pairs)))

    def term_for(z_index):
        value = None
        for side, group in sides:
            inside = [slot // 2 for slot in slots if slot % 2 == side]
            for index, at in enumerate(inside):
                hit = jnp.logical_and(core == side, z_index == at)
                value = group[index] if value is None else jnp.where(hit, group[index], value)
        return value

    total = term_for(place)
    for step in range(1, n_z):
        pairs = [(slot ^ (2 * step), slot) for slot in slots]
        total = total + lax.ppermute(term_for(place ^ step), "dp", pairs)
    return total


def spread_from_owners(piece, n_dp):
    n_z = n_dp // 2
    core, place = lax.axis_index("dp") % 2, lax.axis_index("dp") // 2
    came = [piece]
    for step in range(1, n_z):
        pairs = [(slot, slot ^ (2 * step)) for slot in GRAM_SLOTS]
        came.append(lax.ppermute(piece, "dp", pairs))
    sides = [[slot for slot in GRAM_SLOTS if slot % 2 == side] for side in range(2)]
    have = []
    for index in range(max(len(side) for side in sides)):
        at = [side[min(index, len(side) - 1)] // 2 for side in sides]
        distance = place ^ jnp.where(core == 0, at[0], at[1])
        value = came[0]
        for step in range(1, n_z):
            value = jnp.where(distance == step, came[step], value)
        have.append(value)
    have = jnp.stack(have)
    other = lax.ppermute(have, "dp", [(index, index ^ 1) for index in range(n_dp)])
    result = []
    for slot in GRAM_SLOTS:
        index = sides[slot % 2].index(slot)
        result.append(jnp.where(core == slot % 2, have[index], other[index]))
    return result


def split_two(value):
    high = value.astype(jnp.bfloat16)
    return high, (value - high.astype(jnp.float32)).astype(jnp.bfloat16)


def chain_kernel(place_ref, gram_ref, rows_ref, middle_ref, a_hi, a_lo, p_hi, p_lo, t_hi, t_lo, r_hi, r_lo):
    side = gram_ref.shape[0]
    rows = rows_ref.shape[0]
    block = 256

    def product(left_hi, left_lo, right_hi, right_lo, rows_at, columns_at):
        high = left_hi[rows_at, :]
        dot = lambda x, y: jnp.dot(x, y, preferred_element_type=jnp.float32)
        return (
            dot(high, right_hi[:, columns_at])
            + dot(high, right_lo[:, columns_at])
            + dot(left_lo[rows_at, :], right_hi[:, columns_at])
        )

    def put(high_ref, low_ref, start, value):
        high, low = split_two(value)
        high_ref[pl.ds(start, block), start:] = high
        low_ref[pl.ds(start, block), start:] = low
        for column in range(start + block, side, block):
            inside = slice(column - start, column - start + block)
            high_ref[pl.ds(column, block), start : start + block] = high[:, inside].T
            low_ref[pl.ds(column, block), start : start + block] = low[:, inside].T

    def each(run):
        for start in range(0, side, block):
            run(start)

    def upper(left_hi, left_lo, right_hi, right_lo, start):
        return product(
            left_hi, left_lo, right_hi, right_lo, pl.ds(start, block), slice(start, side)
        )

    def polynomial(start):
        square = upper(a_hi, a_lo, a_hi, a_lo, start)
        here = pl.ds(start, block)
        gram = a_hi[here, start:].astype(jnp.float32) + a_lo[here, start:].astype(jnp.float32)
        row = lax.broadcasted_iota(jnp.int32, (block, side - start), 0)
        column = lax.broadcasted_iota(jnp.int32, (block, side - start), 1)
        unit = jnp.where(row == column, coef_first, 0.0)
        put(p_hi, p_lo, start, unit + coef_second * gram + coef_third * square)

    def times(start):
        put(r_hi, r_lo, start, upper(a_hi, a_lo, p_hi, p_lo, start))

    def again(start):
        put(a_hi, a_lo, start, upper(r_hi, r_lo, p_hi, p_lo, start))

    def collect(start):
        put(r_hi, r_lo, start, upper(t_hi, t_lo, p_hi, p_lo, start))

    def store(start):
        here = pl.ds(start, block)
        t_hi[here, :] = r_hi[here, :]
        t_lo[here, :] = r_lo[here, :]

    def store_first(start):
        here = pl.ds(start, block)
        t_hi[here, :] = p_hi[here, :]
        t_lo[here, :] = p_lo[here, :]

    each(lambda start: put(a_hi, a_lo, start, gram_ref[pl.ds(start, block), start:]))
    each(polynomial)
    each(store_first)
    each(times)
    each(again)

    def step(index, carry):
        each(polynomial)
        each(collect)
        each(store)
        each(times)
        each(again)
        return carry

    lax.fori_loop(0, NS_ITERS - 2, step, 0)
    each(polynomial)
    middle_ref[...] = jnp.zeros_like(middle_ref)

    def trace(start):
        here = pl.ds(start, block)
        left = t_hi[here, :].astype(jnp.float32) + t_lo[here, :].astype(jnp.float32)
        right = p_hi[here, :].astype(jnp.float32) + p_lo[here, :].astype(jnp.float32)
        middle_ref[...] += jnp.sum(left * right, axis=0, keepdims=True)

    each(trace)
    first = pl.multiple_of(place_ref[0] * rows, rows)
    rows_ref[...] = product(t_hi, t_lo, p_hi, p_lo, pl.ds(first, rows), slice(0, side))


def newton_schulz(gram, place, rows):
    side = gram.shape[0]
    return pl.pallas_call(
        chain_kernel,
        grid_spec=pltpu.PrefetchScalarGridSpec(
            num_scalar_prefetch=1,
            grid=(1,),
            in_specs=[pl.BlockSpec((side, side), lambda g, p: (0, 0))],
            out_specs=[
                pl.BlockSpec((rows, side), lambda g, p: (0, 0)),
                pl.BlockSpec((1, side), lambda g, p: (0, 0)),
            ],
            scratch_shapes=[pltpu.VMEM((side, side), jnp.bfloat16)] * 8,
        ),
        out_shape=[
            jax.ShapeDtypeStruct((rows, side), jnp.float32),
            jax.ShapeDtypeStruct((1, side), jnp.float32),
        ],
        compiler_params=pltpu.CompilerParams(vmem_limit_bytes=40 << 20),
    )(place.reshape(1), gram)


def two_cores(n_z):
    mine = lambda g, p: (jnp.minimum(g, n_z - 1), 0, 0, 0, 0)
    other = lambda g, p: (jnp.maximum(g - n_z, 0), 0, 0, 0, 0)
    column = lambda g, p: (0, 2 * (g % n_z) + (p[0] ^ (g // n_z)))
    return mine, other, column


def mlp_forward(core, modulated, mine, other, bias):
    n_z, n_own, _, rows, width = mine.shape
    tokens, features = modulated.shape
    at_mine, at_other, at_column = two_cores(n_z)

    def kernel(core_ref, mod_ref, mine_ref, other_ref, bias_ref, pre_ref, out_ref):
        g = pl.program_id(0)

        @pl.when(g == 0)
        def _():
            out_ref[...] = jnp.zeros_like(out_ref)

        def run(weights):
            first = weights[0, :, 0].reshape(features, width)
            second = weights[0, :, 1].reshape(features, width)
            pre = jnp.dot(mod_ref[...], first, preferred_element_type=jnp.float32) + bias_ref[...]
            pre_ref[...] = pre
            act = gelu_value(pre).astype(jnp.bfloat16)
            out_ref[...] += lax.dot_general(
                act, second, (((1,), (1,)), ((), ())), preferred_element_type=jnp.float32
            )

        @pl.when(g < n_z)
        def _():
            run(mine_ref)

        @pl.when(g >= n_z)
        def _():
            run(other_ref)

    block = (1, n_own, 2, rows, width)
    return pl.pallas_call(
        kernel,
        grid_spec=pltpu.PrefetchScalarGridSpec(
            num_scalar_prefetch=1,
            grid=(2 * n_z,),
            in_specs=[
                pl.BlockSpec((tokens, features), lambda g, p: (0, 0)),
                pl.BlockSpec(block, at_mine),
                pl.BlockSpec(block, at_other),
                pl.BlockSpec((None, 1, width), lambda g, p: (at_column(g, p)[1], 0, 0)),
            ],
            out_specs=[
                pl.BlockSpec((None, tokens, width), lambda g, p: (at_column(g, p)[1], 0, 0)),
                pl.BlockSpec((tokens, features), lambda g, p: (0, 0)),
            ],
        ),
        out_shape=[
            jax.ShapeDtypeStruct((2 * n_z, tokens, width), jnp.float32),
            jax.ShapeDtypeStruct((tokens, features), jnp.float32),
        ],
        compiler_params=pltpu.CompilerParams(vmem_limit_bytes=48 << 20),
    )(core.reshape(1), modulated, mine, other, bias.reshape(2 * n_z, 1, width))


def mlp_backward(core, modulated_t, branch_low, branch_t, pre, mine, other):
    n_z, n_own, _, rows, width = mine.shape
    features, tokens = modulated_t.shape
    at_mine, at_other, at_column = two_cores(n_z)

    def kernel(
        core_ref, mod_ref, low_ref, lowt_ref, pre_ref, mine_ref, other_ref,
        gmine_ref, gother_ref, dmod_ref, gb_ref,
    ):
        g = pl.program_id(0)

        @pl.when(g == 0)
        def _():
            dmod_ref[...] = jnp.zeros_like(dmod_ref)

        def run(weights, grads):
            first = weights[0, :, 0].reshape(features, width)
            second = weights[0, :, 1].reshape(features, width)
            inner = pre_ref[...]
            act = gelu_value(inner).astype(jnp.bfloat16)
            d_act = jnp.dot(low_ref[...], second, preferred_element_type=jnp.float32)
            d_pre = d_act * gelu_slope(inner)
            gb_ref[...] = jnp.sum(d_pre, axis=0, keepdims=True)
            dpre_low = d_pre.astype(jnp.bfloat16)
            g_first = jnp.dot(mod_ref[...], dpre_low, preferred_element_type=jnp.float32)
            g_second = jnp.dot(lowt_ref[...], act, preferred_element_type=jnp.float32)
            grads[0, :, 0] = g_first.astype(jnp.bfloat16).reshape(n_own, rows, width)
            grads[0, :, 1] = g_second.astype(jnp.bfloat16).reshape(n_own, rows, width)
            dmod_ref[...] += lax.dot_general(
                dpre_low, first, (((1,), (1,)), ((), ())), preferred_element_type=jnp.float32
            )

        @pl.when(g < n_z)
        def _():
            run(mine_ref, gmine_ref)

        @pl.when(g >= n_z)
        def _():
            run(other_ref, gother_ref)

    block = (1, n_own, 2, rows, width)
    whole = lambda g, p: (0, 0)
    low = jnp.bfloat16
    grads, others, d_mod, gb = pl.pallas_call(
        kernel,
        grid_spec=pltpu.PrefetchScalarGridSpec(
            num_scalar_prefetch=1,
            grid=(2 * n_z,),
            in_specs=[
                pl.BlockSpec((features, tokens), whole),
                pl.BlockSpec((tokens, features), whole),
                pl.BlockSpec((features, tokens), whole),
                pl.BlockSpec((None, tokens, width), lambda g, p: (at_column(g, p)[1], 0, 0)),
                pl.BlockSpec(block, at_mine),
                pl.BlockSpec(block, at_other),
            ],
            out_specs=[
                pl.BlockSpec(block, at_mine),
                pl.BlockSpec(block, at_other),
                pl.BlockSpec((tokens, features), whole),
                pl.BlockSpec((None, 1, width), lambda g, p: (at_column(g, p)[1], 0, 0)),
            ],
        ),
        out_shape=[
            jax.ShapeDtypeStruct(mine.shape, low),
            jax.ShapeDtypeStruct(mine.shape, low),
            jax.ShapeDtypeStruct((tokens, features), jnp.float32),
            jax.ShapeDtypeStruct((2 * n_z, 1, width), jnp.float32),
        ],
        compiler_params=pltpu.CompilerParams(vmem_limit_bytes=56 << 20),
    )(core.reshape(1), modulated_t, branch_low, branch_t, pre, mine, other)
    return grads, others, d_mod, gb.reshape(-1)


def swap_dp(blocks):
    return lax.all_to_all(blocks, "dp", split_axis=0, concat_axis=0, tiled=True)


def columns_of(blocks, start, width):
    count, rows, _ = blocks.shape
    part = blocks[:, :, start : start + width]
    return part.transpose(1, 0, 2).reshape(rows, count * width)


def batched(form, left, right):
    return jnp.einsum(form, left, right, preferred_element_type=jnp.float32)


def layer_stats(values):
    mean_value = jnp.mean(values, axis=-1, keepdims=True)
    centered = values - mean_value
    inv_std = lax.rsqrt(jnp.mean(centered * centered, axis=-1, keepdims=True) + norm_epsilon)
    return (centered * inv_std, inv_std)


def norm_back(grad_normed, normed, inv_std):
    first = jnp.mean(grad_normed, axis=-1, keepdims=True)
    second = jnp.mean(grad_normed * normed, axis=-1, keepdims=True)
    return inv_std * (grad_normed - first - normed * second)


def gelu_value(inner):
    return 0.5 * inner * (1.0 + jnp.tanh(gelu_scale * (inner + 0.044715 * inner * inner * inner)))


def gelu_slope(inner):
    tangent = jnp.tanh(gelu_scale * (inner + 0.044715 * inner * inner * inner))
    return 0.5 * (1.0 + tangent) + 0.5 * inner * (1.0 - tangent * tangent) * gelu_scale * (
        1.0 + 3.0 * 0.044715 * inner * inner
    )


def attn_gradients(core, modulated_t, attn_t, outer, bias_slots, n_qkv):
    n_dp, tokens, width = outer.shape
    _, n_own, bias_rows, _ = bias_slots.shape
    n_z = n_dp // 2
    features = modulated_t.shape[0]
    rows = features // n_own

    def column(g, p):
        return 2 * (g % n_z) + (p[0] ^ (g // n_z))

    def kernel(core_ref, mod_ref, attn_ref, outer_ref, bias_ref, mine_ref, other_ref):
        g = pl.program_id(0)

        def run(slots):
            left = jnp.dot(mod_ref[...], outer_ref[...], preferred_element_type=jnp.float32)
            right = jnp.dot(attn_ref[...], outer_ref[...], preferred_element_type=jnp.float32)
            lane = lax.broadcasted_iota(jnp.int32, left.shape, 1)
            both = jnp.where(lane < n_qkv, left, right).astype(jnp.bfloat16)
            slots[0, :, :rows] = both.reshape(n_own, rows, width)
            slots[0, :, rows:] = bias_ref[...]

        @pl.when(g < n_z)
        def _():
            run(mine_ref)

        @pl.when(g >= n_z)
        def _():
            run(other_ref)

    whole = lambda g, p: (0, 0)
    block = (1, n_own, rows + bias_rows, width)
    shape = jax.ShapeDtypeStruct((n_z,) + block[1:], jnp.bfloat16)
    return pl.pallas_call(
        kernel,
        grid_spec=pltpu.PrefetchScalarGridSpec(
            num_scalar_prefetch=1,
            grid=(n_dp,),
            in_specs=[
                pl.BlockSpec((features, tokens), whole),
                pl.BlockSpec((features, tokens), whole),
                pl.BlockSpec((None, tokens, width), lambda g, p: (column(g, p), 0, 0)),
                pl.BlockSpec((None, n_own, bias_rows, width), lambda g, p: (column(g, p), 0, 0, 0)),
            ],
            out_specs=[
                pl.BlockSpec(block, lambda g, p: (jnp.minimum(g, n_z - 1), 0, 0, 0)),
                pl.BlockSpec(block, lambda g, p: (jnp.maximum(g - n_z, 0), 0, 0, 0)),
            ],
        ),
        out_shape=[shape, shape],
        compiler_params=pltpu.CompilerParams(vmem_limit_bytes=40 << 20),
    )(core.reshape(1), modulated_t, attn_t, outer, bias_slots)


def block_pass(tokens_in, modulation, cotangent, w_qkv, w_proj, fc_parts, fc_shape, bias_full):
    latents, length, features = tokens_in.shape
    core = lax.axis_index("dp") % 2
    n_dp, n_own = lax.axis_size("dp"), lax.axis_size("own")
    steps = len(own_bits(n_own))
    hidden_units = n_dp * fc_shape[2]
    head_count = HEADS
    head_size = features // head_count
    score_scale = 1.0 / math.sqrt(head_size)
    row_count = latents * length
    b_query = bias_full[:features]
    b_value = bias_full[features : 2 * features]
    b_proj = bias_full[2 * features : 3 * features]
    b_fc1 = bias_full[3 * features : 3 * features + hidden_units]
    b_fc2 = bias_full[3 * features + hidden_units : 4 * features + hidden_units]
    pieces = [
        modulation[:, index * features : (index + 1) * features][:, None, :] for index in range(6)
    ]
    shift_one, scale_one, gate_one, shift_two, scale_two, gate_two = pieces
    residual = tokens_in.astype(jnp.float32)
    normed_one, inv_one = layer_stats(residual)
    modulated_one = (normed_one * (1.0 + scale_one) + shift_one).astype(jnp.bfloat16)
    qkv_proj = jnp.dot(
        modulated_one.reshape(row_count, features), w_qkv, preferred_element_type=jnp.float32
    )
    for index in range(steps - 2):
        fc_parts = share_merge(fc_parts, share_send(fc_parts, n_own, index), n_own, index)
    came = share_send(fc_parts, n_own, steps - 2)
    qkv_proj, came = after(qkv_proj, came)
    fc_parts = share_merge(fc_parts, came, n_own, steps - 2)
    qkv_proj = qkv_proj.reshape(latents, length, 3 * features)
    came = share_send(fc_parts, n_own, steps - 1)
    head_shape = (latents, length, head_count, head_size)
    query_heads = (qkv_proj[..., :features] + b_query).astype(jnp.bfloat16).reshape(head_shape)
    key_heads = qkv_proj[..., features : 2 * features].astype(jnp.bfloat16).reshape(head_shape)
    value_heads = (qkv_proj[..., 2 * features :] + b_value).astype(jnp.bfloat16).reshape(head_shape)
    scores = batched("bqhd,bkhd->bhqk", query_heads, key_heads) * score_scale
    row_max = jnp.max(scores, axis=-1, keepdims=True)
    log_total = row_max + jnp.log(jnp.sum(jnp.exp(scores - row_max), axis=-1, keepdims=True))
    attn_probs = jnp.exp(scores - log_total).astype(jnp.bfloat16)
    attn_out = (
        batched("bhqk,bkhd->bqhd", attn_probs, value_heads)
        .astype(jnp.bfloat16)
        .reshape(row_count, features)
    )
    attn_out, came = after(attn_out, came)
    fc_parts = share_merge(fc_parts, came, n_own, steps - 1)
    fc_mine, fc_other = share_core(fc_parts, n_dp, n_own, fc_shape)
    branch_one = (jnp.dot(attn_out, w_proj, preferred_element_type=jnp.float32) + b_proj).reshape(
        latents, length, features
    )
    middle = residual + gate_one * branch_one
    normed_two, inv_two = layer_stats(middle)
    modulated_two = (
        (normed_two * (1.0 + scale_two) + shift_two)
        .astype(jnp.bfloat16)
        .reshape(row_count, features)
    )
    fc1_pre, branch_two = mlp_forward(core, modulated_two, fc_mine, fc_other, b_fc1)
    branch_two = (branch_two + b_fc2).reshape(latents, length, features)
    block_out = middle + gate_two * branch_two
    cot_float = cotangent.astype(jnp.float32)
    d_gate_two = jnp.sum(cot_float * branch_two, axis=1)
    d_branch_two = cot_float * gate_two
    dbranch_low = d_branch_two.astype(jnp.bfloat16).reshape(row_count, features)
    gb_fc2 = jnp.sum(d_branch_two, axis=(0, 1))
    fc_terms, fc_others, d_mod_two, gb_fc1 = mlp_backward(
        core, modulated_two.T, dbranch_low, dbranch_low.T, fc1_pre, fc_mine, fc_other
    )
    d_mod_two = d_mod_two.reshape(latents, length, features)
    fc_terms, fc_came = reduce_core(fc_terms, fc_others, n_dp, n_own)
    d_shift_two = jnp.sum(d_mod_two, axis=1)
    d_scale_two = jnp.sum(d_mod_two * normed_two, axis=1)
    d_middle = cot_float + norm_back(d_mod_two * (1.0 + scale_two), normed_two, inv_two)
    d_gate_one = jnp.sum(d_middle * branch_one, axis=1)
    d_branch_one = d_middle * gate_one
    dbranch_one_low = d_branch_one.astype(jnp.bfloat16).reshape(row_count, features)
    gb_proj = jnp.sum(d_branch_one, axis=(0, 1))
    d_attn = (
        jnp.dot(dbranch_one_low, w_proj.T, preferred_element_type=jnp.float32)
        .astype(jnp.bfloat16)
        .reshape(head_shape)
    )
    d_attn, fc_came = after(d_attn, fc_came)
    fc_parts = reduce_halves(fc_terms, fc_came, n_dp, n_own)
    for index in range(steps - 1):
        fc_parts = reduce_own(fc_parts, n_own, index)
    scores_again = batched("bqhd,bkhd->bhqk", query_heads, key_heads) * score_scale
    probs_again = jnp.exp(scores_again - log_total)
    d_probs = batched("bqhd,bkhd->bhqk", d_attn, value_heads)
    delta = jnp.sum(probs_again * d_probs, axis=-1, keepdims=True)
    d_scores = (probs_again * (d_probs - delta) * score_scale).astype(jnp.bfloat16)
    d_query = batched("bhqk,bkhd->bqhd", d_scores, key_heads)
    d_key = batched("bhqk,bqhd->bkhd", d_scores, query_heads)
    d_value = batched("bhqk,bqhd->bkhd", probs_again.astype(jnp.bfloat16), d_attn)
    flat_shape = (latents, length, features)
    d_qkv = jnp.concatenate(
        [d_query.reshape(flat_shape), d_key.reshape(flat_shape), d_value.reshape(flat_shape)],
        axis=-1,
    )
    dqkv_low = d_qkv.astype(jnp.bfloat16).reshape(row_count, 3 * features)
    dqkv_low, fc_parts = after(dqkv_low, fc_parts)
    fc_parts = reduce_own(fc_parts, n_own, steps - 1)
    outer = jnp.concatenate(
        [
            dqkv_low.reshape(row_count, n_dp, 3 * features // n_dp),
            dbranch_one_low.reshape(row_count, n_dp, features // n_dp),
        ],
        axis=2,
    ).transpose(1, 0, 2)
    gb_query = jnp.sum(d_query, axis=(0, 1)).reshape(features)
    gb_value = jnp.sum(d_value, axis=(0, 1)).reshape(features)
    d_mod_one = jnp.dot(dqkv_low, w_qkv.T, preferred_element_type=jnp.float32).reshape(flat_shape)
    d_mod_one, fc_parts = after(d_mod_one, fc_parts)
    fc_sums = reduce_z(fc_parts, n_dp)
    d_shift_one = jnp.sum(d_mod_one, axis=1)
    d_scale_one = jnp.sum(d_mod_one * normed_one, axis=1)
    grad_in = d_middle + norm_back(d_mod_one * (1.0 + scale_one), normed_one, inv_one)
    d_modulation = jnp.concatenate(
        [d_shift_one, d_scale_one, d_gate_one, d_shift_two, d_scale_two, d_gate_two], axis=-1
    )
    gb_ada = jnp.sum(d_modulation, axis=0)
    grad_bias = jnp.concatenate([gb_query, gb_value, gb_proj, gb_fc1, gb_fc2, gb_ada])
    width = outer.shape[2]
    bias_count = grad_bias.shape[0] // (n_dp * n_own)
    bias_rows = -(-bias_count // (16 * width)) * 16
    bias_slots = grad_bias.reshape(n_dp, n_own, bias_count).astype(jnp.bfloat16)
    bias_slots = jnp.pad(bias_slots, ((0, 0), (0, 0), (0, bias_rows * width - bias_count)))
    attn_terms, attn_others = attn_gradients(
        core,
        modulated_one.reshape(row_count, features).T,
        attn_out.T,
        outer,
        bias_slots.reshape(n_dp, n_own, bias_rows, width),
        3 * features // n_dp,
    )
    attn_came = reduce_core(attn_terms, attn_others, n_dp, n_own)[1]
    attn_parts = reduce_halves(attn_terms, attn_came, n_dp, n_own)
    return block_out, grad_in, d_modulation, attn_parts, fc_sums


def per_device(
    tokens_in,
    condition,
    cotangent,
    w_qkv,
    w_proj,
    w_fc1,
    w_fc2,
    w_ada,
    mom_qkv,
    mom_proj,
    mom_fc1,
    mom_fc2,
    mom_ada,
    biases,
    bias_mom,
):
    low = jnp.bfloat16
    n_dp, n_own = lax.axis_size("dp"), lax.axis_size("own")
    dp_place, own_place = lax.axis_index("dp"), lax.axis_index("own")
    latents, features = condition.shape
    rows = w_qkv.shape[0]
    n_qkv, n_proj, n_fc1, n_fc2, n_ada = (
        w_qkv.shape[1],
        w_proj.shape[1],
        w_fc1.shape[1],
        w_fc2.shape[0],
        w_ada.shape[1],
    )
    cond_act = jax.nn.silu(condition).astype(low)
    small = jnp.concatenate([cond_act.reshape(-1), biases.astype(low)])
    small_own = gather_dp(small, n_dp)
    cond_own = small_own[:, : latents * features].reshape(n_dp * latents, features)
    w_ada_rows = gather_own(w_ada.astype(low), n_own).reshape(features, n_ada)
    mod_mine = jnp.dot(cond_own, w_ada_rows, preferred_element_type=jnp.float32)
    mod_parts = swap_dp(mod_mine.reshape(n_dp, latents, n_ada))
    small_all = gather_own(small_own, n_own)
    bias_full = (
        small_all[:, :, latents * features :].transpose(1, 0, 2).reshape(-1).astype(jnp.float32)
    )
    core = dp_place % 2
    first = jnp.concatenate([w_qkv, w_proj], axis=1).astype(low)
    second = jnp.stack([w_fc1, w_fc2.T]).astype(low)
    steps = len(own_bits(n_own))
    first_parts = share_z(first, n_dp)
    second, first_parts = after(second, first_parts)
    fc_parts = share_z(second, n_dp)
    for index in range(steps):
        came = share_send(first_parts, n_own, index)
        if index == 0:
            mod_parts, came = after(mod_parts, came)
        first_parts = share_merge(first_parts, came, n_own, index)
    fc_parts, first_parts = after(fc_parts, first_parts)
    first_mine, first_other = share_core(first_parts, n_dp, n_own, first.shape)
    first_all = jnp.where(
        core == 0,
        jnp.stack([first_mine, first_other], axis=1),
        jnp.stack([first_other, first_mine], axis=1),
    ).reshape(n_dp, features, n_qkv + n_proj)
    modulation = mod_parts.transpose(1, 0, 2).reshape(latents, n_dp * n_ada)
    modulation = modulation + bias_full[bias_full.shape[0] - n_dp * n_ada :]
    block_out, grad_in, d_modulation, attn_parts, fc_sums = block_pass(
        tokens_in,
        modulation,
        cotangent,
        columns_of(first_all, 0, n_qkv),
        columns_of(first_all, n_qkv, n_proj),
        fc_parts,
        second.shape,
        bias_full,
    )
    for index in range(steps):
        attn_parts = reduce_own(attn_parts, n_own, index)
    fc_sums, attn_parts = after(fc_sums, attn_parts)
    fc_tile = add_arrived(*fc_sums)
    attn_tile = add_arrived(*reduce_z(attn_parts, n_dp))
    bias_count = biases.shape[0]
    bias_tile = attn_tile[rows:].reshape(-1)[:bias_count]
    dmod_low = d_modulation.astype(low)
    dmod_own = swap_dp(dmod_low.reshape(latents, n_dp, n_ada).transpose(1, 0, 2))
    dmod_own = dmod_own.reshape(n_dp * latents, n_ada)
    cond_terms = jnp.dot(dmod_own, w_ada_rows.T, preferred_element_type=jnp.float32)
    cond_parts = swap_dp(cond_terms.reshape(n_dp, latents, features))
    dmod_all = gather_own(dmod_own, n_own).reshape(n_own * n_dp * latents, n_ada)
    cond_all = small_all[:, :, : latents * features].reshape(n_own * n_dp * latents, features)
    cond_cols = lax.dynamic_slice_in_dim(cond_all, own_place * rows, rows, 1)
    g_ada = jnp.dot(cond_cols.T, dmod_all, preferred_element_type=jnp.float32)
    tiles = (
        attn_tile[:rows, :n_qkv],
        attn_tile[:rows, n_qkv:],
        fc_tile[0],
        fc_tile[1],
        g_ada,
    )
    weights = (w_qkv, w_proj, w_fc1, w_fc2.T, w_ada)
    moments = (mom_qkv, mom_proj, mom_fc1, mom_fc2.T, mom_ada)
    fresh = [momentum_rate * moments[index] + tiles[index] for index in range(5)]
    widths = [n_qkv, n_proj, n_fc1, n_fc2, n_ada]
    fc_rows = jnp.concatenate([fresh[2], fresh[3]], axis=1).astype(low)
    rest_rows = jnp.concatenate([fresh[0], fresh[1], fresh[4]], axis=1).astype(low)
    fc_all = gather_own(fc_rows, n_own).reshape(features, n_fc1 + n_fc2)
    rest_all = gather_own(rest_rows, n_own).reshape(features, n_qkv + n_proj + n_ada)
    low_rows = [
        rest_rows[:, :n_qkv],
        rest_rows[:, n_qkv : n_qkv + n_proj],
        fc_rows[:, :n_fc1],
        fc_rows[:, n_fc1:],
        rest_rows[:, n_qkv + n_proj :],
    ]
    low_all = [
        rest_all[:, :n_qkv],
        rest_all[:, n_qkv : n_qkv + n_proj],
        fc_all[:, :n_fc1],
        fc_all[:, n_fc1:],
        rest_all[:, n_qkv + n_proj :],
    ]
    gram_terms = [
        jnp.dot(low_rows[index], low_all[index].T, preferred_element_type=jnp.float32)
        for index in range(5)
    ]
    fc_gram = gram_to_owner(gram_terms[2:4], GRAM_SLOTS[2:4], n_dp)
    rest_slots = GRAM_SLOTS[:2] + GRAM_SLOTS[4:]
    rest_gram = gram_to_owner(gram_terms[:2] + gram_terms[4:], rest_slots, n_dp)
    fc_owner = jnp.logical_or(dp_place == GRAM_SLOTS[2], dp_place == GRAM_SLOTS[3])
    gram_rows = jnp.where(fc_owner, fc_gram, rest_gram)
    gram_rows, cond_parts = after(gram_rows, cond_parts)
    gram = gather_own(gram_rows, n_own).reshape(features, features)
    sigmoid_c = jax.nn.sigmoid(condition)
    grad_cond = jnp.sum(cond_parts, axis=0) * (sigmoid_c * (1.0 + condition * (1.0 - sigmoid_c)))
    unit = jnp.eye(features, dtype=jnp.float32)
    magnitude = jnp.sqrt(jnp.sum(gram * unit))
    divisor = magnitude + 1e-07
    gram = gram / (divisor * divisor)
    my_rows, by_column = newton_schulz(gram, own_place, rows)
    middle = jnp.sum(by_column) / features
    my_unit = lax.dynamic_slice_in_dim(unit, own_place * rows, rows, 0)
    my_rows = ((my_rows - middle * my_unit) / divisor).astype(low)
    scalars = jnp.stack([middle / divisor, magnitude])
    high_part = scalars.astype(low)
    low_part = (scalars - high_part.astype(jnp.float32)).astype(low)
    extra = jnp.pad(jnp.stack([high_part, low_part]), ((0, 14), (0, features - 2)))
    factors = spread_from_owners(jnp.concatenate([my_rows, extra]), n_dp)
    numbers = [
        factor[rows, :2].astype(jnp.float32) + factor[rows + 1, :2].astype(jnp.float32)
        for factor in factors
    ]
    ortho = [
        numbers[index][0] * fresh[index]
        + jnp.dot(factors[index][:rows], low_all[index], preferred_element_type=jnp.float32)
        for index in range(5)
    ]
    position = lax.iota(jnp.int32, 5)
    moment_norms = sum(jnp.where(position == index, numbers[index][1], 0.0) for index in range(5))
    sides = (n_qkv * n_dp, n_proj * n_dp, n_fc1 * n_dp, n_fc2 * n_dp, n_ada * n_dp)
    updated = [
        weights[index]
        - learn_rate * 0.2 * math.sqrt(max(features, sides[index])) * ortho[index]
        for index in range(5)
    ]
    moment_bias = momentum_rate * bias_mom + bias_tile
    new_bias = biases - bias_rate * moment_bias
    return (
        block_out,
        grad_in,
        grad_cond,
        tiles[0],
        tiles[1],
        tiles[2],
        tiles[3].T,
        tiles[4],
        bias_tile,
        updated[0],
        updated[1],
        updated[2],
        updated[3].T,
        updated[4],
        fresh[0],
        fresh[1],
        fresh[2],
        fresh[3].T,
        fresh[4],
        new_bias,
        moment_bias,
        moment_norms,
    )


def solution(mesh):
    placed = (
        P(("dp", "own"), None, None),
        P(("dp", "own"), None),
        P(("dp", "own"), None, None),
        P("own", "dp"),
        P("own", "dp"),
        P("own", "dp"),
        P("dp", "own"),
        P("own", "dp"),
        P("own", "dp"),
        P("own", "dp"),
        P("own", "dp"),
        P("dp", "own"),
        P("own", "dp"),
        P(("dp", "own")),
        P(("dp", "own")),
    )
    return jax.shard_map(
        per_device,
        mesh=mesh,
        in_specs=placed,
        out_specs=(
            P(("dp", "own"), None, None),
            P(("dp", "own"), None, None),
            P(("dp", "own"), None),
            P("own", "dp"),
            P("own", "dp"),
            P("own", "dp"),
            P("dp", "own"),
            P("own", "dp"),
            P(("dp", "own")),
            P("own", "dp"),
            P("own", "dp"),
            P("own", "dp"),
            P("dp", "own"),
            P("own", "dp"),
            P("own", "dp"),
            P("own", "dp"),
            P("own", "dp"),
            P("dp", "own"),
            P("own", "dp"),
            P(("dp", "own")),
            P(("dp", "own")),
            P(),
        ),
        check_vma=False,
    )
```

```python
import math

import jax
import jax.numpy as jnp
from jax import lax
from jax.experimental import pallas as pl
from jax.experimental.pallas import tpu as pltpu
from jax.sharding import PartitionSpec as P

HEADS = 12
NS_ITERS = 5


momentum_rate = 0.9
learn_rate = 0.15
bias_rate = 0.002
coef_first = 3.4445
coef_second = -4.775
coef_third = 2.0315
gelu_scale = math.sqrt(2.0 / math.pi)
norm_epsilon = 1e-06


def gather_own(piece, count):
    place = lax.axis_index("own")
    whole = jnp.zeros((count,) + piece.shape, piece.dtype)
    whole = lax.dynamic_update_index_in_dim(whole, piece, place, 0)
    for step in range(1, count):
        pairs = [(index, index ^ step) for index in range(count)]
        other = lax.ppermute(piece, "own", pairs)
        whole = lax.dynamic_update_index_in_dim(whole, other, place ^ step, 0)
    return whole


def gather_dp(piece, count):
    return swap_dp(jnp.broadcast_to(piece, (count,) + piece.shape))


def after(value, other):
    return lax.optimization_barrier((value, other))


def own_bits(count):
    return [1 << index for index in range(count.bit_length() - 1)]


def share_z(tile, n_dp):
    n_z = n_dp // 2
    place = lax.axis_index("dp") // 2
    whole = jnp.zeros((n_z,) + tile.shape, tile.dtype)
    whole = lax.dynamic_update_index_in_dim(whole, tile, place, 0)
    for step in range(1, n_z):
        pairs = [(index, index ^ (2 * step)) for index in range(n_dp)]
        whole = lax.dynamic_update_index_in_dim(
            whole, lax.ppermute(tile, "dp", pairs), place ^ step, 0
        )
    return (whole[: n_z // 2], whole[n_z // 2 :])


def orders(n_own):
    bits = own_bits(n_own)
    return (bits, bits[::-1])


def share_send(parts, n_own, index):
    result = []
    for part, order in zip(parts, orders(n_own)):
        pairs = [(place, place ^ order[index]) for place in range(n_own)]
        result.append(lax.ppermute(part, "own", pairs))
    return tuple(result)


def share_merge(parts, arrived, n_own, index):
    me = lax.axis_index("own")
    result = []
    for part, came, order in zip(parts, arrived, orders(n_own)):
        bit = order[index]
        axis = 1 + len([other for other in order[:index] if other > bit])
        upper = (me & bit) != 0
        result.append(
            jnp.where(upper, jnp.stack([came, part], axis), jnp.stack([part, came], axis))
        )
    return tuple(result)


def share_core(parts, n_dp, n_own, shape):
    mine = jnp.concatenate([part.reshape((part.shape[0], n_own) + shape) for part in parts])
    other = lax.ppermute(mine, "dp", [(index, index ^ 1) for index in range(n_dp)])
    return mine, other


def add_low(left, right):
    total = left.astype(jnp.float32) + right.astype(jnp.float32)
    return total.astype(jnp.bfloat16)


def reduce_core(mine, other, n_dp, n_own):
    came = lax.ppermute(other, "dp", [(index, index ^ 1) for index in range(n_dp)])
    return mine, came


def reduce_halves(mine, came, n_dp, n_own):
    n_z = n_dp // 2
    summed = add_low(mine, came)
    inner = (n_z // 2,) + (2,) * len(own_bits(n_own)) + mine.shape[2:]
    return (summed[: n_z // 2].reshape(inner), summed[n_z // 2 :].reshape(inner))


def reduce_own(parts, n_own, index):
    me = lax.axis_index("own")
    result = []
    for part, order in zip(parts, orders(n_own)):
        bit = order[index]
        left = sorted(order[index:], reverse=True)
        axis = 1 + left.index(bit)
        side = jnp.where((me & bit) != 0, 1, 0)
        keep = lax.dynamic_index_in_dim(part, side, axis, keepdims=False)
        send = lax.dynamic_index_in_dim(part, 1 - side, axis, keepdims=False)
        pairs = [(place, place ^ bit) for place in range(n_own)]
        result.append(add_low(keep, lax.ppermute(send, "own", pairs)))
    return tuple(result)


def reduce_z(parts, n_dp):
    n_z = n_dp // 2
    place = lax.axis_index("dp") // 2
    summed = jnp.concatenate(parts)
    total = lax.dynamic_index_in_dim(summed, place, 0, keepdims=False)
    arrived = []
    for step in range(1, n_z):
        pairs = [(index, index ^ (2 * step)) for index in range(n_dp)]
        send = lax.dynamic_index_in_dim(summed, place ^ step, 0, keepdims=False)
        arrived.append(lax.ppermute(send, "dp", pairs))
    return total, tuple(arrived)


def add_arrived(total, arrived):
    total = total.astype(jnp.float32)
    for came in arrived:
        total = total + came.astype(jnp.float32)
    return total


GRAM_SLOTS = (2, 4, 3, 0, 5)


def gram_to_owner(terms, slots, n_dp):
    n_z = n_dp // 2
    core, place = lax.axis_index("dp") % 2, lax.axis_index("dp") // 2
    sides = []
    for side in range(2):
        mine = [term for term, slot in zip(terms, slots) if slot % 2 == side]
        if not mine:
            continue
        group = jnp.stack(mine)
        pairs = [(2 * z + 1 - side, 2 * z + side) for z in range(n_z)]
        sides.append((side, group + lax.ppermute(group, "dp", pairs)))

    def term_for(z_index):
        value = None
        for side, group in sides:
            inside = [slot // 2 for slot in slots if slot % 2 == side]
            for index, at in enumerate(inside):
                hit = jnp.logical_and(core == side, z_index == at)
                value = group[index] if value is None else jnp.where(hit, group[index], value)
        return value

    total = term_for(place)
    for step in range(1, n_z):
        pairs = [(slot ^ (2 * step), slot) for slot in slots]
        total = total + lax.ppermute(term_for(place ^ step), "dp", pairs)
    return total


def spread_from_owners(piece, n_dp):
    n_z = n_dp // 2
    core, place = lax.axis_index("dp") % 2, lax.axis_index("dp") // 2
    came = [piece]
    for step in range(1, n_z):
        pairs = [(slot, slot ^ (2 * step)) for slot in GRAM_SLOTS]
        came.append(lax.ppermute(piece, "dp", pairs))
    sides = [[slot for slot in GRAM_SLOTS if slot % 2 == side] for side in range(2)]
    have = []
    for index in range(max(len(side) for side in sides)):
        at = [side[min(index, len(side) - 1)] // 2 for side in sides]
        distance = place ^ jnp.where(core == 0, at[0], at[1])
        value = came[0]
        for step in range(1, n_z):
            value = jnp.where(distance == step, came[step], value)
        have.append(value)
    have = jnp.stack(have)
    other = lax.ppermute(have, "dp", [(index, index ^ 1) for index in range(n_dp)])
    result = []
    for slot in GRAM_SLOTS:
        index = sides[slot % 2].index(slot)
        result.append(jnp.where(core == slot % 2, have[index], other[index]))
    return result


def split_two(value):
    high = value.astype(jnp.bfloat16)
    return high, (value - high.astype(jnp.float32)).astype(jnp.bfloat16)


def chain_kernel(place_ref, gram_ref, rows_ref, middle_ref, a_hi, a_lo, p_hi, p_lo, t_hi, t_lo, r_hi, r_lo):
    side = gram_ref.shape[0]
    rows = rows_ref.shape[0]
    block = 256

    def product(left_hi, left_lo, right_hi, right_lo, rows_at, columns_at):
        high = left_hi[rows_at, :]
        dot = lambda x, y: jnp.dot(x, y, preferred_element_type=jnp.float32)
        return (
            dot(high, right_hi[:, columns_at])
            + dot(high, right_lo[:, columns_at])
            + dot(left_lo[rows_at, :], right_hi[:, columns_at])
        )

    def put(high_ref, low_ref, start, value):
        high, low = split_two(value)
        high_ref[pl.ds(start, block), start:] = high
        low_ref[pl.ds(start, block), start:] = low
        for column in range(start + block, side, block):
            inside = slice(column - start, column - start + block)
            high_ref[pl.ds(column, block), start : start + block] = high[:, inside].T
            low_ref[pl.ds(column, block), start : start + block] = low[:, inside].T

    def each(run):
        for start in range(0, side, block):
            run(start)

    def upper(left_hi, left_lo, right_hi, right_lo, start):
        return product(
            left_hi, left_lo, right_hi, right_lo, pl.ds(start, block), slice(start, side)
        )

    def polynomial(start):
        square = upper(a_hi, a_lo, a_hi, a_lo, start)
        here = pl.ds(start, block)
        gram = a_hi[here, start:].astype(jnp.float32) + a_lo[here, start:].astype(jnp.float32)
        row = lax.broadcasted_iota(jnp.int32, (block, side - start), 0)
        column = lax.broadcasted_iota(jnp.int32, (block, side - start), 1)
        unit = jnp.where(row == column, coef_first, 0.0)
        put(p_hi, p_lo, start, unit + coef_second * gram + coef_third * square)

    def times(start):
        put(r_hi, r_lo, start, upper(a_hi, a_lo, p_hi, p_lo, start))

    def again(start):
        put(a_hi, a_lo, start, upper(r_hi, r_lo, p_hi, p_lo, start))

    def collect(start):
        put(r_hi, r_lo, start, upper(t_hi, t_lo, p_hi, p_lo, start))

    def store(start):
        here = pl.ds(start, block)
        t_hi[here, :] = r_hi[here, :]
        t_lo[here, :] = r_lo[here, :]

    def store_first(start):
        here = pl.ds(start, block)
        t_hi[here, :] = p_hi[here, :]
        t_lo[here, :] = p_lo[here, :]

    each(lambda start: put(a_hi, a_lo, start, gram_ref[pl.ds(start, block), start:]))
    each(polynomial)
    each(store_first)
    each(times)
    each(again)

    def step(index, carry):
        each(polynomial)
        each(collect)
        each(store)
        each(times)
        each(again)
        return carry

    lax.fori_loop(0, NS_ITERS - 2, step, 0)
    each(polynomial)
    middle_ref[...] = jnp.zeros_like(middle_ref)

    def trace(start):
        here = pl.ds(start, block)
        left = t_hi[here, :].astype(jnp.float32) + t_lo[here, :].astype(jnp.float32)
        right = p_hi[here, :].astype(jnp.float32) + p_lo[here, :].astype(jnp.float32)
        middle_ref[...] += jnp.sum(left * right, axis=0, keepdims=True)

    each(trace)
    first = pl.multiple_of(place_ref[0] * rows, rows)
    rows_ref[...] = product(t_hi, t_lo, p_hi, p_lo, pl.ds(first, rows), slice(0, side))


def newton_schulz(gram, place, rows):
    side = gram.shape[0]
    return pl.pallas_call(
        chain_kernel,
        grid_spec=pltpu.PrefetchScalarGridSpec(
            num_scalar_prefetch=1,
            grid=(1,),
            in_specs=[pl.BlockSpec((side, side), lambda g, p: (0, 0))],
            out_specs=[
                pl.BlockSpec((rows, side), lambda g, p: (0, 0)),
                pl.BlockSpec((1, side), lambda g, p: (0, 0)),
            ],
            scratch_shapes=[pltpu.VMEM((side, side), jnp.bfloat16)] * 8,
        ),
        out_shape=[
            jax.ShapeDtypeStruct((rows, side), jnp.float32),
            jax.ShapeDtypeStruct((1, side), jnp.float32),
        ],
        compiler_params=pltpu.CompilerParams(vmem_limit_bytes=40 << 20),
    )(place.reshape(1), gram)


def two_cores(n_z):
    mine = lambda g, p: (jnp.minimum(g, n_z - 1), 0, 0, 0, 0)
    other = lambda g, p: (jnp.maximum(g - n_z, 0), 0, 0, 0, 0)
    column = lambda g, p: (0, 2 * (g % n_z) + (p[0] ^ (g // n_z)))
    return mine, other, column


def mlp_forward(core, modulated, mine, other, bias):
    n_z, n_own, _, rows, width = mine.shape
    tokens, features = modulated.shape
    at_mine, at_other, at_column = two_cores(n_z)

    def kernel(core_ref, mod_ref, mine_ref, other_ref, bias_ref, pre_ref, out_ref):
        g = pl.program_id(0)

        @pl.when(g == 0)
        def _():
            out_ref[...] = jnp.zeros_like(out_ref)

        def run(weights):
            first = weights[0, :, 0].reshape(features, width)
            second = weights[0, :, 1].reshape(features, width)
            pre = jnp.dot(mod_ref[...], first, preferred_element_type=jnp.float32) + bias_ref[...]
            pre_ref[...] = pre
            act = gelu_value(pre).astype(jnp.bfloat16)
            out_ref[...] += lax.dot_general(
                act, second, (((1,), (1,)), ((), ())), preferred_element_type=jnp.float32
            )

        @pl.when(g < n_z)
        def _():
            run(mine_ref)

        @pl.when(g >= n_z)
        def _():
            run(other_ref)

    block = (1, n_own, 2, rows, width)
    return pl.pallas_call(
        kernel,
        grid_spec=pltpu.PrefetchScalarGridSpec(
            num_scalar_prefetch=1,
            grid=(2 * n_z,),
            in_specs=[
                pl.BlockSpec((tokens, features), lambda g, p: (0, 0)),
                pl.BlockSpec(block, at_mine),
                pl.BlockSpec(block, at_other),
                pl.BlockSpec((None, 1, width), lambda g, p: (at_column(g, p)[1], 0, 0)),
            ],
            out_specs=[
                pl.BlockSpec((None, tokens, width), lambda g, p: (at_column(g, p)[1], 0, 0)),
                pl.BlockSpec((tokens, features), lambda g, p: (0, 0)),
            ],
        ),
        out_shape=[
            jax.ShapeDtypeStruct((2 * n_z, tokens, width), jnp.float32),
            jax.ShapeDtypeStruct((tokens, features), jnp.float32),
        ],
        compiler_params=pltpu.CompilerParams(vmem_limit_bytes=48 << 20),
    )(core.reshape(1), modulated, mine, other, bias.reshape(2 * n_z, 1, width))


def mlp_backward(core, modulated_t, branch_low, branch_t, pre, mine, other):
    n_z, n_own, _, rows, width = mine.shape
    features, tokens = modulated_t.shape
    at_mine, at_other, at_column = two_cores(n_z)

    def kernel(
        core_ref, mod_ref, low_ref, lowt_ref, pre_ref, mine_ref, other_ref,
        gmine_ref, gother_ref, dmod_ref, gb_ref,
    ):
        g = pl.program_id(0)

        @pl.when(g == 0)
        def _():
            dmod_ref[...] = jnp.zeros_like(dmod_ref)

        def run(weights, grads):
            first = weights[0, :, 0].reshape(features, width)
            second = weights[0, :, 1].reshape(features, width)
            inner = pre_ref[...]
            act = gelu_value(inner).astype(jnp.bfloat16)
            d_act = jnp.dot(low_ref[...], second, preferred_element_type=jnp.float32)
            d_pre = d_act * gelu_slope(inner)
            gb_ref[...] = jnp.sum(d_pre, axis=0, keepdims=True)
            dpre_low = d_pre.astype(jnp.bfloat16)
            g_first = jnp.dot(mod_ref[...], dpre_low, preferred_element_type=jnp.float32)
            g_second = jnp.dot(lowt_ref[...], act, preferred_element_type=jnp.float32)
            grads[0, :, 0] = g_first.astype(jnp.bfloat16).reshape(n_own, rows, width)
            grads[0, :, 1] = g_second.astype(jnp.bfloat16).reshape(n_own, rows, width)
            dmod_ref[...] += lax.dot_general(
                dpre_low, first, (((1,), (1,)), ((), ())), preferred_element_type=jnp.float32
            )

        @pl.when(g < n_z)
        def _():
            run(mine_ref, gmine_ref)

        @pl.when(g >= n_z)
        def _():
            run(other_ref, gother_ref)

    block = (1, n_own, 2, rows, width)
    whole = lambda g, p: (0, 0)
    low = jnp.bfloat16
    grads, others, d_mod, gb = pl.pallas_call(
        kernel,
        grid_spec=pltpu.PrefetchScalarGridSpec(
            num_scalar_prefetch=1,
            grid=(2 * n_z,),
            in_specs=[
                pl.BlockSpec((features, tokens), whole),
                pl.BlockSpec((tokens, features), whole),
                pl.BlockSpec((features, tokens), whole),
                pl.BlockSpec((None, tokens, width), lambda g, p: (at_column(g, p)[1], 0, 0)),
                pl.BlockSpec(block, at_mine),
                pl.BlockSpec(block, at_other),
            ],
            out_specs=[
                pl.BlockSpec(block, at_mine),
                pl.BlockSpec(block, at_other),
                pl.BlockSpec((tokens, features), whole),
                pl.BlockSpec((None, 1, width), lambda g, p: (at_column(g, p)[1], 0, 0)),
            ],
        ),
        out_shape=[
            jax.ShapeDtypeStruct(mine.shape, low),
            jax.ShapeDtypeStruct(mine.shape, low),
            jax.ShapeDtypeStruct((tokens, features), jnp.float32),
            jax.ShapeDtypeStruct((2 * n_z, 1, width), jnp.float32),
        ],
        compiler_params=pltpu.CompilerParams(vmem_limit_bytes=56 << 20),
    )(core.reshape(1), modulated_t, branch_low, branch_t, pre, mine, other)
    return grads, others, d_mod, gb.reshape(-1)


def swap_dp(blocks):
    return lax.all_to_all(blocks, "dp", split_axis=0, concat_axis=0, tiled=True)


def columns_of(blocks, start, width):
    count, rows, _ = blocks.shape
    part = blocks[:, :, start : start + width]
    return part.transpose(1, 0, 2).reshape(rows, count * width)


def batched(form, left, right):
    return jnp.einsum(form, left, right, preferred_element_type=jnp.float32)


def layer_stats(values):
    mean_value = jnp.mean(values, axis=-1, keepdims=True)
    centered = values - mean_value
    inv_std = lax.rsqrt(jnp.mean(centered * centered, axis=-1, keepdims=True) + norm_epsilon)
    return (centered * inv_std, inv_std)


def norm_back(grad_normed, normed, inv_std):
    first = jnp.mean(grad_normed, axis=-1, keepdims=True)
    second = jnp.mean(grad_normed * normed, axis=-1, keepdims=True)
    return inv_std * (grad_normed - first - normed * second)


def gelu_value(inner):
    return 0.5 * inner * (1.0 + jnp.tanh(gelu_scale * (inner + 0.044715 * inner * inner * inner)))


def gelu_slope(inner):
    tangent = jnp.tanh(gelu_scale * (inner + 0.044715 * inner * inner * inner))
    return 0.5 * (1.0 + tangent) + 0.5 * inner * (1.0 - tangent * tangent) * gelu_scale * (
        1.0 + 3.0 * 0.044715 * inner * inner
    )


def attention_backward(query, key, value, d_out, length, head_size):
    rows, features = query.shape
    lanes = 2 * head_size
    scale = 1.0 / math.sqrt(head_size)

    def kernel(q_ref, k_ref, v_ref, d_ref, dq_ref, dk_ref, dv_ref, gq_ref, gv_ref):
        lane = lax.broadcasted_iota(jnp.int32, (length, lanes), 1)
        q, k, v, d = q_ref[...], k_ref[...], v_ref[...], d_ref[...]
        nothing = jnp.zeros_like(q)
        across = (((1,), (1,)), ((), ()))
        pieces = []
        for head in range(2):
            mine = (lane // head_size) == head
            scores = lax.dot_general(
                jnp.where(mine, q, nothing), k, across, preferred_element_type=jnp.float32
            )
            scores = scores * scale
            top = jnp.max(scores, axis=1, keepdims=True)
            log_total = top + jnp.log(jnp.sum(jnp.exp(scores - top), axis=1, keepdims=True))
            probs = jnp.exp(scores - log_total)
            d_probs = lax.dot_general(
                jnp.where(mine, d, nothing), v, across, preferred_element_type=jnp.float32
            )
            delta = jnp.sum(probs * d_probs, axis=1, keepdims=True)
            d_scores = probs * (d_probs - delta) * scale
            low_scores = d_scores.astype(jnp.bfloat16)
            dot = lambda x, y: jnp.dot(x, y, preferred_element_type=jnp.float32)
            pieces.append(
                (
                    dot(low_scores, k),
                    dot(low_scores.T, q),
                    dot(probs.astype(jnp.bfloat16).T, d),
                )
            )
        first = lane < head_size
        dq, dk, dv = [jnp.where(first, *pair) for pair in zip(*pieces)]
        dq_ref[...] = dq.astype(jnp.bfloat16)
        dk_ref[...] = dk.astype(jnp.bfloat16)
        dv_ref[...] = dv.astype(jnp.bfloat16)

        @pl.when(pl.program_id(1) == 0)
        def _():
            gq_ref[...] = jnp.zeros_like(gq_ref)
            gv_ref[...] = jnp.zeros_like(gv_ref)

        gq_ref[...] += jnp.sum(dq, axis=0, keepdims=True)
        gv_ref[...] += jnp.sum(dv, axis=0, keepdims=True)

    block = pl.BlockSpec((length, lanes), lambda pair, latent: (latent, pair))
    total = pl.BlockSpec((1, lanes), lambda pair, latent: (0, pair))
    low = jax.ShapeDtypeStruct((rows, features), jnp.bfloat16)
    sums = jax.ShapeDtypeStruct((1, features), jnp.float32)
    return pl.pallas_call(
        kernel,
        grid=(features // lanes, rows // length),
        in_specs=[block] * 4,
        out_specs=[block] * 3 + [total] * 2,
        out_shape=[low] * 3 + [sums] * 2,
    )(query, key, value, d_out)


def attn_gradients(core, modulated_t, attn_t, outer, bias_slots, n_qkv):
    n_dp, tokens, width = outer.shape
    _, n_own, bias_rows, _ = bias_slots.shape
    n_z = n_dp // 2
    features = modulated_t.shape[0]
    rows = features // n_own

    def column(g, p):
        return 2 * (g % n_z) + (p[0] ^ (g // n_z))

    def kernel(core_ref, mod_ref, attn_ref, outer_ref, bias_ref, mine_ref, other_ref):
        g = pl.program_id(0)

        def run(slots):
            left = jnp.dot(mod_ref[...], outer_ref[...], preferred_element_type=jnp.float32)
            right = jnp.dot(attn_ref[...], outer_ref[...], preferred_element_type=jnp.float32)
            lane = lax.broadcasted_iota(jnp.int32, left.shape, 1)
            both = jnp.where(lane < n_qkv, left, right).astype(jnp.bfloat16)
            slots[0, :, :rows] = both.reshape(n_own, rows, width)
            slots[0, :, rows:] = bias_ref[...]

        @pl.when(g < n_z)
        def _():
            run(mine_ref)

        @pl.when(g >= n_z)
        def _():
            run(other_ref)

    whole = lambda g, p: (0, 0)
    block = (1, n_own, rows + bias_rows, width)
    shape = jax.ShapeDtypeStruct((n_z,) + block[1:], jnp.bfloat16)
    return pl.pallas_call(
        kernel,
        grid_spec=pltpu.PrefetchScalarGridSpec(
            num_scalar_prefetch=1,
            grid=(n_dp,),
            in_specs=[
                pl.BlockSpec((features, tokens), whole),
                pl.BlockSpec((features, tokens), whole),
                pl.BlockSpec((None, tokens, width), lambda g, p: (column(g, p), 0, 0)),
                pl.BlockSpec((None, n_own, bias_rows, width), lambda g, p: (column(g, p), 0, 0, 0)),
            ],
            out_specs=[
                pl.BlockSpec(block, lambda g, p: (jnp.minimum(g, n_z - 1), 0, 0, 0)),
                pl.BlockSpec(block, lambda g, p: (jnp.maximum(g - n_z, 0), 0, 0, 0)),
            ],
        ),
        out_shape=[shape, shape],
        compiler_params=pltpu.CompilerParams(vmem_limit_bytes=40 << 20),
    )(core.reshape(1), modulated_t, attn_t, outer, bias_slots)


def block_pass(tokens_in, modulation, cotangent, w_qkv, w_proj, fc_parts, fc_shape, bias_full):
    latents, length, features = tokens_in.shape
    core = lax.axis_index("dp") % 2
    n_dp, n_own = lax.axis_size("dp"), lax.axis_size("own")
    steps = len(own_bits(n_own))
    hidden_units = n_dp * fc_shape[2]
    head_count = HEADS
    head_size = features // head_count
    score_scale = 1.0 / math.sqrt(head_size)
    row_count = latents * length
    b_query = bias_full[:features]
    b_value = bias_full[features : 2 * features]
    b_proj = bias_full[2 * features : 3 * features]
    b_fc1 = bias_full[3 * features : 3 * features + hidden_units]
    b_fc2 = bias_full[3 * features + hidden_units : 4 * features + hidden_units]
    pieces = [
        modulation[:, index * features : (index + 1) * features][:, None, :] for index in range(6)
    ]
    shift_one, scale_one, gate_one, shift_two, scale_two, gate_two = pieces
    residual = tokens_in.astype(jnp.float32)
    normed_one, inv_one = layer_stats(residual)
    modulated_one = (normed_one * (1.0 + scale_one) + shift_one).astype(jnp.bfloat16)
    qkv_proj = jnp.dot(
        modulated_one.reshape(row_count, features), w_qkv, preferred_element_type=jnp.float32
    )
    for index in range(steps - 2):
        fc_parts = share_merge(fc_parts, share_send(fc_parts, n_own, index), n_own, index)
    came = share_send(fc_parts, n_own, steps - 2)
    qkv_proj, came = after(qkv_proj, came)
    fc_parts = share_merge(fc_parts, came, n_own, steps - 2)
    qkv_proj = qkv_proj.reshape(latents, length, 3 * features)
    came = share_send(fc_parts, n_own, steps - 1)
    head_shape = (latents, length, head_count, head_size)
    query_flat = (qkv_proj[..., :features] + b_query).astype(jnp.bfloat16)
    key_flat = qkv_proj[..., features : 2 * features].astype(jnp.bfloat16)
    value_flat = (qkv_proj[..., 2 * features :] + b_value).astype(jnp.bfloat16)
    query_heads, key_heads, value_heads = (
        part.reshape(head_shape) for part in (query_flat, key_flat, value_flat)
    )
    scores = batched("bqhd,bkhd->bhqk", query_heads, key_heads) * score_scale
    row_max = jnp.max(scores, axis=-1, keepdims=True)
    log_total = row_max + jnp.log(jnp.sum(jnp.exp(scores - row_max), axis=-1, keepdims=True))
    attn_probs = jnp.exp(scores - log_total).astype(jnp.bfloat16)
    attn_out = (
        batched("bhqk,bkhd->bqhd", attn_probs, value_heads)
        .astype(jnp.bfloat16)
        .reshape(row_count, features)
    )
    attn_out, came = after(attn_out, came)
    fc_parts = share_merge(fc_parts, came, n_own, steps - 1)
    fc_mine, fc_other = share_core(fc_parts, n_dp, n_own, fc_shape)
    branch_one = (jnp.dot(attn_out, w_proj, preferred_element_type=jnp.float32) + b_proj).reshape(
        latents, length, features
    )
    middle = residual + gate_one * branch_one
    normed_two, inv_two = layer_stats(middle)
    modulated_two = (
        (normed_two * (1.0 + scale_two) + shift_two)
        .astype(jnp.bfloat16)
        .reshape(row_count, features)
    )
    fc1_pre, branch_two = mlp_forward(core, modulated_two, fc_mine, fc_other, b_fc1)
    branch_two = (branch_two + b_fc2).reshape(latents, length, features)
    block_out = middle + gate_two * branch_two
    cot_float = cotangent.astype(jnp.float32)
    d_gate_two = jnp.sum(cot_float * branch_two, axis=1)
    d_branch_two = cot_float * gate_two
    dbranch_low = d_branch_two.astype(jnp.bfloat16).reshape(row_count, features)
    gb_fc2 = jnp.sum(d_branch_two, axis=(0, 1))
    fc_terms, fc_others, d_mod_two, gb_fc1 = mlp_backward(
        core, modulated_two.T, dbranch_low, dbranch_low.T, fc1_pre, fc_mine, fc_other
    )
    d_mod_two = d_mod_two.reshape(latents, length, features)
    fc_terms, fc_came = reduce_core(fc_terms, fc_others, n_dp, n_own)
    d_shift_two = jnp.sum(d_mod_two, axis=1)
    d_scale_two = jnp.sum(d_mod_two * normed_two, axis=1)
    d_middle = cot_float + norm_back(d_mod_two * (1.0 + scale_two), normed_two, inv_two)
    d_gate_one = jnp.sum(d_middle * branch_one, axis=1)
    d_branch_one = d_middle * gate_one
    dbranch_one_low = d_branch_one.astype(jnp.bfloat16).reshape(row_count, features)
    gb_proj = jnp.sum(d_branch_one, axis=(0, 1))
    d_attn = jnp.dot(dbranch_one_low, w_proj.T, preferred_element_type=jnp.float32).astype(
        jnp.bfloat16
    )
    d_attn, fc_came = after(d_attn, fc_came)
    fc_parts = reduce_halves(fc_terms, fc_came, n_dp, n_own)
    for index in range(steps - 1):
        fc_parts = reduce_own(fc_parts, n_own, index)
    flat_shape = (latents, length, features)
    d_query, d_key, d_value, gb_query, gb_value = attention_backward(
        query_flat.reshape(row_count, features),
        key_flat.reshape(row_count, features),
        value_flat.reshape(row_count, features),
        d_attn,
        length,
        head_size,
    )
    gb_query, gb_value = gb_query.reshape(-1), gb_value.reshape(-1)
    dqkv_low = jnp.concatenate([d_query, d_key, d_value], axis=1)
    dqkv_low, fc_parts = after(dqkv_low, fc_parts)
    fc_parts = reduce_own(fc_parts, n_own, steps - 1)
    outer = jnp.concatenate(
        [
            dqkv_low.reshape(row_count, n_dp, 3 * features // n_dp),
            dbranch_one_low.reshape(row_count, n_dp, features // n_dp),
        ],
        axis=2,
    ).transpose(1, 0, 2)
    d_mod_one = jnp.dot(dqkv_low, w_qkv.T, preferred_element_type=jnp.float32).reshape(flat_shape)
    d_mod_one, fc_parts = after(d_mod_one, fc_parts)
    d_shift_one = jnp.sum(d_mod_one, axis=1)
    d_scale_one = jnp.sum(d_mod_one * normed_one, axis=1)
    grad_in = d_middle + norm_back(d_mod_one * (1.0 + scale_one), normed_one, inv_one)
    d_modulation = jnp.concatenate(
        [d_shift_one, d_scale_one, d_gate_one, d_shift_two, d_scale_two, d_gate_two], axis=-1
    )
    gb_ada = jnp.sum(d_modulation, axis=0)
    grad_bias = jnp.concatenate([gb_query, gb_value, gb_proj, gb_fc1, gb_fc2, gb_ada])
    width = outer.shape[2]
    bias_count = grad_bias.shape[0] // (n_dp * n_own)
    bias_rows = -(-bias_count // (16 * width)) * 16
    bias_slots = grad_bias.reshape(n_dp, n_own, bias_count).astype(jnp.bfloat16)
    bias_slots = jnp.pad(bias_slots, ((0, 0), (0, 0), (0, bias_rows * width - bias_count)))
    attn_terms, attn_others = attn_gradients(
        core,
        modulated_one.reshape(row_count, features).T,
        attn_out.T,
        outer,
        bias_slots.reshape(n_dp, n_own, bias_rows, width),
        3 * features // n_dp,
    )
    attn_came = reduce_core(attn_terms, attn_others, n_dp, n_own)[1]
    (fc_parts, d_modulation), attn_came = after((fc_parts, d_modulation), attn_came)
    attn_parts = reduce_halves(attn_terms, attn_came, n_dp, n_own)
    fc_sums = reduce_z(fc_parts, n_dp)
    return block_out, grad_in, d_modulation, attn_parts, fc_sums


def per_device(
    tokens_in,
    condition,
    cotangent,
    w_qkv,
    w_proj,
    w_fc1,
    w_fc2,
    w_ada,
    mom_qkv,
    mom_proj,
    mom_fc1,
    mom_fc2,
    mom_ada,
    biases,
    bias_mom,
):
    low = jnp.bfloat16
    n_dp, n_own = lax.axis_size("dp"), lax.axis_size("own")
    dp_place, own_place = lax.axis_index("dp"), lax.axis_index("own")
    latents, features = condition.shape
    rows = w_qkv.shape[0]
    n_qkv, n_proj, n_fc1, n_fc2, n_ada = (
        w_qkv.shape[1],
        w_proj.shape[1],
        w_fc1.shape[1],
        w_fc2.shape[0],
        w_ada.shape[1],
    )
    cond_act = jax.nn.silu(condition).astype(low)
    small = jnp.concatenate([cond_act.reshape(-1), biases.astype(low)])
    small_own = gather_dp(small, n_dp)
    cond_own = small_own[:, : latents * features].reshape(n_dp * latents, features)
    w_ada_rows = gather_own(w_ada.astype(low), n_own).reshape(features, n_ada)
    mod_mine = jnp.dot(cond_own, w_ada_rows, preferred_element_type=jnp.float32)
    mod_parts = swap_dp(mod_mine.reshape(n_dp, latents, n_ada))
    small_all = gather_own(small_own, n_own)
    bias_full = (
        small_all[:, :, latents * features :].transpose(1, 0, 2).reshape(-1).astype(jnp.float32)
    )
    core = dp_place % 2
    first = jnp.concatenate([w_qkv, w_proj], axis=1).astype(low)
    second = jnp.stack([w_fc1, w_fc2.T]).astype(low)
    steps = len(own_bits(n_own))
    first_parts = share_z(first, n_dp)
    second, mod_parts = after(second, mod_parts)
    fc_parts = share_z(second, n_dp)
    for index in range(steps):
        came = share_send(first_parts, n_own, index)
        if index == 0:
            mod_parts, came = after(mod_parts, came)
        first_parts = share_merge(first_parts, came, n_own, index)
    fc_parts, first_parts = after(fc_parts, first_parts)
    first_mine, first_other = share_core(first_parts, n_dp, n_own, first.shape)
    first_all = jnp.where(
        core == 0,
        jnp.stack([first_mine, first_other], axis=1),
        jnp.stack([first_other, first_mine], axis=1),
    ).reshape(n_dp, features, n_qkv + n_proj)
    modulation = mod_parts.transpose(1, 0, 2).reshape(latents, n_dp * n_ada)
    modulation = modulation + bias_full[bias_full.shape[0] - n_dp * n_ada :]
    block_out, grad_in, d_modulation, attn_parts, fc_sums = block_pass(
        tokens_in,
        modulation,
        cotangent,
        columns_of(first_all, 0, n_qkv),
        columns_of(first_all, n_qkv, n_proj),
        fc_parts,
        second.shape,
        bias_full,
    )
    for index in range(steps):
        attn_parts = reduce_own(attn_parts, n_own, index)
    fc_sums, attn_parts = after(fc_sums, attn_parts)
    fc_tile = add_arrived(*fc_sums)
    attn_tile = add_arrived(*reduce_z(attn_parts, n_dp))
    bias_count = biases.shape[0]
    bias_tile = attn_tile[rows:].reshape(-1)[:bias_count]
    dmod_low = d_modulation.astype(low)
    dmod_own = swap_dp(dmod_low.reshape(latents, n_dp, n_ada).transpose(1, 0, 2))
    dmod_own = dmod_own.reshape(n_dp * latents, n_ada)
    cond_terms = jnp.dot(dmod_own, w_ada_rows.T, preferred_element_type=jnp.float32)
    cond_parts = swap_dp(cond_terms.reshape(n_dp, latents, features))
    dmod_all = gather_own(dmod_own, n_own).reshape(n_own * n_dp * latents, n_ada)
    cond_all = small_all[:, :, : latents * features].reshape(n_own * n_dp * latents, features)
    cond_cols = lax.dynamic_slice_in_dim(cond_all, own_place * rows, rows, 1)
    g_ada = jnp.dot(cond_cols.T, dmod_all, preferred_element_type=jnp.float32)
    tiles = (
        attn_tile[:rows, :n_qkv],
        attn_tile[:rows, n_qkv:],
        fc_tile[0],
        fc_tile[1],
        g_ada,
    )
    weights = (w_qkv, w_proj, w_fc1, w_fc2.T, w_ada)
    moments = (mom_qkv, mom_proj, mom_fc1, mom_fc2.T, mom_ada)
    fresh = [momentum_rate * moments[index] + tiles[index] for index in range(5)]
    widths = [n_qkv, n_proj, n_fc1, n_fc2, n_ada]
    fc_rows = jnp.concatenate([fresh[2], fresh[3]], axis=1).astype(low)
    rest_rows = jnp.concatenate([fresh[0], fresh[1], fresh[4]], axis=1).astype(low)
    fc_all = gather_own(fc_rows, n_own).reshape(features, n_fc1 + n_fc2)
    rest_all = gather_own(rest_rows, n_own).reshape(features, n_qkv + n_proj + n_ada)
    low_rows = [
        rest_rows[:, :n_qkv],
        rest_rows[:, n_qkv : n_qkv + n_proj],
        fc_rows[:, :n_fc1],
        fc_rows[:, n_fc1:],
        rest_rows[:, n_qkv + n_proj :],
    ]
    low_all = [
        rest_all[:, :n_qkv],
        rest_all[:, n_qkv : n_qkv + n_proj],
        fc_all[:, :n_fc1],
        fc_all[:, n_fc1:],
        rest_all[:, n_qkv + n_proj :],
    ]
    gram_terms = [
        jnp.dot(low_rows[index], low_all[index].T, preferred_element_type=jnp.float32)
        for index in range(5)
    ]
    fc_gram = gram_to_owner(gram_terms[2:4], GRAM_SLOTS[2:4], n_dp)
    rest_slots = GRAM_SLOTS[:2] + GRAM_SLOTS[4:]
    rest_gram = gram_to_owner(gram_terms[:2] + gram_terms[4:], rest_slots, n_dp)
    fc_owner = jnp.logical_or(dp_place == GRAM_SLOTS[2], dp_place == GRAM_SLOTS[3])
    gram_rows = jnp.where(fc_owner, fc_gram, rest_gram)
    gram_rows, cond_parts = after(gram_rows, cond_parts)
    gram = gather_own(gram_rows, n_own).reshape(features, features)
    sigmoid_c = jax.nn.sigmoid(condition)
    grad_cond = jnp.sum(cond_parts, axis=0) * (sigmoid_c * (1.0 + condition * (1.0 - sigmoid_c)))
    unit = jnp.eye(features, dtype=jnp.float32)
    magnitude = jnp.sqrt(jnp.sum(gram * unit))
    divisor = magnitude + 1e-07
    gram = gram / (divisor * divisor)
    my_rows, by_column = newton_schulz(gram, own_place, rows)
    middle = jnp.sum(by_column) / features
    my_unit = lax.dynamic_slice_in_dim(unit, own_place * rows, rows, 0)
    my_rows = ((my_rows - middle * my_unit) / divisor).astype(low)
    scalars = jnp.stack([middle / divisor, magnitude])
    high_part = scalars.astype(low)
    low_part = (scalars - high_part.astype(jnp.float32)).astype(low)
    extra = jnp.pad(jnp.stack([high_part, low_part]), ((0, 14), (0, features - 2)))
    factors = spread_from_owners(jnp.concatenate([my_rows, extra]), n_dp)
    numbers = [
        factor[rows, :2].astype(jnp.float32) + factor[rows + 1, :2].astype(jnp.float32)
        for factor in factors
    ]
    ortho = [
        numbers[index][0] * fresh[index]
        + jnp.dot(factors[index][:rows], low_all[index], preferred_element_type=jnp.float32)
        for index in range(5)
    ]
    position = lax.iota(jnp.int32, 5)
    moment_norms = sum(jnp.where(position == index, numbers[index][1], 0.0) for index in range(5))
    sides = (n_qkv * n_dp, n_proj * n_dp, n_fc1 * n_dp, n_fc2 * n_dp, n_ada * n_dp)
    updated = [
        weights[index]
        - learn_rate * 0.2 * math.sqrt(max(features, sides[index])) * ortho[index]
        for index in range(5)
    ]
    moment_bias = momentum_rate * bias_mom + bias_tile
    new_bias = biases - bias_rate * moment_bias
    return (
        block_out,
        grad_in,
        grad_cond,
        tiles[0],
        tiles[1],
        tiles[2],
        tiles[3].T,
        tiles[4],
        bias_tile,
        updated[0],
        updated[1],
        updated[2],
        updated[3].T,
        updated[4],
        fresh[0],
        fresh[1],
        fresh[2],
        fresh[3].T,
        fresh[4],
        new_bias,
        moment_bias,
        moment_norms,
    )


def solution(mesh):
    placed = (
        P(("dp", "own"), None, None),
        P(("dp", "own"), None),
        P(("dp", "own"), None, None),
        P("own", "dp"),
        P("own", "dp"),
        P("own", "dp"),
        P("dp", "own"),
        P("own", "dp"),
        P("own", "dp"),
        P("own", "dp"),
        P("own", "dp"),
        P("dp", "own"),
        P("own", "dp"),
        P(("dp", "own")),
        P(("dp", "own")),
    )
    return jax.shard_map(
        per_device,
        mesh=mesh,
        in_specs=placed,
        out_specs=(
            P(("dp", "own"), None, None),
            P(("dp", "own"), None, None),
            P(("dp", "own"), None),
            P("own", "dp"),
            P("own", "dp"),
            P("own", "dp"),
            P("dp", "own"),
            P("own", "dp"),
            P(("dp", "own")),
            P("own", "dp"),
            P("own", "dp"),
            P("own", "dp"),
            P("dp", "own"),
            P("own", "dp"),
            P("own", "dp"),
            P("own", "dp"),
            P("own", "dp"),
            P("dp", "own"),
            P("own", "dp"),
            P(("dp", "own")),
            P(("dp", "own")),
            P(),
        ),
        check_vma=False,
    )
```

```python
import math

import jax
import jax.numpy as jnp
from jax import lax
from jax.experimental import pallas as pl
from jax.experimental.pallas import tpu as pltpu
from jax.sharding import PartitionSpec as P

HEADS = 12
NS_ITERS = 5


momentum_rate = 0.9
learn_rate = 0.15
bias_rate = 0.002
coef_first = 3.4445
coef_second = -4.775
coef_third = 2.0315
gelu_scale = math.sqrt(2.0 / math.pi)
norm_epsilon = 1e-06


def gather_own(piece, count):
    place = lax.axis_index("own")
    whole = jnp.zeros((count,) + piece.shape, piece.dtype)
    whole = lax.dynamic_update_index_in_dim(whole, piece, place, 0)
    for step in range(1, count):
        pairs = [(index, index ^ step) for index in range(count)]
        other = lax.ppermute(piece, "own", pairs)
        whole = lax.dynamic_update_index_in_dim(whole, other, place ^ step, 0)
    return whole


def gather_dp(piece, count):
    return swap_dp(jnp.broadcast_to(piece, (count,) + piece.shape))


def after(value, other):
    return lax.optimization_barrier((value, other))


def own_bits(count):
    return [1 << index for index in range(count.bit_length() - 1)]


def share_z(tile, n_dp):
    n_z = n_dp // 2
    place = lax.axis_index("dp") // 2
    whole = jnp.zeros((n_z,) + tile.shape, tile.dtype)
    whole = lax.dynamic_update_index_in_dim(whole, tile, place, 0)
    for step in range(1, n_z):
        pairs = [(index, index ^ (2 * step)) for index in range(n_dp)]
        whole = lax.dynamic_update_index_in_dim(
            whole, lax.ppermute(tile, "dp", pairs), place ^ step, 0
        )
    return (whole[: n_z // 2], whole[n_z // 2 :])


def orders(n_own):
    bits = own_bits(n_own)
    return (bits, bits[::-1])


def share_send(parts, n_own, index):
    result = []
    for part, order in zip(parts, orders(n_own)):
        pairs = [(place, place ^ order[index]) for place in range(n_own)]
        result.append(lax.ppermute(part, "own", pairs))
    return tuple(result)


def share_merge(parts, arrived, n_own, index):
    me = lax.axis_index("own")
    result = []
    for part, came, order in zip(parts, arrived, orders(n_own)):
        bit = order[index]
        axis = 1 + len([other for other in order[:index] if other > bit])
        upper = (me & bit) != 0
        result.append(
            jnp.where(upper, jnp.stack([came, part], axis), jnp.stack([part, came], axis))
        )
    return tuple(result)


def share_core(parts, n_dp, n_own, shape):
    mine = jnp.concatenate([part.reshape((part.shape[0], n_own) + shape) for part in parts])
    other = lax.ppermute(mine, "dp", [(index, index ^ 1) for index in range(n_dp)])
    return mine, other


def add_low(left, right):
    total = left.astype(jnp.float32) + right.astype(jnp.float32)
    return total.astype(jnp.bfloat16)


def reduce_core(mine, other, n_dp, n_own):
    came = lax.ppermute(other, "dp", [(index, index ^ 1) for index in range(n_dp)])
    return mine, came


def reduce_halves(mine, came, n_dp, n_own):
    n_z = n_dp // 2
    summed = add_low(mine, came)
    inner = (n_z // 2,) + (2,) * len(own_bits(n_own)) + mine.shape[2:]
    return (summed[: n_z // 2].reshape(inner), summed[n_z // 2 :].reshape(inner))


def reduce_own(parts, n_own, index):
    me = lax.axis_index("own")
    result = []
    for part, order in zip(parts, orders(n_own)):
        bit = order[index]
        left = sorted(order[index:], reverse=True)
        axis = 1 + left.index(bit)
        side = jnp.where((me & bit) != 0, 1, 0)
        keep = lax.dynamic_index_in_dim(part, side, axis, keepdims=False)
        send = lax.dynamic_index_in_dim(part, 1 - side, axis, keepdims=False)
        pairs = [(place, place ^ bit) for place in range(n_own)]
        result.append(add_low(keep, lax.ppermute(send, "own", pairs)))
    return tuple(result)


def reduce_z(parts, n_dp):
    n_z = n_dp // 2
    place = lax.axis_index("dp") // 2
    summed = jnp.concatenate(parts)
    total = lax.dynamic_index_in_dim(summed, place, 0, keepdims=False)
    arrived = []
    for step in range(1, n_z):
        pairs = [(index, index ^ (2 * step)) for index in range(n_dp)]
        send = lax.dynamic_index_in_dim(summed, place ^ step, 0, keepdims=False)
        arrived.append(lax.ppermute(send, "dp", pairs))
    return total, tuple(arrived)


def add_arrived(total, arrived):
    total = total.astype(jnp.float32)
    for came in arrived:
        total = total + came.astype(jnp.float32)
    return total


GRAM_SLOTS = (2, 4, 3, 0, 5)


def gram_to_owner(terms, slots, n_dp):
    n_z = n_dp // 2
    core, place = lax.axis_index("dp") % 2, lax.axis_index("dp") // 2
    sides = []
    for side in range(2):
        mine = [term for term, slot in zip(terms, slots) if slot % 2 == side]
        if not mine:
            continue
        group = jnp.stack(mine)
        pairs = [(2 * z + 1 - side, 2 * z + side) for z in range(n_z)]
        sides.append((side, group + lax.ppermute(group, "dp", pairs)))

    def term_for(z_index):
        value = None
        for side, group in sides:
            inside = [slot // 2 for slot in slots if slot % 2 == side]
            for index, at in enumerate(inside):
                hit = jnp.logical_and(core == side, z_index == at)
                value = group[index] if value is None else jnp.where(hit, group[index], value)
        return value

    total = term_for(place)
    for step in range(1, n_z):
        pairs = [(slot ^ (2 * step), slot) for slot in slots]
        total = total + lax.ppermute(term_for(place ^ step), "dp", pairs)
    return total


def spread_from_owners(piece, n_dp):
    n_z = n_dp // 2
    core, place = lax.axis_index("dp") % 2, lax.axis_index("dp") // 2
    came = [piece]
    for step in range(1, n_z):
        pairs = [(slot, slot ^ (2 * step)) for slot in GRAM_SLOTS]
        came.append(lax.ppermute(piece, "dp", pairs))
    sides = [[slot for slot in GRAM_SLOTS if slot % 2 == side] for side in range(2)]
    have = []
    for index in range(max(len(side) for side in sides)):
        at = [side[min(index, len(side) - 1)] // 2 for side in sides]
        distance = place ^ jnp.where(core == 0, at[0], at[1])
        value = came[0]
        for step in range(1, n_z):
            value = jnp.where(distance == step, came[step], value)
        have.append(value)
    have = jnp.stack(have)
    other = lax.ppermute(have, "dp", [(index, index ^ 1) for index in range(n_dp)])
    result = []
    for slot in GRAM_SLOTS:
        index = sides[slot % 2].index(slot)
        result.append(jnp.where(core == slot % 2, have[index], other[index]))
    return result


def split_two(value):
    high = value.astype(jnp.bfloat16)
    return high, (value - high.astype(jnp.float32)).astype(jnp.bfloat16)


def chain_kernel(place_ref, gram_ref, rows_ref, middle_ref, a_hi, a_lo, p_hi, p_lo, t_hi, t_lo, r_hi, r_lo):
    side = gram_ref.shape[0]
    rows = rows_ref.shape[0]
    block = 256

    def product(left_hi, left_lo, right_hi, right_lo, rows_at, columns_at):
        high = left_hi[rows_at, :]
        dot = lambda x, y: jnp.dot(x, y, preferred_element_type=jnp.float32)
        return (
            dot(high, right_hi[:, columns_at])
            + dot(high, right_lo[:, columns_at])
            + dot(left_lo[rows_at, :], right_hi[:, columns_at])
        )

    def put(high_ref, low_ref, start, value):
        high, low = split_two(value)
        high_ref[pl.ds(start, block), start:] = high
        low_ref[pl.ds(start, block), start:] = low
        for column in range(start + block, side, block):
            inside = slice(column - start, column - start + block)
            high_ref[pl.ds(column, block), start : start + block] = high[:, inside].T
            low_ref[pl.ds(column, block), start : start + block] = low[:, inside].T

    def each(run):
        for start in range(0, side, block):
            run(start)

    def upper(left_hi, left_lo, right_hi, right_lo, start):
        return product(
            left_hi, left_lo, right_hi, right_lo, pl.ds(start, block), slice(start, side)
        )

    def polynomial(start):
        square = upper(a_hi, a_lo, a_hi, a_lo, start)
        here = pl.ds(start, block)
        gram = a_hi[here, start:].astype(jnp.float32) + a_lo[here, start:].astype(jnp.float32)
        row = lax.broadcasted_iota(jnp.int32, (block, side - start), 0)
        column = lax.broadcasted_iota(jnp.int32, (block, side - start), 1)
        unit = jnp.where(row == column, coef_first, 0.0)
        put(p_hi, p_lo, start, unit + coef_second * gram + coef_third * square)

    def times(start):
        put(r_hi, r_lo, start, upper(a_hi, a_lo, p_hi, p_lo, start))

    def again(start):
        put(a_hi, a_lo, start, upper(r_hi, r_lo, p_hi, p_lo, start))

    def collect(start):
        put(r_hi, r_lo, start, upper(t_hi, t_lo, p_hi, p_lo, start))

    def store(start):
        here = pl.ds(start, block)
        t_hi[here, :] = r_hi[here, :]
        t_lo[here, :] = r_lo[here, :]

    def store_first(start):
        here = pl.ds(start, block)
        t_hi[here, :] = p_hi[here, :]
        t_lo[here, :] = p_lo[here, :]

    each(lambda start: put(a_hi, a_lo, start, gram_ref[pl.ds(start, block), start:]))
    each(polynomial)
    each(store_first)
    each(times)
    each(again)

    def step(index, carry):
        each(polynomial)
        each(collect)
        each(store)
        each(times)
        each(again)
        return carry

    lax.fori_loop(0, NS_ITERS - 2, step, 0)
    each(polynomial)
    middle_ref[...] = jnp.zeros_like(middle_ref)

    def trace(start):
        here = pl.ds(start, block)
        left = t_hi[here, :].astype(jnp.float32) + t_lo[here, :].astype(jnp.float32)
        right = p_hi[here, :].astype(jnp.float32) + p_lo[here, :].astype(jnp.float32)
        middle_ref[...] += jnp.sum(left * right, axis=0, keepdims=True)

    each(trace)
    first = pl.multiple_of(place_ref[0] * rows, rows)
    rows_ref[...] = product(t_hi, t_lo, p_hi, p_lo, pl.ds(first, rows), slice(0, side))


def newton_schulz(gram, place, rows):
    side = gram.shape[0]
    return pl.pallas_call(
        chain_kernel,
        grid_spec=pltpu.PrefetchScalarGridSpec(
            num_scalar_prefetch=1,
            grid=(1,),
            in_specs=[pl.BlockSpec((side, side), lambda g, p: (0, 0))],
            out_specs=[
                pl.BlockSpec((rows, side), lambda g, p: (0, 0)),
                pl.BlockSpec((1, side), lambda g, p: (0, 0)),
            ],
            scratch_shapes=[pltpu.VMEM((side, side), jnp.bfloat16)] * 8,
        ),
        out_shape=[
            jax.ShapeDtypeStruct((rows, side), jnp.float32),
            jax.ShapeDtypeStruct((1, side), jnp.float32),
        ],
        compiler_params=pltpu.CompilerParams(vmem_limit_bytes=40 << 20),
    )(place.reshape(1), gram)


def two_cores(n_z):
    mine = lambda g, p: (jnp.minimum(g, n_z - 1), 0, 0, 0, 0)
    other = lambda g, p: (jnp.maximum(g - n_z, 0), 0, 0, 0, 0)
    column = lambda g, p: (0, 2 * (g % n_z) + (p[0] ^ (g // n_z)))
    return mine, other, column


def mlp_forward(core, modulated, mine, other, bias):
    n_z, n_own, _, rows, width = mine.shape
    tokens, features = modulated.shape
    at_mine, at_other, at_column = two_cores(n_z)

    def kernel(core_ref, mod_ref, mine_ref, other_ref, bias_ref, pre_ref, out_ref):
        g = pl.program_id(0)

        @pl.when(g == 0)
        def _():
            out_ref[...] = jnp.zeros_like(out_ref)

        def run(weights):
            first = weights[0, :, 0].reshape(features, width)
            second = weights[0, :, 1].reshape(features, width)
            pre = jnp.dot(mod_ref[...], first, preferred_element_type=jnp.float32) + bias_ref[...]
            pre_ref[...] = pre
            act = gelu_value(pre).astype(jnp.bfloat16)
            out_ref[...] += lax.dot_general(
                act, second, (((1,), (1,)), ((), ())), preferred_element_type=jnp.float32
            )

        @pl.when(g < n_z)
        def _():
            run(mine_ref)

        @pl.when(g >= n_z)
        def _():
            run(other_ref)

    block = (1, n_own, 2, rows, width)
    return pl.pallas_call(
        kernel,
        grid_spec=pltpu.PrefetchScalarGridSpec(
            num_scalar_prefetch=1,
            grid=(2 * n_z,),
            in_specs=[
                pl.BlockSpec((tokens, features), lambda g, p: (0, 0)),
                pl.BlockSpec(block, at_mine),
                pl.BlockSpec(block, at_other),
                pl.BlockSpec((None, 1, width), lambda g, p: (at_column(g, p)[1], 0, 0)),
            ],
            out_specs=[
                pl.BlockSpec((None, tokens, width), lambda g, p: (at_column(g, p)[1], 0, 0)),
                pl.BlockSpec((tokens, features), lambda g, p: (0, 0)),
            ],
        ),
        out_shape=[
            jax.ShapeDtypeStruct((2 * n_z, tokens, width), jnp.float32),
            jax.ShapeDtypeStruct((tokens, features), jnp.float32),
        ],
        compiler_params=pltpu.CompilerParams(vmem_limit_bytes=48 << 20),
    )(core.reshape(1), modulated, mine, other, bias.reshape(2 * n_z, 1, width))


def mlp_backward(core, modulated_t, branch_low, branch_t, pre, mine, other):
    n_z, n_own, _, rows, width = mine.shape
    features, tokens = modulated_t.shape
    at_mine, at_other, at_column = two_cores(n_z)

    def kernel(
        core_ref, mod_ref, low_ref, lowt_ref, pre_ref, mine_ref, other_ref,
        gmine_ref, gother_ref, dmod_ref, gb_ref,
    ):
        g = pl.program_id(0)

        @pl.when(g == 0)
        def _():
            dmod_ref[...] = jnp.zeros_like(dmod_ref)

        def run(weights, grads):
            first = weights[0, :, 0].reshape(features, width)
            second = weights[0, :, 1].reshape(features, width)
            inner = pre_ref[...]
            act = gelu_value(inner).astype(jnp.bfloat16)
            d_act = jnp.dot(low_ref[...], second, preferred_element_type=jnp.float32)
            d_pre = d_act * gelu_slope(inner)
            gb_ref[...] = jnp.sum(d_pre, axis=0, keepdims=True)
            dpre_low = d_pre.astype(jnp.bfloat16)
            g_first = jnp.dot(mod_ref[...], dpre_low, preferred_element_type=jnp.float32)
            g_second = jnp.dot(lowt_ref[...], act, preferred_element_type=jnp.float32)
            grads[0, :, 0] = g_first.astype(jnp.bfloat16).reshape(n_own, rows, width)
            grads[0, :, 1] = g_second.astype(jnp.bfloat16).reshape(n_own, rows, width)
            dmod_ref[...] += lax.dot_general(
                dpre_low, first, (((1,), (1,)), ((), ())), preferred_element_type=jnp.float32
            )

        @pl.when(g < n_z)
        def _():
            run(mine_ref, gmine_ref)

        @pl.when(g >= n_z)
        def _():
            run(other_ref, gother_ref)

    block = (1, n_own, 2, rows, width)
    whole = lambda g, p: (0, 0)
    low = jnp.bfloat16
    grads, others, d_mod, gb = pl.pallas_call(
        kernel,
        grid_spec=pltpu.PrefetchScalarGridSpec(
            num_scalar_prefetch=1,
            grid=(2 * n_z,),
            in_specs=[
                pl.BlockSpec((features, tokens), whole),
                pl.BlockSpec((tokens, features), whole),
                pl.BlockSpec((features, tokens), whole),
                pl.BlockSpec((None, tokens, width), lambda g, p: (at_column(g, p)[1], 0, 0)),
                pl.BlockSpec(block, at_mine),
                pl.BlockSpec(block, at_other),
            ],
            out_specs=[
                pl.BlockSpec(block, at_mine),
                pl.BlockSpec(block, at_other),
                pl.BlockSpec((tokens, features), whole),
                pl.BlockSpec((None, 1, width), lambda g, p: (at_column(g, p)[1], 0, 0)),
            ],
        ),
        out_shape=[
            jax.ShapeDtypeStruct(mine.shape, low),
            jax.ShapeDtypeStruct(mine.shape, low),
            jax.ShapeDtypeStruct((tokens, features), jnp.float32),
            jax.ShapeDtypeStruct((2 * n_z, 1, width), jnp.float32),
        ],
        compiler_params=pltpu.CompilerParams(vmem_limit_bytes=56 << 20),
    )(core.reshape(1), modulated_t, branch_low, branch_t, pre, mine, other)
    return grads, others, d_mod, gb.reshape(-1)


def swap_dp(blocks):
    return lax.all_to_all(blocks, "dp", split_axis=0, concat_axis=0, tiled=True)


def columns_of(blocks, start, width):
    count, rows, _ = blocks.shape
    part = blocks[:, :, start : start + width]
    return part.transpose(1, 0, 2).reshape(rows, count * width)


def batched(form, left, right):
    return jnp.einsum(form, left, right, preferred_element_type=jnp.float32)


def layer_stats(values):
    mean_value = jnp.mean(values, axis=-1, keepdims=True)
    centered = values - mean_value
    inv_std = lax.rsqrt(jnp.mean(centered * centered, axis=-1, keepdims=True) + norm_epsilon)
    return (centered * inv_std, inv_std)


def norm_back(grad_normed, normed, inv_std):
    first = jnp.mean(grad_normed, axis=-1, keepdims=True)
    second = jnp.mean(grad_normed * normed, axis=-1, keepdims=True)
    return inv_std * (grad_normed - first - normed * second)


def gelu_value(inner):
    return 0.5 * inner * (1.0 + jnp.tanh(gelu_scale * (inner + 0.044715 * inner * inner * inner)))


def gelu_slope(inner):
    tangent = jnp.tanh(gelu_scale * (inner + 0.044715 * inner * inner * inner))
    return 0.5 * (1.0 + tangent) + 0.5 * inner * (1.0 - tangent * tangent) * gelu_scale * (
        1.0 + 3.0 * 0.044715 * inner * inner
    )


def attention_backward(query, key, value, d_out, length, head_size):
    rows, features = query.shape
    lanes = 2 * head_size
    scale = 1.0 / math.sqrt(head_size)

    def kernel(q_ref, k_ref, v_ref, d_ref, dq_ref, dk_ref, dv_ref, gq_ref, gv_ref):
        lane = lax.broadcasted_iota(jnp.int32, (length, lanes), 1)
        q, k, v, d = q_ref[...], k_ref[...], v_ref[...], d_ref[...]
        nothing = jnp.zeros_like(q)
        across = (((1,), (1,)), ((), ()))
        pieces = []
        for head in range(2):
            mine = (lane // head_size) == head
            scores = lax.dot_general(
                jnp.where(mine, q, nothing), k, across, preferred_element_type=jnp.float32
            )
            scores = scores * scale
            top = jnp.max(scores, axis=1, keepdims=True)
            log_total = top + jnp.log(jnp.sum(jnp.exp(scores - top), axis=1, keepdims=True))
            probs = jnp.exp(scores - log_total)
            d_probs = lax.dot_general(
                jnp.where(mine, d, nothing), v, across, preferred_element_type=jnp.float32
            )
            delta = jnp.sum(probs * d_probs, axis=1, keepdims=True)
            d_scores = probs * (d_probs - delta) * scale
            low_scores = d_scores.astype(jnp.bfloat16)
            dot = lambda x, y: jnp.dot(x, y, preferred_element_type=jnp.float32)
            pieces.append(
                (
                    dot(low_scores, k),
                    dot(low_scores.T, q),
                    dot(probs.astype(jnp.bfloat16).T, d),
                )
            )
        first = lane < head_size
        dq, dk, dv = [jnp.where(first, *pair) for pair in zip(*pieces)]
        dq_ref[...] = dq.astype(jnp.bfloat16)
        dk_ref[...] = dk.astype(jnp.bfloat16)
        dv_ref[...] = dv.astype(jnp.bfloat16)

        @pl.when(pl.program_id(1) == 0)
        def _():
            gq_ref[...] = jnp.zeros_like(gq_ref)
            gv_ref[...] = jnp.zeros_like(gv_ref)

        gq_ref[...] += jnp.sum(dq, axis=0, keepdims=True)
        gv_ref[...] += jnp.sum(dv, axis=0, keepdims=True)

    block = pl.BlockSpec((length, lanes), lambda pair, latent: (latent, pair))
    total = pl.BlockSpec((1, lanes), lambda pair, latent: (0, pair))
    low = jax.ShapeDtypeStruct((rows, features), jnp.bfloat16)
    sums = jax.ShapeDtypeStruct((1, features), jnp.float32)
    return pl.pallas_call(
        kernel,
        grid=(features // lanes, rows // length),
        in_specs=[block] * 4,
        out_specs=[block] * 3 + [total] * 2,
        out_shape=[low] * 3 + [sums] * 2,
    )(query, key, value, d_out)


def attn_gradients(core, modulated_t, attn_t, outer, bias_slots, n_qkv):
    n_dp, tokens, width = outer.shape
    _, n_own, bias_rows, _ = bias_slots.shape
    n_z = n_dp // 2
    features = modulated_t.shape[0]
    rows = features // n_own

    def column(g, p):
        return 2 * (g % n_z) + (p[0] ^ (g // n_z))

    def kernel(core_ref, mod_ref, attn_ref, outer_ref, bias_ref, mine_ref, other_ref):
        g = pl.program_id(0)

        def run(slots):
            left = jnp.dot(mod_ref[...], outer_ref[...], preferred_element_type=jnp.float32)
            right = jnp.dot(attn_ref[...], outer_ref[...], preferred_element_type=jnp.float32)
            lane = lax.broadcasted_iota(jnp.int32, left.shape, 1)
            both = jnp.where(lane < n_qkv, left, right).astype(jnp.bfloat16)
            slots[0, :, :rows] = both.reshape(n_own, rows, width)
            slots[0, :, rows:] = bias_ref[...]

        @pl.when(g < n_z)
        def _():
            run(mine_ref)

        @pl.when(g >= n_z)
        def _():
            run(other_ref)

    whole = lambda g, p: (0, 0)
    block = (1, n_own, rows + bias_rows, width)
    shape = jax.ShapeDtypeStruct((n_z,) + block[1:], jnp.bfloat16)
    return pl.pallas_call(
        kernel,
        grid_spec=pltpu.PrefetchScalarGridSpec(
            num_scalar_prefetch=1,
            grid=(n_dp,),
            in_specs=[
                pl.BlockSpec((features, tokens), whole),
                pl.BlockSpec((features, tokens), whole),
                pl.BlockSpec((None, tokens, width), lambda g, p: (column(g, p), 0, 0)),
                pl.BlockSpec((None, n_own, bias_rows, width), lambda g, p: (column(g, p), 0, 0, 0)),
            ],
            out_specs=[
                pl.BlockSpec(block, lambda g, p: (jnp.minimum(g, n_z - 1), 0, 0, 0)),
                pl.BlockSpec(block, lambda g, p: (jnp.maximum(g - n_z, 0), 0, 0, 0)),
            ],
        ),
        out_shape=[shape, shape],
        compiler_params=pltpu.CompilerParams(vmem_limit_bytes=40 << 20),
    )(core.reshape(1), modulated_t, attn_t, outer, bias_slots)


def block_pass(tokens_in, modulation, cotangent, w_qkv, w_proj, fc_parts, fc_shape, bias_full):
    latents, length, features = tokens_in.shape
    core = lax.axis_index("dp") % 2
    n_dp, n_own = lax.axis_size("dp"), lax.axis_size("own")
    steps = len(own_bits(n_own))
    hidden_units = n_dp * fc_shape[2]
    head_count = HEADS
    head_size = features // head_count
    score_scale = 1.0 / math.sqrt(head_size)
    row_count = latents * length
    b_query = bias_full[:features]
    b_value = bias_full[features : 2 * features]
    b_proj = bias_full[2 * features : 3 * features]
    b_fc1 = bias_full[3 * features : 3 * features + hidden_units]
    b_fc2 = bias_full[3 * features + hidden_units : 4 * features + hidden_units]
    pieces = [
        modulation[:, index * features : (index + 1) * features][:, None, :] for index in range(6)
    ]
    shift_one, scale_one, gate_one, shift_two, scale_two, gate_two = pieces
    residual = tokens_in.astype(jnp.float32)
    normed_one, inv_one = layer_stats(residual)
    modulated_one = (normed_one * (1.0 + scale_one) + shift_one).astype(jnp.bfloat16)
    qkv_proj = jnp.dot(
        modulated_one.reshape(row_count, features), w_qkv, preferred_element_type=jnp.float32
    )
    for index in range(steps - 2):
        fc_parts = share_merge(fc_parts, share_send(fc_parts, n_own, index), n_own, index)
    came = share_send(fc_parts, n_own, steps - 2)
    qkv_proj, came = after(qkv_proj, came)
    fc_parts = share_merge(fc_parts, came, n_own, steps - 2)
    qkv_proj = qkv_proj.reshape(latents, length, 3 * features)
    came = share_send(fc_parts, n_own, steps - 1)
    head_shape = (latents, length, head_count, head_size)
    query_flat = (qkv_proj[..., :features] + b_query).astype(jnp.bfloat16)
    key_flat = qkv_proj[..., features : 2 * features].astype(jnp.bfloat16)
    value_flat = (qkv_proj[..., 2 * features :] + b_value).astype(jnp.bfloat16)
    query_heads, key_heads, value_heads = (
        part.reshape(head_shape) for part in (query_flat, key_flat, value_flat)
    )
    scores = batched("bqhd,bkhd->bhqk", query_heads, key_heads) * score_scale
    row_max = jnp.max(scores, axis=-1, keepdims=True)
    log_total = row_max + jnp.log(jnp.sum(jnp.exp(scores - row_max), axis=-1, keepdims=True))
    attn_probs = jnp.exp(scores - log_total).astype(jnp.bfloat16)
    attn_out = (
        batched("bhqk,bkhd->bqhd", attn_probs, value_heads)
        .astype(jnp.bfloat16)
        .reshape(row_count, features)
    )
    attn_out, came = after(attn_out, came)
    fc_parts = share_merge(fc_parts, came, n_own, steps - 1)
    fc_mine, fc_other = share_core(fc_parts, n_dp, n_own, fc_shape)
    branch_one = (jnp.dot(attn_out, w_proj, preferred_element_type=jnp.float32) + b_proj).reshape(
        latents, length, features
    )
    middle = residual + gate_one * branch_one
    normed_two, inv_two = layer_stats(middle)
    modulated_two = (
        (normed_two * (1.0 + scale_two) + shift_two)
        .astype(jnp.bfloat16)
        .reshape(row_count, features)
    )
    fc1_pre, branch_two = mlp_forward(core, modulated_two, fc_mine, fc_other, b_fc1)
    branch_two = (branch_two + b_fc2).reshape(latents, length, features)
    block_out = middle + gate_two * branch_two
    cot_float = cotangent.astype(jnp.float32)
    d_gate_two = jnp.sum(cot_float * branch_two, axis=1)
    d_branch_two = cot_float * gate_two
    dbranch_low = d_branch_two.astype(jnp.bfloat16).reshape(row_count, features)
    gb_fc2 = jnp.sum(d_branch_two, axis=(0, 1))
    fc_terms, fc_others, d_mod_two, gb_fc1 = mlp_backward(
        core, modulated_two.T, dbranch_low, dbranch_low.T, fc1_pre, fc_mine, fc_other
    )
    d_mod_two = d_mod_two.reshape(latents, length, features)
    fc_terms, fc_came = reduce_core(fc_terms, fc_others, n_dp, n_own)
    d_shift_two = jnp.sum(d_mod_two, axis=1)
    d_scale_two = jnp.sum(d_mod_two * normed_two, axis=1)
    d_middle = cot_float + norm_back(d_mod_two * (1.0 + scale_two), normed_two, inv_two)
    d_gate_one = jnp.sum(d_middle * branch_one, axis=1)
    d_branch_one = d_middle * gate_one
    dbranch_one_low = d_branch_one.astype(jnp.bfloat16).reshape(row_count, features)
    gb_proj = jnp.sum(d_branch_one, axis=(0, 1))
    d_attn = jnp.dot(dbranch_one_low, w_proj.T, preferred_element_type=jnp.float32).astype(
        jnp.bfloat16
    )
    d_attn, fc_came = after(d_attn, fc_came)
    fc_parts = reduce_halves(fc_terms, fc_came, n_dp, n_own)
    for index in range(steps - 1):
        fc_parts = reduce_own(fc_parts, n_own, index)
    flat_shape = (latents, length, features)
    d_query, d_key, d_value, gb_query, gb_value = attention_backward(
        query_flat.reshape(row_count, features),
        key_flat.reshape(row_count, features),
        value_flat.reshape(row_count, features),
        d_attn,
        length,
        head_size,
    )
    gb_query, gb_value = gb_query.reshape(-1), gb_value.reshape(-1)
    dqkv_low = jnp.concatenate([d_query, d_key, d_value], axis=1)
    dqkv_low, fc_parts = after(dqkv_low, fc_parts)
    fc_parts = reduce_own(fc_parts, n_own, steps - 1)
    outer = jnp.concatenate(
        [
            dqkv_low.reshape(row_count, n_dp, 3 * features // n_dp),
            dbranch_one_low.reshape(row_count, n_dp, features // n_dp),
        ],
        axis=2,
    ).transpose(1, 0, 2)
    d_mod_one = jnp.dot(dqkv_low, w_qkv.T, preferred_element_type=jnp.float32).reshape(flat_shape)
    d_mod_one, fc_parts = after(d_mod_one, fc_parts)
    d_shift_one = jnp.sum(d_mod_one, axis=1)
    d_scale_one = jnp.sum(d_mod_one * normed_one, axis=1)
    grad_in = d_middle + norm_back(d_mod_one * (1.0 + scale_one), normed_one, inv_one)
    d_modulation = jnp.concatenate(
        [d_shift_one, d_scale_one, d_gate_one, d_shift_two, d_scale_two, d_gate_two], axis=-1
    )
    gb_ada = jnp.sum(d_modulation, axis=0)
    grad_bias = jnp.concatenate([gb_query, gb_value, gb_proj, gb_fc1, gb_fc2, gb_ada])
    width = outer.shape[2]
    bias_count = grad_bias.shape[0] // (n_dp * n_own)
    bias_rows = -(-bias_count // (16 * width)) * 16
    bias_slots = grad_bias.reshape(n_dp, n_own, bias_count).astype(jnp.bfloat16)
    bias_slots = jnp.pad(bias_slots, ((0, 0), (0, 0), (0, bias_rows * width - bias_count)))
    attn_terms, attn_others = attn_gradients(
        core,
        modulated_one.reshape(row_count, features).T,
        attn_out.T,
        outer,
        bias_slots.reshape(n_dp, n_own, bias_rows, width),
        3 * features // n_dp,
    )
    attn_came = reduce_core(attn_terms, attn_others, n_dp, n_own)[1]
    (fc_parts, d_modulation), attn_came = after((fc_parts, d_modulation), attn_came)
    attn_parts = reduce_halves(attn_terms, attn_came, n_dp, n_own)
    fc_sums = reduce_z(fc_parts, n_dp)
    return block_out, grad_in, d_modulation, attn_parts, fc_sums


def per_device(
    tokens_in,
    condition,
    cotangent,
    w_qkv,
    w_proj,
    w_fc1,
    w_fc2,
    w_ada,
    mom_qkv,
    mom_proj,
    mom_fc1,
    mom_fc2,
    mom_ada,
    biases,
    bias_mom,
):
    low = jnp.bfloat16
    n_dp, n_own = lax.axis_size("dp"), lax.axis_size("own")
    dp_place, own_place = lax.axis_index("dp"), lax.axis_index("own")
    latents, features = condition.shape
    rows = w_qkv.shape[0]
    n_qkv, n_proj, n_fc1, n_fc2, n_ada = (
        w_qkv.shape[1],
        w_proj.shape[1],
        w_fc1.shape[1],
        w_fc2.shape[0],
        w_ada.shape[1],
    )
    cond_act = jax.nn.silu(condition).astype(low)
    small = jnp.concatenate([cond_act.reshape(-1), biases.astype(low)])
    small_own = gather_dp(small, n_dp)
    cond_own = small_own[:, : latents * features].reshape(n_dp * latents, features)
    w_ada_rows = gather_own(w_ada.astype(low), n_own).reshape(features, n_ada)
    mod_mine = jnp.dot(cond_own, w_ada_rows, preferred_element_type=jnp.float32)
    mod_parts = swap_dp(mod_mine.reshape(n_dp, latents, n_ada))
    small_all = gather_own(small_own, n_own)
    bias_full = (
        small_all[:, :, latents * features :].transpose(1, 0, 2).reshape(-1).astype(jnp.float32)
    )
    core = dp_place % 2
    first = jnp.concatenate([w_qkv, w_proj], axis=1).astype(low)
    second = jnp.stack([w_fc1, w_fc2.T]).astype(low)
    steps = len(own_bits(n_own))
    first_parts = share_z(first, n_dp)
    second, mod_parts = after(second, mod_parts)
    fc_parts = share_z(second, n_dp)
    for index in range(steps):
        came = share_send(first_parts, n_own, index)
        if index == 0:
            mod_parts, came = after(mod_parts, came)
        first_parts = share_merge(first_parts, came, n_own, index)
    fc_parts, first_parts = after(fc_parts, first_parts)
    first_mine, first_other = share_core(first_parts, n_dp, n_own, first.shape)
    first_all = jnp.where(
        core == 0,
        jnp.stack([first_mine, first_other], axis=1),
        jnp.stack([first_other, first_mine], axis=1),
    ).reshape(n_dp, features, n_qkv + n_proj)
    modulation = mod_parts.transpose(1, 0, 2).reshape(latents, n_dp * n_ada)
    modulation = modulation + bias_full[bias_full.shape[0] - n_dp * n_ada :]
    block_out, grad_in, d_modulation, attn_parts, fc_sums = block_pass(
        tokens_in,
        modulation,
        cotangent,
        columns_of(first_all, 0, n_qkv),
        columns_of(first_all, n_qkv, n_proj),
        fc_parts,
        second.shape,
        bias_full,
    )
    for index in range(steps):
        attn_parts = reduce_own(attn_parts, n_own, index)
    fc_sums, attn_parts = after(fc_sums, attn_parts)
    fc_tile = add_arrived(*fc_sums)
    attn_tile = add_arrived(*reduce_z(attn_parts, n_dp))
    bias_count = biases.shape[0]
    bias_tile = attn_tile[rows:].reshape(-1)[:bias_count]
    dmod_low = d_modulation.astype(low)
    dmod_own = swap_dp(dmod_low.reshape(latents, n_dp, n_ada).transpose(1, 0, 2))
    dmod_own = dmod_own.reshape(n_dp * latents, n_ada)
    cond_terms = jnp.dot(dmod_own, w_ada_rows.T, preferred_element_type=jnp.float32)
    cond_parts = swap_dp(cond_terms.reshape(n_dp, latents, features))
    dmod_all = gather_own(dmod_own, n_own).reshape(n_own * n_dp * latents, n_ada)
    cond_all = small_all[:, :, : latents * features].reshape(n_own * n_dp * latents, features)
    cond_cols = lax.dynamic_slice_in_dim(cond_all, own_place * rows, rows, 1)
    g_ada = jnp.dot(cond_cols.T, dmod_all, preferred_element_type=jnp.float32)
    tiles = (
        attn_tile[:rows, :n_qkv],
        attn_tile[:rows, n_qkv:],
        fc_tile[0],
        fc_tile[1],
        g_ada,
    )
    weights = (w_qkv, w_proj, w_fc1, w_fc2.T, w_ada)
    moments = (mom_qkv, mom_proj, mom_fc1, mom_fc2.T, mom_ada)
    fresh = [momentum_rate * moments[index] + tiles[index] for index in range(5)]
    widths = [n_qkv, n_proj, n_fc1, n_fc2, n_ada]
    fc_rows = jnp.concatenate([fresh[2], fresh[3]], axis=1).astype(low)
    rest_rows = jnp.concatenate([fresh[0], fresh[1], fresh[4]], axis=1).astype(low)
    fc_all = gather_own(fc_rows, n_own).reshape(features, n_fc1 + n_fc2)
    rest_all = gather_own(rest_rows, n_own).reshape(features, n_qkv + n_proj + n_ada)
    low_rows = [
        rest_rows[:, :n_qkv],
        rest_rows[:, n_qkv : n_qkv + n_proj],
        fc_rows[:, :n_fc1],
        fc_rows[:, n_fc1:],
        rest_rows[:, n_qkv + n_proj :],
    ]
    low_all = [
        rest_all[:, :n_qkv],
        rest_all[:, n_qkv : n_qkv + n_proj],
        fc_all[:, :n_fc1],
        fc_all[:, n_fc1:],
        rest_all[:, n_qkv + n_proj :],
    ]
    gram_terms = [
        jnp.dot(low_rows[index], low_all[index].T, preferred_element_type=jnp.float32)
        for index in range(5)
    ]
    gram_rows = gram_to_owner(gram_terms, GRAM_SLOTS, n_dp)
    gram_rows, cond_parts = after(gram_rows, cond_parts)
    gram = gather_own(gram_rows, n_own).reshape(features, features)
    sigmoid_c = jax.nn.sigmoid(condition)
    grad_cond = jnp.sum(cond_parts, axis=0) * (sigmoid_c * (1.0 + condition * (1.0 - sigmoid_c)))
    unit = jnp.eye(features, dtype=jnp.float32)
    magnitude = jnp.sqrt(jnp.sum(gram * unit))
    divisor = magnitude + 1e-07
    gram = gram / (divisor * divisor)
    my_rows, by_column = newton_schulz(gram, own_place, rows)
    middle = jnp.sum(by_column) / features
    my_unit = lax.dynamic_slice_in_dim(unit, own_place * rows, rows, 0)
    my_rows = ((my_rows - middle * my_unit) / divisor).astype(low)
    scalars = jnp.stack([middle / divisor, magnitude])
    high_part = scalars.astype(low)
    low_part = (scalars - high_part.astype(jnp.float32)).astype(low)
    extra = jnp.pad(jnp.stack([high_part, low_part]), ((0, 14), (0, features - 2)))
    factors = spread_from_owners(jnp.concatenate([my_rows, extra]), n_dp)
    numbers = [
        factor[rows, :2].astype(jnp.float32) + factor[rows + 1, :2].astype(jnp.float32)
        for factor in factors
    ]
    ortho = [
        numbers[index][0] * fresh[index]
        + jnp.dot(factors[index][:rows], low_all[index], preferred_element_type=jnp.float32)
        for index in range(5)
    ]
    position = lax.iota(jnp.int32, 5)
    moment_norms = sum(jnp.where(position == index, numbers[index][1], 0.0) for index in range(5))
    sides = (n_qkv * n_dp, n_proj * n_dp, n_fc1 * n_dp, n_fc2 * n_dp, n_ada * n_dp)
    updated = [
        weights[index]
        - learn_rate * 0.2 * math.sqrt(max(features, sides[index])) * ortho[index]
        for index in range(5)
    ]
    moment_bias = momentum_rate * bias_mom + bias_tile
    new_bias = biases - bias_rate * moment_bias
    return (
        block_out,
        grad_in,
        grad_cond,
        tiles[0],
        tiles[1],
        tiles[2],
        tiles[3].T,
        tiles[4],
        bias_tile,
        updated[0],
        updated[1],
        updated[2],
        updated[3].T,
        updated[4],
        fresh[0],
        fresh[1],
        fresh[2],
        fresh[3].T,
        fresh[4],
        new_bias,
        moment_bias,
        moment_norms,
    )


def solution(mesh):
    placed = (
        P(("dp", "own"), None, None),
        P(("dp", "own"), None),
        P(("dp", "own"), None, None),
        P("own", "dp"),
        P("own", "dp"),
        P("own", "dp"),
        P("dp", "own"),
        P("own", "dp"),
        P("own", "dp"),
        P("own", "dp"),
        P("own", "dp"),
        P("dp", "own"),
        P("own", "dp"),
        P(("dp", "own")),
        P(("dp", "own")),
    )
    return jax.shard_map(
        per_device,
        mesh=mesh,
        in_specs=placed,
        out_specs=(
            P(("dp", "own"), None, None),
            P(("dp", "own"), None, None),
            P(("dp", "own"), None),
            P("own", "dp"),
            P("own", "dp"),
            P("own", "dp"),
            P("dp", "own"),
            P("own", "dp"),
            P(("dp", "own")),
            P("own", "dp"),
            P("own", "dp"),
            P("own", "dp"),
            P("dp", "own"),
            P("own", "dp"),
            P("own", "dp"),
            P("own", "dp"),
            P("own", "dp"),
            P("dp", "own"),
            P("own", "dp"),
            P(("dp", "own")),
            P(("dp", "own")),
            P(),
        ),
        check_vma=False,
    )
```
